32 devices in a mesh: gx: 4 (over y, x), gy: 4 (over z), gz: 2 (over core).
Axes of the slice: x: 2, y: 2, z: 4, core: 2. Of those that a mesh axis runs over, the one named last changes fastest.
Arguments:
- rhs: float32 [7, 7, 7, 4, 16, 256], P(None, None, None, 'gx', 'gy', 'gz'), may hold values from -6 to 6
- orders: int32 [4, 16, 256], P('gx', 'gy', 'gz'), may hold values from 3 to 6
Outputs:
- smoothed: float32 [7, 7, 7, 4, 16, 256], P(None, None, None, 'gx', 'gy', 'gz')
- coarse_residual: float32 [4, 16, 256], P('gx', 'gy')
The draws below stay inside these ranges and needn't reach their ends.
All inputs are finite; a program needn't handle non-finite values.
Results may differ from the reference program's by a relative error of at most 0.00016.
Values sent between devices are 32-bit elements; how exact they have to be, the bound alone decides.
A program may use at most 64 MiB of HBM per device.

```python
import jax
import jax.numpy as jnp
import numpy as np
from jax import lax

MODES = 7
NX = 4
NY = 16
NZ = 256


def set_ends(drawn, own_key, smallest, largest):
    dims = drawn.shape
    spot = [jax.random.randint(jax.random.fold_in(own_key, axis), (), 0, dims[axis]) for axis in range(len(dims))]
    drawn = drawn.at[tuple(spot)].set(smallest)
    longest = dims.index(max(dims))
    spot[longest] = (spot[longest] + 1) % dims[longest]
    return drawn.at[tuple(spot)].set(largest)


def block_levels(key, dims, pieces, smallest, largest):
    factor_of, own = 1.0, jax.random.fold_in(key, 6)
    for dim, blocks in pieces:
        draws = jnp.exp(jax.random.uniform(jax.random.fold_in(own, dim), (blocks,), jnp.float32, smallest / len(pieces), largest / len(pieces)))
        factor_of = factor_of * jnp.repeat(draws, dims[dim] // blocks).reshape([-1 if axis == dim else 1 for axis in range(len(dims))])
    return factor_of


def scatter_about(stream_key, shape, width, most, shards=(), dtype=jnp.bfloat16):
    values = jax.random.normal(stream_key, shape, jnp.float32) * width
    if len(shards) > 0:
        values = block_levels(stream_key, shape, shards, -0.22, 0.18) * values
    return jnp.clip(values, min=-most, max=most).astype(dtype)


def setup_inputs(seed: int = 0) -> dict:
    key_list = jax.random.split(jax.random.key(seed), 3)
    return {
        "rhs": scatter_about(key_list[0], (MODES, MODES, MODES, NX, NY, NZ), 1.0, 6.0, ((3, 4), (4, 4), (5, 2)), jnp.float32),
        "orders": set_ends(jax.random.randint(key_list[1], (NX, NY, NZ), 3, 7), jax.random.fold_in(key_list[1], 1), 3, 6).astype(jnp.int32),
    }


PENALTY = 49.0
EIGEN_HIGH = 2.4
EIGEN_LOW = 0.24
PRECISE = lax.Precision.HIGHEST

def basis_tables():
    degree = np.arange(7)
    normed = np.sqrt((2.0 * degree + 1.0) / 2.0)
    smaller = np.minimum(degree[:, None], degree[None, :])
    parity = (degree[:, None] + degree[None, :]) % 2 == 0
    stiffness = np.where(parity, normed[:, None] * normed[None, :] * smaller * (smaller + 1), 0.0)
    signs = (-1.0) ** degree
    slope = normed * degree * (degree + 1) / 2.0
    traces = np.stack([normed * signs, -slope * signs, normed, slope])
    stiff_diag = normed * normed * degree * (degree + 1)
    one_axis = stiff_diag + 2.0 * (PENALTY * normed * normed - normed * slope)
    diagonal = (one_axis[:, None, None] + one_axis[None, :, None] + one_axis[None, None, :]) / PENALTY
    highest = np.maximum(np.maximum(degree[:, None, None], degree[None, :, None]), degree[None, None, :])
    third = np.sqrt(1.5) / 3.0
    vertex = np.array([[np.sqrt(0.5), np.sqrt(0.5)], [-third, third]])
    return (stiffness, traces, diagonal, highest, vertex)

def face_stack(field, direction, traces):
    return jnp.stack([jnp.tensordot(traces[row], field, axes=(0, direction), precision=PRECISE) for row in range(4)])

def place(vector, plane, direction):
    return jnp.moveaxis(vector.reshape((7,) + (1,) * plane.ndim) * plane[None], 0, direction)

def middle(array, axis_cells, start):
    return lax.slice_in_dim(array, start, start + array.shape[axis_cells] - 2, axis=axis_cells)

def flux(extended, direction, traces):
    axis_cells = 3 + direction
    own = middle(extended, axis_cells, 1)
    lower = middle(extended, axis_cells, 0)
    upper = middle(extended, axis_cells, 2)
    jump_up = own[2] - upper[0]
    mean_up = 0.5 * (own[3] + upper[1])
    jump_low = lower[2] - own[0]
    mean_low = 0.5 * (lower[3] + own[1])
    result = place(traces[2], PENALTY * jump_up - mean_up, direction) - 0.5 * place(traces[3], jump_up, direction)
    return result + place(traces[0], mean_low - PENALTY * jump_low, direction) - 0.5 * place(traces[1], jump_low, direction)

def rim_stacks(padded, traces):
    stacks = []
    for direction in range(3):
        index = [slice(None)] * 6
        for other in range(3):
            if other != direction:
                index[3 + other] = slice(1, -1)
        stacks.append(face_stack(padded[tuple(index)], direction, traces))
    return stacks

def operate(field, mask, stacks, stiffness, traces):
    total = jnp.zeros_like(field)
    for direction in range(3):
        total = total + jnp.moveaxis(jnp.tensordot(stiffness, field, axes=(1, direction), precision=PRECISE), 0, direction)
        total = total + flux(stacks[direction], direction, traces)
    return mask * total / PENALTY

def carry_global(pair, axis_cells):
    leading = pair[1]
    count = leading.shape[axis_cells]
    moved = jnp.concatenate([jnp.zeros_like(lax.slice_in_dim(leading, 0, 1, axis=axis_cells)), lax.slice_in_dim(leading, 0, count - 1, axis=axis_cells)], axis=axis_cells)
    return pair[0] + moved

def reference(rhs, orders):
    tables = basis_tables()
    stiffness = jnp.asarray(tables[0], jnp.float32)
    traces = jnp.asarray(tables[1], jnp.float32)
    diagonal = jnp.asarray(tables[2], jnp.float32)
    highest = jnp.asarray(tables[3], jnp.int32)
    vertex = jnp.asarray(tables[4], jnp.float32)
    mask = (highest[:, :, :, None, None, None] <= orders[None, None, None]).astype(jnp.float32)
    inv_diag = mask / diagonal[:, :, :, None, None, None]

    def apply(field):
        padded = jnp.pad(field, ((0, 0),) * 3 + ((1, 1),) * 3)
        return operate(field, mask, rim_stacks(padded, traces), stiffness, traces)
    theta = 0.5 * (EIGEN_HIGH + EIGEN_LOW)
    delta = 0.5 * (EIGEN_HIGH - EIGEN_LOW)
    rho_first = delta / theta
    rho_second = 1.0 / (2.0 * theta / delta - rho_first)
    forcing = mask * rhs
    first = inv_diag * forcing / theta
    resid_one = forcing - apply(first)
    smoothed = first + (rho_second * rho_first * first + 2.0 * rho_second / delta * (inv_diag * resid_one))
    resid_two = forcing - apply(smoothed)
    corner = jnp.einsum('ai,bj,ck,abcxyz->ijkxyz', vertex, vertex, vertex, resid_two[:2, :2, :2], precision=PRECISE)
    along_x = carry_global(corner, 2)
    along_y = carry_global(along_x, 2)
    along_z = carry_global(along_y, 2)
    inside_x = (jnp.arange(NX) > 0).astype(jnp.float32)
    inside_y = (jnp.arange(NY) > 0).astype(jnp.float32)
    inside_z = (jnp.arange(NZ) > 0).astype(jnp.float32)
    interior = inside_x[:, None, None] * inside_y[None, :, None] * inside_z[None, None, :]
    return (smoothed, along_z * interior)
```

```python
import functools

import jax
import jax.numpy as jnp
import numpy as np
from jax import lax
from jax.experimental import pallas as pl
from jax.experimental.pallas import tpu as pltpu
from jax.sharding import PartitionSpec as P

PENALTY = 49.0
EIGEN_HIGH = 2.4
EIGEN_LOW = 0.24
MODES = 7
MESH = pl.DeviceIdType.MESH


def tables():
    degree = np.arange(MODES)
    normed = np.sqrt((2.0 * degree + 1.0) / 2.0)
    smaller = np.minimum(degree[:, None], degree[None, :])
    parity = (degree[:, None] + degree[None, :]) % 2 == 0
    stiffness = np.where(parity, normed[:, None] * normed[None, :] * smaller * (smaller + 1), 0.0)
    signs = (-1.0) ** degree
    slope = normed * degree * (degree + 1) / 2.0
    low, low_slope = normed * signs, -slope * signs
    own = stiffness + np.outer(normed, PENALTY * normed - 0.5 * slope) - 0.5 * np.outer(slope, normed)
    own = own + np.outer(low, PENALTY * low + 0.5 * low_slope) + 0.5 * np.outer(low_slope, low)
    one_axis = normed * normed * degree * (degree + 1) + 2.0 * (
        PENALTY * normed * normed - normed * slope
    )
    diagonal = (
        one_axis[:, None, None] + one_axis[None, :, None] + one_axis[None, None, :]
    ) / PENALTY
    return (
        own / PENALTY,
        0.5 * slope - PENALTY * normed,
        0.5 * normed,
        normed / PENALTY,
        slope / PENALTY,
        diagonal,
    )


OWN, JUMP, HALF, VALUE, SLOPE, DIAGONAL = tables()
THETA = 0.5 * (EIGEN_HIGH + EIGEN_LOW)
DELTA = 0.5 * (EIGEN_HIGH - EIGEN_LOW)
RHO_FIRST = DELTA / THETA
RHO_SECOND = 1.0 / (2.0 * THETA / DELTA - RHO_FIRST)
KEEP = 1.0 + RHO_SECOND * RHO_FIRST
STEP = 2.0 * RHO_SECOND / DELTA * THETA


def combine(weights, values):
    total = None
    for weight, value in zip(weights, values):
        term = value * float(weight)
        total = term if total is None else total + term
    return total


def traces(values):
    even, odd = values[0::2], values[1::2]
    jump_even, jump_odd = combine(JUMP[0::2], even), combine(JUMP[1::2], odd)
    half_even, half_odd = combine(HALF[0::2], even), combine(HALF[1::2], odd)
    down = (jump_even - jump_odd, half_even - half_odd)
    up = (jump_even + jump_odd, half_even + half_odd)
    return down, up


def own_row(row, values):
    start = row % 2
    return combine(OWN[row, start::2], values[start::2])


def face_terms(from_up, from_down):
    both = (from_up[0] + from_down[0], from_up[1] + from_down[1])
    apart = (from_up[0] - from_down[0], from_up[1] - from_down[1])

    def term(mode):
        pair = both if mode % 2 == 0 else apart
        if mode == 0:
            return pair[0] * float(VALUE[0])
        return pair[0] * float(VALUE[mode]) + pair[1] * float(SLOPE[mode])

    return term


def vertex_pair(zero, one):
    flat, tilt = np.sqrt(0.5) * zero, (np.sqrt(1.5) / 3.0) * one
    return flat - tilt, flat + tilt


def one_sided(data, mode, from_below):
    if mode == 0:
        return data[0] * float(VALUE[0])
    sign = -1.0 if from_below else 1.0
    return data[0] * (sign * float(VALUE[1])) + data[1] * (sign * float(SLOPE[1]))


def corners(values):
    for axis in range(3):
        done = {}
        for key in values:
            if key[axis] == 0:
                other = tuple(1 if n == axis else key[n] for n in range(3))
                done[key], done[other] = vertex_pair(values[key], values[other])
        values = done
    return values


PAIRS = [(a, b) for a in range(2) for b in range(2)]
OCTET = [(a, b, e) for a in range(2) for b in range(2) for e in range(2)]
FIRST_CHUNKS = ((0, 4, 0, 2), (4, MODES, 0, 2), (0, 2, 2, MODES))
LATE = MODES - 2
CHUNKS = len(FIRST_CHUNKS) + LATE


def kernel(
    sizes, cells_y, cells_z, rhs_hbm, orders_hbm, table_hbm, smooth, coarse_ref,
    rhs, first, acc, coef, orders_ref, table_ref,
    xs, xr, ys, yr, zs, zr, y_up, y_down,
    order_line, order_x, order_y, order_z, order_tile, pads,
    out_mid, out_high, out_low, in_mid, in_high, in_low, column,
    relay, local_sem, send_sem, recv_sem, x_send, x_recv, relay_in, relay_out,
):
    nx, ny, nz = sizes
    rows = pads.shape[1]
    x, y, z = lax.axis_index("gx"), lax.axis_index("gy"), lax.axis_index("gz")
    barrier = pltpu.get_barrier_semaphore()

    def neighbour(axis, sign):
        here = (x, y, z)[axis]
        to = [x, y, z]
        to[axis] = here + sign
        back = [x, y, z]
        back[axis] = here - sign
        below, above = here > 0, here < sizes[axis] - 1
        return (tuple(to), below if sign < 0 else above, tuple(back), above if sign < 0 else below)

    halos = [neighbour(axis, sign) for axis in range(3) for sign in (-1, 1)]
    always = x >= 0

    def offset(dx, dy):
        ok_to, ok_from = always, x > 0
        if dx > 0:
            ok_to, ok_from = ok_to & (x + dx < nx), ok_from & (x >= dx)
        else:
            ok_to, ok_from = ok_to & (x + dx > 0), ok_from & (x - dx < nx)
        if dy > 0:
            ok_to, ok_from = ok_to & (y + dy < ny), ok_from & (y >= dy)
        if dy < 0:
            ok_to, ok_from = ok_to & (y + dy >= 0), ok_from & (y - dy < ny)
        return ((x + dx, y + dy, z), ok_to, (x - dx, y - dy, z), ok_from)

    carries = []
    for dx, dy in ((2, 1), (1, 1), (1, -1), (1, 0), (2, 0), (-1, 1), (-1, 0), (0, 1), (0, -1)):
        carries.append(offset(dx, dy) + (dx, dy))
    columns = []
    for r in range(1, nz):
        source = lax.rem(z - r + nz, nz)
        columns.append(((x, y, lax.rem(z + r, nz)), always, (x, y, source), always, source))

    odd = lax.rem(x, 2) == 1
    even = jnp.logical_not(odd)
    relays = (
        ((x - 2, y, z), even & (x >= 2), (x + 2, y, z), even & (x + 2 < nx), (x + 1, y, z)),
        ((x + 2, y, z), odd & (x + 2 < nx), (x - 2, y, z), odd & (x >= 3), (x - 1, y, z)),
    )

    expected = jnp.int32(0)
    for entry in halos[:4] + columns + list(relays) + carries[:1]:
        to, ok_to, back, ok_from = entry[:4]

        @pl.when(ok_from)
        def _(back=back):
            pl.semaphore_signal(barrier, inc=1, device_id=back, device_id_type=MESH)

        expected = expected + jnp.where(ok_to, 1, 0).astype(jnp.int32)

    loads = [
        pltpu.make_async_copy(orders_hbm, orders_ref, local_sem.at[MODES]),
        pltpu.make_async_copy(table_hbm, table_ref, local_sem.at[MODES + 1]),
    ]
    for copy in loads:
        copy.start()

    def rhs_load(b):
        return pltpu.make_async_copy(rhs_hbm.at[:, b], rhs.at[:, b], local_sem.at[b])

    for b in range(MODES):
        rhs_load(b).start()

    def remote(src, dst, slot, to):
        return pltpu.make_async_remote_copy(
            src_ref=src, dst_ref=dst, send_sem=send_sem.at[slot], recv_sem=recv_sem.at[slot],
            device_id=to, device_id_type=MESH,
        )

    def start(entry, slot, src, dst):
        to, ok_to = entry[:2]

        @pl.when(ok_to)
        def _():
            remote(src, dst, slot, to).start()

    def receive(entry, slot, src, dst):
        to, _, _, ok_from = entry[:4]

        @pl.when(ok_from)
        def _():
            remote(src, dst, slot, to).wait_recv()

    def finish(entry, slot, src, dst):
        to, ok_to = entry[:2]

        @pl.when(ok_to)
        def _():
            remote(src, dst, slot, to).wait_send()

    stages = (
        ((xs, xr), (ys, yr), (zs, zr)),
        ((orders_ref, order_x), (order_line, order_y), (orders_ref, order_z)),
    )

    def over(action, stage, axis):
        src, dst = stages[stage][axis]
        for side in range(2):
            index = 2 * axis + side
            action(halos[index], 6 * stage + index, src.at[0 if src is orders_ref else side], dst.at[side])

    for stage, empty in ((0, 0.0), (1, -1)):
        for axis in range(3):
            for side in range(2):
                dst = stages[stage][axis][1]

                @pl.when(jnp.logical_not(halos[2 * axis + side][3]))
                def _(dst=dst, side=side, empty=empty):
                    dst[side] = jnp.full(dst.shape[1:], empty, dst.dtype)

    pads[...] = jnp.zeros(pads.shape, jnp.float32)
    order_tile[...] = jnp.full(order_tile.shape, -1, jnp.int32)
    targets = {0: (out_mid, in_mid), 1: (out_high, in_high), -1: (out_low, in_low)}

    def carry_refs(dx, dy):
        src, dst = targets[dy]
        at = dx if dy < 0 else dx + 1
        return src.at[at], dst.at[at]

    for _, _, _, ok_from, dx, dy in carries:

        @pl.when(jnp.logical_not(ok_from))
        def _(dx=dx, dy=dy):
            dst = carry_refs(dx, dy)[1]
            dst[...] = jnp.zeros(dst.shape, jnp.float32)

    for copy in loads:
        copy.wait()
    orders = orders_ref[0]
    order_line[0] = orders[0:1]
    order_line[1] = orders[cells_y - 1 : cells_y]
    tile = (MODES, cells_y, cells_z)
    last_mode = lax.broadcasted_iota(jnp.int32, tile, 0)
    lane = lax.broadcasted_iota(jnp.int32, (1, 1, cells_z), 2)

    def active(a, b):
        return jnp.maximum(jnp.maximum(a, b), last_mode) <= orders[None]

    def loop(body, low=0, high=MODES):
        def step(index, carry):
            body(index)
            return carry

        lax.fori_loop(low, high, step, 0)

    def chunk(ref, side, number):
        if isinstance(number, int) and number < len(FIRST_CHUNKS):
            b0, b1, e0, e1 = FIRST_CHUNKS[number]
            return ref.at[side, b0:b1, :, e0:e1]
        return ref.at[side, number - len(FIRST_CHUNKS) + 2, :, 2:MODES]

    def x_copy(side, number, to):
        return pltpu.make_async_remote_copy(
            src_ref=chunk(xs, side, number), dst_ref=chunk(xr, side, number),
            send_sem=x_send.at[side, number], recv_sem=x_recv.at[side, number],
            device_id=to, device_id_type=MESH,
        )

    def to_relay(side, number, to):
        late = number - len(FIRST_CHUNKS)
        return pltpu.make_async_remote_copy(
            src_ref=chunk(xs, side, number), dst_ref=relay.at[side, late],
            send_sem=x_send.at[side, number], recv_sem=relay_in.at[side, late],
            device_id=to, device_id_type=MESH,
        )

    def from_relay(side, number, to):
        late = number - len(FIRST_CHUNKS)
        return pltpu.make_async_remote_copy(
            src_ref=relay.at[side, late], dst_ref=chunk(xr, side, number),
            send_sem=relay_out.at[side, late], recv_sem=x_recv.at[side, number],
            device_id=to, device_id_type=MESH,
        )

    def forward(number):
        for side in range(2):
            back, relaying, target = relays[side][2:]

            @pl.when(relaying)
            def _():
                to_relay(side, number, target).wait_recv()
                from_relay(side, number, target).start()

    def x_receive(number):
        for side in range(2):

            @pl.when(halos[side][3])
            def _():
                x_copy(side, number, halos[side][0]).wait_recv()

    def x_traces(b):
        rhs_load(b).wait()
        values = []
        for a in range(MODES):
            value = jnp.where(active(a, b), table_ref[a, b] * rhs[a, b], 0.0)
            first[a, b] = value
            values.append(value)
        sides = traces(values)
        for side in range(2):
            for kind in range(2):
                xs[side, b, kind] = sides[side][kind]

    loop(x_traces)
    pl.semaphore_wait(barrier, expected)

    def x_start(number, wanted):
        for side in range(2):
            to, ok_to = halos[side][:2]
            via, used = relays[side][:2]
            if wanted == "relayed":

                @pl.when(used)
                def _():
                    to_relay(side, number, via).start()
            elif wanted == "two hops":

                @pl.when(used)
                def _():
                    x_copy(side, number, to).start()
            else:

                @pl.when(ok_to & jnp.logical_not(used))
                def _():
                    x_copy(side, number, to).start()

    early = range(len(FIRST_CHUNKS))
    late = range(len(FIRST_CHUNKS), CHUNKS)
    for number in early:
        x_start(number, "two hops")
        x_start(number, "direct")
    over(start, 1, 0)
    for number in late:
        x_start(number, "relayed")
        x_start(number, "direct")
    over(start, 1, 2)
    over(start, 1, 1)

    def y_faces(a, values, send, up_buf, down_buf):
        down, up = traces(values)
        for kind in range(2):
            up_buf[kind, a, :, 0:cells_y, :] = down[kind]
            down_buf[kind, a, :, 1 : cells_y + 1, :] = up[kind]
            send[0, kind, a] = down[kind][:, 0:1, :]
            send[1, kind, a] = up[kind][:, cells_y - 1 : cells_y, :]

    def y_neighbours(a, received, up_buf, down_buf):
        for kind in range(2):
            up_buf[kind, a, :, cells_y : cells_y + 1, :] = received[0, kind, a]
            down_buf[kind, a, :, 0:1, :] = received[1, kind, a]
        return face_terms(
            [up_buf[kind, a, :, 1 : cells_y + 1, :] for kind in range(2)],
            [down_buf[kind, a, :, 0:cells_y, :] for kind in range(2)],
        )

    def z_faces(a, values, send):
        sides = traces(values)
        for side in range(2):
            for kind in range(2):
                send[side, kind, a] = sides[side][kind]

    def z_neighbours(a, send, received):
        def moved(side, kind, edge, amount):
            picked = jnp.where(lane == edge, received[side, kind, a], send[side, kind, a])
            return pltpu.roll(picked, amount, 2)

        return face_terms(
            [moved(0, kind, 0, cells_z - 1) for kind in range(2)],
            [moved(1, kind, cells_z - 1, 1) for kind in range(2)],
        )

    loop(lambda a: y_faces(a, [first[a, b] for b in range(MODES)], ys, y_up, y_down))
    over(start, 0, 1)
    loop(lambda a: z_faces(a, [first[a, :, e] for e in range(MODES)], zs))
    over(start, 0, 2)

    def x_own(b):
        values = [first[a, b] for a in range(MODES)]
        for a in range(MODES):
            acc[a, b] = own_row(a, values)

    def y_own(a):
        values = [first[a, b] for b in range(MODES)]
        for b in range(MODES):
            acc[a, b] += own_row(b, values)

    def z_own(a):
        values = [first[a, :, e] for e in range(MODES)]
        for e in range(MODES):
            acc[a, :, e] += own_row(e, values)

    loop(x_own)
    loop(y_own)
    loop(z_own)
    over(receive, 0, 2)

    def z_flux(a):
        term = z_neighbours(a, zs, zr)
        for e in range(MODES):
            acc[a, :, e] += term(e)

    loop(z_flux)
    over(receive, 0, 1)

    def y_flux(a):
        term = y_neighbours(a, yr, y_up, y_down)
        for b in range(MODES):
            right = rhs[a, b]
            total = acc[a, b] + term(b)
            scale = jnp.where(active(a, b), table_ref[a, b], 0.0)
            acc[a, b] = scale * (KEEP * right + STEP * (right - total))
            coef[a, b] = scale * (-STEP)

    loop(y_flux)

    for axis in range(3):
        over(receive, 1, axis)
    order_tile[1 : cells_y + 1] = orders
    order_tile[0:1] = order_y[1]
    order_tile[cells_y + 1 : cells_y + 2] = order_y[0]
    for number in late:
        forward(number)
    for number in early:
        x_receive(number)

    def update(a, b, low, high, term):
        part = slice(low, high)
        smooth[a, b, part] = acc[a, b, part] + coef[a, b, part] * term(a)

    def x_terms(b, low, high):
        part = slice(low, high)
        return face_terms(
            [xr[0, b, kind, part] for kind in range(2)], [xr[1, b, kind, part] for kind in range(2)]
        )

    for b in range(2):
        term = x_terms(b, 0, MODES)
        for a in range(2):
            update(a, b, 0, MODES, term)
        term = x_terms(b, 0, 2)
        for a in range(2, MODES):
            update(a, b, 0, 2, term)
    for b in range(2, MODES):
        term = x_terms(b, 0, 2)
        for a in range(2):
            update(a, b, 0, 2, term)

    centre, edge, x_low, x_high, y_low, y_high = {}, {}, {}, {}, {}, {}
    edge_orders = jnp.where(lane[0] == cells_z - 1, order_z[1], order_z[0])
    for key in OCTET:
        centre[key] = rhs[key]
    for b in range(2):
        values = [smooth[a, b, 0:2] for a in range(MODES)]
        down, up = traces(values)
        for a in range(2):
            own = own_row(a, values)
            below, above = one_sided(down, a, False), one_sided(up, a, True)
            for e in range(2):
                centre[a, b, e] = centre[a, b, e] - own[e]
                x_low[a, b, e] = jnp.where(order_x[1] >= max(a, b, e), -below[e], 0.0)
                x_high[a, b, e] = jnp.where(order_x[0] >= max(a, b, e), -above[e], 0.0)
    for a in range(2):
        values = [smooth[a, b, 0:2] for b in range(MODES)]
        down, up = traces(values)
        for b in range(2):
            own = own_row(b, values)
            below, above = one_sided(down, b, False), one_sided(up, b, True)
            for e in range(2):
                centre[a, b, e] = centre[a, b, e] - own[e]
                y_low[a, b, e], y_high[a, b, e] = below[e], above[e]
        values = [smooth[a, 0:2, e] for e in range(MODES)]
        down, up = traces(values)
        for e in range(2):
            below = pltpu.roll(one_sided(down, e, False), cells_z - 1, 2)
            above = pltpu.roll(one_sided(up, e, True), 1, 2)
            inner = jnp.where(lane == cells_z - 1, 0.0, below) + jnp.where(lane == 0, 0.0, above)
            outer = jnp.where(lane == cells_z - 1, below, jnp.where(lane == 0, above, 0.0))
            own = own_row(e, values) + inner
            for b in range(2):
                centre[a, b, e] = centre[a, b, e] - own[b]
                edge[a, b, e] = jnp.where(edge_orders >= max(a, b, e), -outer[b], 0.0)

    slots = iter(range(pads.shape[0]))

    def padded(value, at):
        slot = next(slots)
        pads[slot, at : at + cells_y, :] = value
        return pads[slot]

    own_tile = order_tile[...]
    resid = {}
    for key in OCTET:
        total = padded(centre[key], 1) - padded(y_low[key], 0) - padded(y_high[key], 2)
        resid[key] = jnp.where(own_tile >= max(key), total, 0.0)
    resid = corners(resid)
    near = {key: (corners(x_low)[key], corners(x_high)[key]) for key in OCTET}
    edge = corners(edge)
    row_lane = lane[0]
    sums = {}
    for dx in range(-1, 3):
        layers = []
        for k in range(2):
            parts = []
            if dx in (0, 1):
                parts += [resid[dx, 0, k], pltpu.roll(resid[dx, 1, k], 1, 0)]
            for side, i in ((0, dx + 1), (1, dx - 1)):
                if i in (0, 1):
                    parts += [padded(near[i, j, k][side], 1 + j) for j in range(2)]
            layers.append(functools.reduce(lambda p, q: p + q, parts))
        moved = pltpu.roll(layers[1], 1, 1)
        if dx in (0, 1):
            outer = [padded(edge[dx, 0, k], 1) + padded(edge[dx, 1, k], 2) for k in range(2)]
            outer_moved = pltpu.roll(outer[1], 1, 1)
            inside = layers[0] + jnp.where(row_lane == 0, outer_moved, moved)
            beyond = jnp.where(row_lane == 0, moved, outer_moved) + outer[0]
        else:
            inside = layers[0] + jnp.where(row_lane == 0, 0.0, moved)
            beyond = jnp.where(row_lane == 0, moved, 0.0)
        for part, value in enumerate((inside, beyond)):
            if dx == 0:
                sums[part] = value[1 : cells_y + 1]
            else:
                out_mid[dx + 1, part] = value[1 : cells_y + 1]
            out_high[dx + 1, part] = value[cells_y + 1 : cells_y + 3]
            if dx in (0, 1):
                out_low[dx, part] = value[0:1]

    for number, entry in enumerate(carries):
        start(entry, 12 + number, *carry_refs(*entry[4:]))

    def late_flux(b):
        x_receive(b - 2 + len(FIRST_CHUNKS))
        term = x_terms(b, 2, MODES)
        for a in range(2):
            update(a, b, 2, MODES, term)
        term = x_terms(b, 0, MODES)
        for a in range(2, MODES):
            update(a, b, 0, MODES, term)

    for b in range(2):
        term = x_terms(b, 2, MODES)
        for a in range(2, MODES):
            update(a, b, 2, MODES, term)
    loop(late_flux, 2)

    for number, entry in enumerate(carries):
        receive(entry, 12 + number, *carry_refs(*entry[4:]))

    for part in range(2):
        value = sums[part]
        for at in (0, 2, 3):
            value = value + in_mid[at, part]
        high = in_high[0, part] + in_high[1, part] + in_high[2, part] + in_high[3, part]
        low = in_low[0, part] + in_low[1, part]
        column[pl.ds(z, 1), part] = value[None]
        column[pl.ds(z, 1), part, 0:2] += high[None]
        column[pl.ds(z, 1), part, cells_y - 1 : cells_y] += low[None]

    def gather(number, arriving):
        entry = columns[number]
        at = entry[4] if arriving else z
        return remote(column.at[at], column.at[at], 12 + len(carries) + number, entry[0])

    for number in range(len(columns)):
        gather(number, False).start()
    for number in range(len(columns)):
        gather(number, True).wait_recv()

    row = lax.broadcasted_iota(jnp.int32, (cells_y, cells_z), 0)
    spot = lax.broadcasted_iota(jnp.int32, (cells_y, cells_z), 1)
    for zz in range(nz):
        total = column[zz, 0]
        if zz > 0:
            total = total + jnp.where(spot < 2, column[zz - 1, 1], 0.0)
        if zz < nz - 1:
            total = total + jnp.where(spot == cells_z - 1, column[zz + 1, 1], 0.0)
        inside = (x > 0) & ((row > 0) | (y > 0))
        if zz == 0:
            inside = inside & (spot > 0)
        coarse_ref[0, :, zz * cells_z : (zz + 1) * cells_z] = jnp.where(inside, total, 0.0)

    for stage in range(2):
        for axis in range(3):
            if (stage, axis) != (0, 0):
                over(finish, stage, axis)
    for number in range(CHUNKS):
        for side in range(2):

            @pl.when(halos[side][1])
            def _():
                x_copy(side, number, halos[side][0]).wait_send()

    for number in late:
        for side in range(2):

            @pl.when(relays[side][3])
            def _():
                from_relay(side, number, relays[side][4]).wait_send()

    for number, entry in enumerate(carries):
        finish(entry, 12 + number, *carry_refs(*entry[4:]))
    for number in range(len(columns)):
        gather(number, False).wait_send()


def drain(smooth, coarse, smooth_hbm, coarse_hbm, sem):
    copies = [
        pltpu.make_async_copy(smooth.at[a], smooth_hbm.at[a], sem.at[a]) for a in range(MODES)
    ]
    copies.append(pltpu.make_async_copy(coarse, coarse_hbm, sem.at[MODES]))
    for copy in copies:
        copy.start()
    for copy in copies:
        copy.wait()


def per_device(sizes, rhs, orders):
    _, cells_y, cells_z = orders.shape
    nz = sizes[2]
    table = jnp.asarray(
        np.broadcast_to(
            (1.0 / (DIAGONAL * THETA))[:, :, :, None, None], DIAGONAL.shape + (1, cells_z)
        ),
        jnp.float32,
    )
    field = rhs.reshape(rhs.shape[:3] + rhs.shape[4:])
    cells = (cells_y, cells_z)
    rows = 8 * ((cells_y + 8) // 8)
    tall = 8 * ((cells_y + 10) // 8)
    line = (2, 2, MODES, MODES)

    def buf(*shape):
        return pltpu.VMEM(shape, jnp.float32)

    def whole(*shape):
        return pltpu.VMEM(shape, jnp.int32)

    slots = 12 + 9 + nz - 1
    coarse_shape = (1, cells_y, nz * cells_z)
    vmem = pl.BlockSpec(memory_space=pltpu.VMEM)
    hbm = pl.BlockSpec(memory_space=pltpu.HBM)
    smoothed, coarse = pl.pallas_call(
        functools.partial(kernel, sizes, cells_y, cells_z),
        out_shape=(pltpu.VMEM(field.shape, jnp.float32), pltpu.VMEM(coarse_shape, jnp.float32)),
        in_specs=[hbm, hbm, hbm],
        out_specs=(vmem, vmem),
        scratch_shapes=[buf(*field.shape)] * 4
        + [
            whole(*orders.shape), buf(*table.shape),
            buf(2, MODES, 2, MODES, *cells), buf(2, MODES, 2, MODES, *cells),
            buf(*line, 1, cells_z), buf(*line, 1, cells_z),
            buf(*line, *cells), buf(*line, *cells),
            buf(2, MODES, MODES, rows, cells_z), buf(2, MODES, MODES, rows, cells_z),
            whole(2, 1, cells_z), whole(2, *cells), whole(2, 1, cells_z), whole(2, *cells),
            whole(tall, cells_z), buf(48, tall, cells_z),
            buf(4, 2, *cells), buf(4, 2, 2, cells_z), buf(2, 2, 1, cells_z),
            buf(4, 2, *cells), buf(4, 2, 2, cells_z), buf(2, 2, 1, cells_z),
            buf(nz, 2, *cells),
            buf(2, LATE, 2, LATE, *cells),
            pltpu.SemaphoreType.DMA((MODES + 2,)),
            pltpu.SemaphoreType.DMA((slots,)),
            pltpu.SemaphoreType.DMA((slots,)),
            pltpu.SemaphoreType.DMA((2, CHUNKS)),
            pltpu.SemaphoreType.DMA((2, CHUNKS)),
            pltpu.SemaphoreType.DMA((2, LATE)),
            pltpu.SemaphoreType.DMA((2, LATE)),
        ],
        compiler_params=pltpu.CompilerParams(collective_id=0, has_side_effects=True),
        name="smoother",
    )(field, orders, table)
    smoothed, coarse = pl.pallas_call(
        drain,
        out_shape=(
            jax.ShapeDtypeStruct(field.shape, jnp.float32),
            jax.ShapeDtypeStruct(coarse_shape, jnp.float32),
        ),
        in_specs=[vmem, vmem],
        out_specs=(hbm, hbm),
        scratch_shapes=[pltpu.SemaphoreType.DMA((MODES + 1,))],
        name="drain",
    )(
        pltpu.with_memory_space_constraint(smoothed, pltpu.VMEM),
        pltpu.with_memory_space_constraint(coarse, pltpu.VMEM),
    )
    return smoothed.reshape(rhs.shape), coarse


def solution(mesh):
    sizes = tuple(mesh.shape[axis] for axis in ("gx", "gy", "gz"))
    return jax.shard_map(
        functools.partial(per_device, sizes),
        mesh=mesh,
        in_specs=(P(None, None, None, "gx", "gy", "gz"), P("gx", "gy", "gz")),
        out_specs=(P(None, None, None, "gx", "gy", "gz"), P("gx", "gy", None)),
        check_vma=False,
    )
```

```python
import functools

import jax
import jax.numpy as jnp
import numpy as np
from jax import lax
from jax.experimental import pallas as pl
from jax.experimental.pallas import tpu as pltpu
from jax.sharding import PartitionSpec as P

PENALTY = 49.0
EIGEN_HIGH = 2.4
EIGEN_LOW = 0.24
MODES = 7
MESH = pl.DeviceIdType.MESH


def tables():
    degree = np.arange(MODES)
    normed = np.sqrt((2.0 * degree + 1.0) / 2.0)
    smaller = np.minimum(degree[:, None], degree[None, :])
    parity = (degree[:, None] + degree[None, :]) % 2 == 0
    stiffness = np.where(parity, normed[:, None] * normed[None, :] * smaller * (smaller + 1), 0.0)
    signs = (-1.0) ** degree
    slope = normed * degree * (degree + 1) / 2.0
    low, low_slope = normed * signs, -slope * signs
    own = stiffness + np.outer(normed, PENALTY * normed - 0.5 * slope) - 0.5 * np.outer(slope, normed)
    own = own + np.outer(low, PENALTY * low + 0.5 * low_slope) + 0.5 * np.outer(low_slope, low)
    one_axis = normed * normed * degree * (degree + 1) + 2.0 * (
        PENALTY * normed * normed - normed * slope
    )
    diagonal = (
        one_axis[:, None, None] + one_axis[None, :, None] + one_axis[None, None, :]
    ) / PENALTY
    return (
        own / PENALTY,
        0.5 * slope - PENALTY * normed,
        0.5 * normed,
        normed / PENALTY,
        slope / PENALTY,
        diagonal,
    )


OWN, JUMP, HALF, VALUE, SLOPE, DIAGONAL = tables()
THETA = 0.5 * (EIGEN_HIGH + EIGEN_LOW)
DELTA = 0.5 * (EIGEN_HIGH - EIGEN_LOW)
RHO_FIRST = DELTA / THETA
RHO_SECOND = 1.0 / (2.0 * THETA / DELTA - RHO_FIRST)
KEEP = 1.0 + RHO_SECOND * RHO_FIRST
STEP = 2.0 * RHO_SECOND / DELTA * THETA


def combine(weights, values):
    total = None
    for weight, value in zip(weights, values):
        term = value * float(weight)
        total = term if total is None else total + term
    return total


def traces(values):
    even, odd = values[0::2], values[1::2]
    jump_even, jump_odd = combine(JUMP[0::2], even), combine(JUMP[1::2], odd)
    half_even, half_odd = combine(HALF[0::2], even), combine(HALF[1::2], odd)
    down = (jump_even - jump_odd, half_even - half_odd)
    up = (jump_even + jump_odd, half_even + half_odd)
    return down, up


def own_row(row, values):
    start = row % 2
    return combine(OWN[row, start::2], values[start::2])


def face_terms(from_up, from_down):
    both = (from_up[0] + from_down[0], from_up[1] + from_down[1])
    apart = (from_up[0] - from_down[0], from_up[1] - from_down[1])

    def term(mode):
        pair = both if mode % 2 == 0 else apart
        if mode == 0:
            return pair[0] * float(VALUE[0])
        return pair[0] * float(VALUE[mode]) + pair[1] * float(SLOPE[mode])

    return term


def vertex_pair(zero, one):
    flat, tilt = np.sqrt(0.5) * zero, (np.sqrt(1.5) / 3.0) * one
    return flat - tilt, flat + tilt


def one_sided(data, mode, from_below):
    if mode == 0:
        return data[0] * float(VALUE[0])
    sign = -1.0 if from_below and mode % 2 else 1.0
    return data[0] * (sign * float(VALUE[mode])) + data[1] * (sign * float(SLOPE[mode]))


def corners(values):
    for axis in range(3):
        done = {}
        for key in values:
            if key[axis] == 0:
                other = tuple(1 if n == axis else key[n] for n in range(3))
                done[key], done[other] = vertex_pair(values[key], values[other])
        values = done
    return values


OCTET = [(a, b, e) for a in range(2) for b in range(2) for e in range(2)]
RELAYED = 4
REACH = range(-2, 4)
CARRIES = (
    (3, 1), (2, 1), (-2, 1), (1, 1), (-1, 1), (2, -1), (1, -1), (-1, -1),
    (3, 0), (2, 0), (-2, 0), (1, 0), (-1, 0), (0, 1), (0, -1),
)


def kernel(
    sizes, cells_y, cells_z, rhs_hbm, orders_hbm, table_hbm, smooth, coarse_ref,
    rhs, first, acc, coef, orders_ref, table_ref,
    xs, xr, ys, yr, zs, zr, y_up, y_down,
    order_line, order_x, order_y, order_z, pack, pack_in, pads,
    out_mid, out_high, out_low, in_mid, in_high, in_low, column,
    relay, local_sem, send_sem, recv_sem, x_send, x_recv, relay_in, relay_out,
):
    nx, ny, nz = sizes
    tall = pads.shape[1]
    x, y, z = lax.axis_index("gx"), lax.axis_index("gy"), lax.axis_index("gz")
    barrier = pltpu.get_barrier_semaphore()

    def neighbour(axis, sign):
        here = (x, y, z)[axis]
        to = [x, y, z]
        to[axis] = here + sign
        back = [x, y, z]
        back[axis] = here - sign
        below, above = here > 0, here < sizes[axis] - 1
        return (tuple(to), below if sign < 0 else above, tuple(back), above if sign < 0 else below)

    halos = [neighbour(axis, sign) for axis in range(3) for sign in (-1, 1)]
    always = x >= 0

    def offset(dx, dy):
        ok_to = (x + dx > 0) & (x + dx < nx)
        ok_from = (x > 0) & (x - dx >= 0) & (x - dx < nx)
        if dy > 0:
            ok_to, ok_from = ok_to & (y + dy < ny), ok_from & (y >= dy)
        if dy < 0:
            ok_to, ok_from = ok_to & (y + dy >= 0), ok_from & (y - dy < ny)
        return ((x + dx, y + dy, z), ok_to, (x - dx, y - dy, z), ok_from)

    carries = [offset(dx, dy) + (dx, dy) for dx, dy in CARRIES]
    columns = []
    for r in range(1, nz):
        source = lax.rem(z - r + nz, nz)
        columns.append(((x, y, lax.rem(z + r, nz)), always, (x, y, source), always, source))

    odd = lax.rem(x, 2) == 1
    even = jnp.logical_not(odd)
    relays = (
        ((x - 2, y, z), even & (x >= 2), (x + 2, y, z), even & (x + 2 < nx), (x + 1, y, z)),
        ((x + 2, y, z), odd & (x + 2 < nx), (x - 2, y, z), odd & (x >= 3), (x - 1, y, z)),
    )

    expected = jnp.int32(0)
    for entry in halos[:4] + columns + list(relays) + carries[:1]:
        to, ok_to, back, ok_from = entry[:4]

        @pl.when(ok_from)
        def _(back=back):
            pl.semaphore_signal(barrier, inc=1, device_id=back, device_id_type=MESH)

        expected = expected + jnp.where(ok_to, 1, 0).astype(jnp.int32)

    loads = [
        pltpu.make_async_copy(orders_hbm, orders_ref, local_sem.at[MODES]),
        pltpu.make_async_copy(table_hbm, table_ref, local_sem.at[MODES + 1]),
    ]
    for copy in loads:
        copy.start()

    def rhs_load(b):
        return pltpu.make_async_copy(rhs_hbm.at[:, b], rhs.at[:, b], local_sem.at[b])

    for b in range(MODES):
        rhs_load(b).start()

    def remote(src, dst, slot, to):
        return pltpu.make_async_remote_copy(
            src_ref=src, dst_ref=dst, send_sem=send_sem.at[slot], recv_sem=recv_sem.at[slot],
            device_id=to, device_id_type=MESH,
        )

    def start(entry, slot, src, dst):
        to, ok_to = entry[:2]

        @pl.when(ok_to)
        def _():
            remote(src, dst, slot, to).start()

    def receive(entry, slot, src, dst):
        to, _, _, ok_from = entry[:4]

        @pl.when(ok_from)
        def _():
            remote(src, dst, slot, to).wait_recv()

    def finish(entry, slot, src, dst):
        to, ok_to = entry[:2]

        @pl.when(ok_to)
        def _():
            remote(src, dst, slot, to).wait_send()

    stages = (
        ((xs, xr), (ys, yr), (zs, zr)),
        ((orders_ref, order_x), (order_line, order_y), (orders_ref, order_z)),
        ((pack, pack_in),),
    )

    def over(action, stage, axis):
        src, dst = stages[stage][axis]
        for side in range(2):
            index = 2 * axis + side
            action(halos[index], 6 * stage + index, src.at[0 if src is orders_ref else side], dst.at[side])

    for stage, empty in ((0, 0.0), (1, -1), (2, -1)):
        for axis in range(len(stages[stage])):
            for side in range(2):
                dst = stages[stage][axis][1]

                @pl.when(jnp.logical_not(halos[2 * axis + side][3]))
                def _(dst=dst, side=side, empty=empty):
                    dst[side] = jnp.full(dst.shape[1:], empty, dst.dtype)

    pads[...] = jnp.zeros(pads.shape, jnp.float32)
    pack[...] = jnp.full(pack.shape, -1, jnp.int32)
    targets = {0: (out_mid, in_mid), 1: (out_high, in_high), -1: (out_low, in_low)}

    def carry_refs(dx, dy):
        src, dst = targets[dy]
        at = dx + 1 if dy < 0 else dx + 2
        return src.at[at], dst.at[at]

    for _, _, _, ok_from, dx, dy in carries:

        @pl.when(jnp.logical_not(ok_from))
        def _(dx=dx, dy=dy):
            dst = carry_refs(dx, dy)[1]
            dst[...] = jnp.zeros(dst.shape, jnp.float32)

    for copy in loads:
        copy.wait()
    orders = orders_ref[0]
    order_line[0] = orders[0:1]
    order_line[1] = orders[cells_y - 1 : cells_y]
    tile = (MODES, cells_y, cells_z)
    last_mode = lax.broadcasted_iota(jnp.int32, tile, 0)
    lane = lax.broadcasted_iota(jnp.int32, (1, 1, cells_z), 2)

    def active(a, b):
        return jnp.maximum(jnp.maximum(a, b), last_mode) <= orders[None]

    def loop(body, low=0, high=MODES):
        def step(index, carry):
            body(index)
            return carry

        lax.fori_loop(low, high, step, 0)

    def x_copy(side, b, to):
        return pltpu.make_async_remote_copy(
            src_ref=xs.at[side, b], dst_ref=xr.at[side, b],
            send_sem=x_send.at[side, b], recv_sem=x_recv.at[side, b],
            device_id=to, device_id_type=MESH,
        )

    def to_relay(side, b, to):
        return pltpu.make_async_remote_copy(
            src_ref=xs.at[side, b], dst_ref=relay.at[side, b],
            send_sem=x_send.at[side, b], recv_sem=relay_in.at[side, b],
            device_id=to, device_id_type=MESH,
        )

    def from_relay(side, b, to):
        return pltpu.make_async_remote_copy(
            src_ref=relay.at[side, b], dst_ref=xr.at[side, b],
            send_sem=relay_out.at[side, b], recv_sem=x_recv.at[side, b],
            device_id=to, device_id_type=MESH,
        )

    def forward(number):
        for side in range(2):
            back, relaying, target = relays[side][2:]

            @pl.when(relaying)
            def _():
                to_relay(side, number, target).wait_recv()
                from_relay(side, number, target).start()

    def x_receive(number):
        for side in range(2):

            @pl.when(halos[side][3])
            def _():
                x_copy(side, number, halos[side][0]).wait_recv()

    def x_traces(b):
        rhs_load(b).wait()
        values = []
        for a in range(MODES):
            value = jnp.where(active(a, b), table_ref[a, b] * rhs[a, b], 0.0)
            first[a, b] = value
            values.append(value)
        sides = traces(values)
        for side in range(2):
            for kind in range(2):
                xs[side, b, kind] = sides[side][kind]

    def x_start(b):
        for side in range(2):
            to, ok_to = halos[side][:2]
            via, used = relays[side][:2]
            if b < RELAYED:

                @pl.when(used)
                def _():
                    to_relay(side, b, via).start()

                ok_to = ok_to & jnp.logical_not(used)

            @pl.when(ok_to)
            def _():
                x_copy(side, b, to).start()

    loop(x_traces, 0, 2)
    pl.semaphore_wait(barrier, expected)
    over(start, 1, 0)
    x_start(0)
    x_start(1)
    over(start, 1, 1)
    over(start, 1, 2)
    loop(x_traces, 2)
    x_start(2)

    def y_faces(a, values, send, up_buf, down_buf):
        down, up = traces(values)
        for kind in range(2):
            up_buf[kind, a, :, 0:cells_y, :] = down[kind]
            down_buf[kind, a, :, 1 : cells_y + 1, :] = up[kind]
            send[0, kind, a] = down[kind][:, 0:1, :]
            send[1, kind, a] = up[kind][:, cells_y - 1 : cells_y, :]

    def y_neighbours(a, received, up_buf, down_buf):
        for kind in range(2):
            up_buf[kind, a, :, cells_y : cells_y + 1, :] = received[0, kind, a]
            down_buf[kind, a, :, 0:1, :] = received[1, kind, a]
        return face_terms(
            [up_buf[kind, a, :, 1 : cells_y + 1, :] for kind in range(2)],
            [down_buf[kind, a, :, 0:cells_y, :] for kind in range(2)],
        )

    def z_faces(a, values, send):
        sides = traces(values)
        for side in range(2):
            for kind in range(2):
                send[side, kind, a] = sides[side][kind]

    def z_neighbours(a, send, received):
        def moved(side, kind, edge, amount):
            picked = jnp.where(lane == edge, received[side, kind, a], send[side, kind, a])
            return pltpu.roll(picked, amount, 2)

        return face_terms(
            [moved(0, kind, 0, cells_z - 1) for kind in range(2)],
            [moved(1, kind, cells_z - 1, 1) for kind in range(2)],
        )

    loop(lambda a: y_faces(a, [first[a, b] for b in range(MODES)], ys, y_up, y_down))
    over(start, 0, 1)
    loop(lambda a: z_faces(a, [first[a, :, e] for e in range(MODES)], zs))
    over(start, 0, 2)
    x_start(3)

    def x_own(b):
        values = [first[a, b] for a in range(MODES)]
        for a in range(MODES):
            acc[a, b] = own_row(a, values)

    def y_own(a):
        values = [first[a, b] for b in range(MODES)]
        for b in range(MODES):
            acc[a, b] += own_row(b, values)

    def z_own(a):
        values = [first[a, :, e] for e in range(MODES)]
        for e in range(MODES):
            acc[a, :, e] += own_row(e, values)

    loop(x_own)
    loop(y_own)
    loop(z_own)
    for axis in range(3):
        over(receive, 1, axis)
    orders_edge = jnp.where(lane[0] == cells_z - 1, order_z[1], order_z[0])
    for side in range(2):
        pack[side, 1 : cells_y + 1] = orders
        pack[side, 0:1] = order_y[1]
        pack[side, cells_y + 1 : cells_y + 2] = order_y[0]
        pack[side, tall : tall + cells_y] = orders_edge
        pack[side, 2 * tall : 2 * tall + cells_y] = order_x[side]
    over(start, 2, 0)
    x_start(4)
    over(receive, 0, 2)

    def z_flux(a):
        term = z_neighbours(a, zs, zr)
        for e in range(MODES):
            acc[a, :, e] += term(e)

    loop(z_flux)
    x_start(5)
    forward(0)
    over(receive, 0, 1)

    def y_flux(a):
        term = y_neighbours(a, yr, y_up, y_down)
        for b in range(MODES):
            right = rhs[a, b]
            total = acc[a, b] + term(b)
            scale = jnp.where(active(a, b), table_ref[a, b], 0.0)
            acc[a, b] = scale * (KEEP * right + STEP * (right - total))
            coef[a, b] = scale * (-STEP)

    loop(y_flux)
    x_start(6)
    forward(1)

    slots = iter(range(pads.shape[0]))

    def padded(value, at):
        slot = next(slots)
        pads[slot, at : at + cells_y, :] = value
        return pads[slot]

    near, border, layers = {}, {}, {}

    def gather_into(where_to, key, value):
        where_to[key] = where_to[key] + value if key in where_to else value

    def spread(values, shift, forced, tile_orders, low_orders, high_orders, edge_orders):
        centre, edge, x_low, x_high, y_low, y_high = {}, {}, {}, {}, {}, {}
        for b in range(2):
            line = [values[a, b, 0:2] for a in range(MODES)]
            down, up = traces(line)
            for a in range(2):
                own = own_row(a, line)
                below, above = one_sided(down, a, False), one_sided(up, a, True)
                for e in range(2):
                    centre[a, b, e] = forced[a, b, e] - own[e] if forced is not None else -own[e]
                    x_low[a, b, e] = jnp.where(low_orders >= max(a, b, e), -below[e], 0.0)
                    x_high[a, b, e] = jnp.where(high_orders >= max(a, b, e), -above[e], 0.0)
        for a in range(2):
            line = [values[a, b, 0:2] for b in range(MODES)]
            down, up = traces(line)
            for b in range(2):
                own = own_row(b, line)
                below, above = one_sided(down, b, False), one_sided(up, b, True)
                for e in range(2):
                    centre[a, b, e] = centre[a, b, e] - own[e]
                    y_low[a, b, e], y_high[a, b, e] = below[e], above[e]
            line = [values[a, 0:2, e] for e in range(MODES)]
            down, up = traces(line)
            for e in range(2):
                below = pltpu.roll(one_sided(down, e, False), cells_z - 1, 2)
                above = pltpu.roll(one_sided(up, e, True), 1, 2)
                inner = jnp.where(lane == cells_z - 1, 0.0, below) + jnp.where(lane == 0, 0.0, above)
                outer = jnp.where(lane == cells_z - 1, below, jnp.where(lane == 0, above, 0.0))
                own = own_row(e, line) + inner
                for b in range(2):
                    centre[a, b, e] = centre[a, b, e] - own[b]
                    edge[a, b, e] = jnp.where(edge_orders >= max(a, b, e), -outer[b], 0.0)
        resid = {}
        for key in OCTET:
            total = padded(centre[key], 1) - padded(y_low[key], 0) - padded(y_high[key], 2)
            resid[key] = jnp.where(tile_orders >= max(key), total, 0.0)
        resid, edge, x_low, x_high = corners(resid), corners(edge), corners(x_low), corners(x_high)
        for i, j, k in OCTET:
            moved = pltpu.roll(resid[i, j, k], 1, 0) if j else resid[i, j, k]
            gather_into(layers, (shift + i, k), moved)
            gather_into(border, (shift + i, j, k), edge[i, j, k])
            gather_into(near, (shift - 1 + i, j, k), x_low[i, j, k])
            gather_into(near, (shift + 1 + i, j, k), x_high[i, j, k])

    def ghost(values, side, other_orders):
        def put(a, b, high):
            part = slice(0, high)
            data = [xs[side, b, kind, part] for kind in range(2)]
            modes = jnp.maximum(last_mode[part], max(a, b))
            scale = jnp.where(modes <= other_orders[None], table_ref[a, b, part], 0.0) * (-STEP)
            values[a, b, part] = scale * one_sided(data, a, side == 1)

        for b in range(2):
            for a in range(MODES):
                put(a, b, MODES if a < 2 else 2)
        for b in range(2, MODES):
            for a in range(2):
                put(a, b, 2)

    spread(acc, 0, rhs, pack[0, 0:tall], order_x[1], order_x[0], orders_edge)
    ghost(first, 1, order_x[0])
    ghost(smooth, 0, order_x[1])
    forward(2)
    over(receive, 2, 0)
    far = slice(2 * tall, 2 * tall + cells_y)
    rim = slice(tall, tall + cells_y)
    spread(first, 1, None, pack_in[0, 0:tall], orders, pack_in[0, far], pack_in[0, rim])
    spread(smooth, -1, None, pack_in[1, 0:tall], pack_in[1, far], orders, pack_in[1, rim])

    row_lane = lane[0]
    sums = {}
    for dx in REACH:
        pair = []
        for k in range(2):
            parts = [layers[dx, k]] if (dx, k) in layers else []
            parts += [padded(near[dx, j, k], 1 + j) for j in range(2)]
            pair.append(functools.reduce(lambda p, q: p + q, parts))
        moved = pltpu.roll(pair[1], 1, 1)
        if (dx, 0, 0) in border:
            outer = [padded(border[dx, 0, k], 1) + padded(border[dx, 1, k], 2) for k in range(2)]
            outer_moved = pltpu.roll(outer[1], 1, 1)
            inside = pair[0] + jnp.where(row_lane == 0, outer_moved, moved)
            beyond = jnp.where(row_lane == 0, moved, outer_moved) + outer[0]
        else:
            inside = pair[0] + jnp.where(row_lane == 0, 0.0, moved)
            beyond = jnp.where(row_lane == 0, moved, 0.0)
        for part, value in enumerate((inside, beyond)):
            if dx == 0:
                sums[part] = value[1 : cells_y + 1]
            else:
                out_mid[dx + 2, part] = value[1 : cells_y + 1]
            out_high[dx + 2, part] = value[cells_y + 1 : cells_y + 3]
            if -1 <= dx <= 2:
                out_low[dx + 1, part] = value[0:1]

    for number, entry in enumerate(carries):
        start(entry, 14 + number, *carry_refs(*entry[4:]))
    forward(3)

    def x_flux(b):
        x_receive(b)
        term = face_terms(
            [xr[0, b, kind] for kind in range(2)], [xr[1, b, kind] for kind in range(2)]
        )
        for a in range(MODES):
            smooth[a, b] = acc[a, b] + coef[a, b] * term(a)

    loop(x_flux, RELAYED)

    for number, entry in enumerate(carries):
        receive(entry, 14 + number, *carry_refs(*entry[4:]))

    for part in range(2):
        value = sums[part]
        for dx in REACH:
            if dx:
                value = value + in_mid[dx + 2, part]
        high = functools.reduce(lambda p, q: p + q, [in_high[at, part] for at in range(6)])
        low = functools.reduce(lambda p, q: p + q, [in_low[at, part] for at in range(4)])
        column[pl.ds(z, 1), part] = value[None]
        column[pl.ds(z, 1), part, 0:2] += high[None]
        column[pl.ds(z, 1), part, cells_y - 1 : cells_y] += low[None]

    def gather(number, arriving):
        entry = columns[number]
        at = entry[4] if arriving else z
        return remote(column.at[at], column.at[at], 14 + len(carries) + number, entry[0])

    for number in range(len(columns)):
        gather(number, False).start()
    loop(x_flux, 0, RELAYED)
    for number in range(len(columns)):
        gather(number, True).wait_recv()

    row = lax.broadcasted_iota(jnp.int32, (cells_y, cells_z), 0)
    spot = lax.broadcasted_iota(jnp.int32, (cells_y, cells_z), 1)
    for zz in range(nz):
        total = column[zz, 0]
        if zz > 0:
            total = total + jnp.where(spot < 2, column[zz - 1, 1], 0.0)
        if zz < nz - 1:
            total = total + jnp.where(spot == cells_z - 1, column[zz + 1, 1], 0.0)
        inside = (x > 0) & ((row > 0) | (y > 0))
        if zz == 0:
            inside = inside & (spot > 0)
        coarse_ref[0, :, zz * cells_z : (zz + 1) * cells_z] = jnp.where(inside, total, 0.0)

    for stage in range(3):
        for axis in range(len(stages[stage])):
            if (stage, axis) != (0, 0):
                over(finish, stage, axis)
    for b in range(MODES):
        for side in range(2):

            @pl.when(halos[side][1])
            def _():
                x_copy(side, b, halos[side][0]).wait_send()

    for b in range(RELAYED):
        for side in range(2):

            @pl.when(relays[side][3])
            def _():
                from_relay(side, b, relays[side][4]).wait_send()

    for number, entry in enumerate(carries):
        finish(entry, 14 + number, *carry_refs(*entry[4:]))
    for number in range(len(columns)):
        gather(number, False).wait_send()


def drain(smooth, coarse, smooth_hbm, coarse_hbm, sem):
    copies = [
        pltpu.make_async_copy(smooth.at[a], smooth_hbm.at[a], sem.at[a]) for a in range(MODES)
    ]
    copies.append(pltpu.make_async_copy(coarse, coarse_hbm, sem.at[MODES]))
    for copy in copies:
        copy.start()
    for copy in copies:
        copy.wait()


def per_device(sizes, rhs, orders):
    _, cells_y, cells_z = orders.shape
    nz = sizes[2]
    table = jnp.asarray(
        np.broadcast_to(
            (1.0 / (DIAGONAL * THETA))[:, :, :, None, None], DIAGONAL.shape + (1, cells_z)
        ),
        jnp.float32,
    )
    field = rhs.reshape(rhs.shape[:3] + rhs.shape[4:])
    cells = (cells_y, cells_z)
    rows = 8 * ((cells_y + 8) // 8)
    tall = 8 * ((cells_y + 10) // 8)
    line = (2, 2, MODES, MODES)

    def buf(*shape):
        return pltpu.VMEM(shape, jnp.float32)

    def whole(*shape):
        return pltpu.VMEM(shape, jnp.int32)

    slots = 14 + len(CARRIES) + nz - 1
    coarse_shape = (1, cells_y, nz * cells_z)
    vmem = pl.BlockSpec(memory_space=pltpu.VMEM)
    hbm = pl.BlockSpec(memory_space=pltpu.HBM)
    smoothed, coarse = pl.pallas_call(
        functools.partial(kernel, sizes, cells_y, cells_z),
        out_shape=(pltpu.VMEM(field.shape, jnp.float32), pltpu.VMEM(coarse_shape, jnp.float32)),
        in_specs=[hbm, hbm, hbm],
        out_specs=(vmem, vmem),
        scratch_shapes=[buf(*field.shape)] * 4
        + [
            whole(*orders.shape), buf(*table.shape),
            buf(2, MODES, 2, MODES, *cells), buf(2, MODES, 2, MODES, *cells),
            buf(*line, 1, cells_z), buf(*line, 1, cells_z),
            buf(*line, *cells), buf(*line, *cells),
            buf(2, MODES, MODES, rows, cells_z), buf(2, MODES, MODES, rows, cells_z),
            whole(2, 1, cells_z), whole(2, *cells), whole(2, 1, cells_z), whole(2, *cells),
            whole(2, 3 * tall, cells_z), whole(2, 3 * tall, cells_z), buf(112, tall, cells_z),
            buf(6, 2, *cells), buf(6, 2, 2, cells_z), buf(4, 2, 1, cells_z),
            buf(6, 2, *cells), buf(6, 2, 2, cells_z), buf(4, 2, 1, cells_z),
            buf(nz, 2, *cells),
            buf(2, RELAYED, 2, MODES, *cells),
            pltpu.SemaphoreType.DMA((MODES + 2,)),
            pltpu.SemaphoreType.DMA((slots,)),
            pltpu.SemaphoreType.DMA((slots,)),
            pltpu.SemaphoreType.DMA((2, MODES)),
            pltpu.SemaphoreType.DMA((2, MODES)),
            pltpu.SemaphoreType.DMA((2, RELAYED)),
            pltpu.SemaphoreType.DMA((2, RELAYED)),
        ],
        compiler_params=pltpu.CompilerParams(collective_id=0, has_side_effects=True),
        name="smoother",
    )(field, orders, table)
    smoothed, coarse = pl.pallas_call(
        drain,
        out_shape=(
            jax.ShapeDtypeStruct(field.shape, jnp.float32),
            jax.ShapeDtypeStruct(coarse_shape, jnp.float32),
        ),
        in_specs=[vmem, vmem],
        out_specs=(hbm, hbm),
        scratch_shapes=[pltpu.SemaphoreType.DMA((MODES + 1,))],
        name="drain",
    )(
        pltpu.with_memory_space_constraint(smoothed, pltpu.VMEM),
        pltpu.with_memory_space_constraint(coarse, pltpu.VMEM),
    )
    return smoothed.reshape(rhs.shape), coarse


def solution(mesh):
    sizes = tuple(mesh.shape[axis] for axis in ("gx", "gy", "gz"))
    return jax.shard_map(
        functools.partial(per_device, sizes),
        mesh=mesh,
        in_specs=(P(None, None, None, "gx", "gy", "gz"), P("gx", "gy", "gz")),
        out_specs=(P(None, None, None, "gx", "gy", "gz"), P("gx", "gy", None)),
        check_vma=False,
    )
```

```python
import functools

import jax
import jax.numpy as jnp
import numpy as np
from jax import lax
from jax.experimental import pallas as pl
from jax.experimental.pallas import tpu as pltpu
from jax.sharding import PartitionSpec as P

PENALTY = 49.0
EIGEN_HIGH = 2.4
EIGEN_LOW = 0.24
MODES = 7
MESH = pl.DeviceIdType.MESH


def tables():
    degree = np.arange(MODES)
    normed = np.sqrt((2.0 * degree + 1.0) / 2.0)
    smaller = np.minimum(degree[:, None], degree[None, :])
    parity = (degree[:, None] + degree[None, :]) % 2 == 0
    stiffness = np.where(parity, normed[:, None] * normed[None, :] * smaller * (smaller + 1), 0.0)
    signs = (-1.0) ** degree
    slope = normed * degree * (degree + 1) / 2.0
    low, low_slope = normed * signs, -slope * signs
    own = stiffness + np.outer(normed, PENALTY * normed - 0.5 * slope) - 0.5 * np.outer(slope, normed)
    own = own + np.outer(low, PENALTY * low + 0.5 * low_slope) + 0.5 * np.outer(low_slope, low)
    one_axis = normed * normed * degree * (degree + 1) + 2.0 * (
        PENALTY * normed * normed - normed * slope
    )
    diagonal = (
        one_axis[:, None, None] + one_axis[None, :, None] + one_axis[None, None, :]
    ) / PENALTY
    return (
        own / PENALTY,
        0.5 * slope - PENALTY * normed,
        0.5 * normed,
        normed / PENALTY,
        slope / PENALTY,
        diagonal,
    )


OWN, JUMP, HALF, VALUE, SLOPE, DIAGONAL = tables()
THETA = 0.5 * (EIGEN_HIGH + EIGEN_LOW)
DELTA = 0.5 * (EIGEN_HIGH - EIGEN_LOW)
RHO_FIRST = DELTA / THETA
RHO_SECOND = 1.0 / (2.0 * THETA / DELTA - RHO_FIRST)
KEEP = 1.0 + RHO_SECOND * RHO_FIRST
STEP = 2.0 * RHO_SECOND / DELTA * THETA


def combine(weights, values):
    total = None
    for weight, value in zip(weights, values):
        term = value * float(weight)
        total = term if total is None else total + term
    return total


def traces(values):
    even, odd = values[0::2], values[1::2]
    jump_even, jump_odd = combine(JUMP[0::2], even), combine(JUMP[1::2], odd)
    half_even, half_odd = combine(HALF[0::2], even), combine(HALF[1::2], odd)
    down = (jump_even - jump_odd, half_even - half_odd)
    up = (jump_even + jump_odd, half_even + half_odd)
    return down, up


def own_row(row, values):
    start = row % 2
    return combine(OWN[row, start::2], values[start::2])


def face_terms(from_up, from_down):
    both = (from_up[0] + from_down[0], from_up[1] + from_down[1])
    apart = (from_up[0] - from_down[0], from_up[1] - from_down[1])

    def term(mode):
        pair = both if mode % 2 == 0 else apart
        if mode == 0:
            return pair[0] * float(VALUE[0])
        return pair[0] * float(VALUE[mode]) + pair[1] * float(SLOPE[mode])

    return term


def vertex_pair(zero, one):
    flat, tilt = np.sqrt(0.5) * zero, (np.sqrt(1.5) / 3.0) * one
    return flat - tilt, flat + tilt


def one_sided(data, mode, from_below):
    if mode == 0:
        return data[0] * float(VALUE[0])
    sign = -1.0 if from_below and mode % 2 else 1.0
    return data[0] * (sign * float(VALUE[mode])) + data[1] * (sign * float(SLOPE[mode]))


def corners(values):
    for axis in range(3):
        done = {}
        for key in values:
            if key[axis] == 0:
                other = tuple(1 if n == axis else key[n] for n in range(3))
                done[key], done[other] = vertex_pair(values[key], values[other])
        values = done
    return values


OCTET = [(a, b, e) for a in range(2) for b in range(2) for e in range(2)]
RELAYED = 4
SIGNS = (1, -1)
DIAGONALS = (
    [(dx, dy, 0) for dx in SIGNS for dy in SIGNS]
    + [(dx, 0, dz) for dx in SIGNS for dz in SIGNS]
    + [(2 * dx, 0, 0) for dx in SIGNS]
)
Y_PARTS = ((slice(0, 2), slice(0, MODES)), (slice(2, MODES), slice(0, 2)), (slice(2, MODES), slice(2, MODES)))
REACH = range(-2, 4)
CARRIES = (
    (3, 1), (2, 1), (-2, 1), (1, 1), (-1, 1), (2, -1), (1, -1), (-1, -1),
    (3, 0), (2, 0), (-2, 0), (1, 0), (-1, 0), (0, 1), (0, -1),
)


def kernel(
    sizes, cells_y, cells_z, rhs_hbm, orders_hbm, table_hbm, smooth, coarse_ref,
    rhs, first, acc, coef, lead, ghost_up, ghost_down, orders_ref, table_ref,
    xs, xr, ys, yr, zs, zr, y_up, y_down,
    order_line, order_x, order_y, order_z, order_xy, order_xz, order_far, order_tile, pads,
    out_mid, out_high, out_low, in_mid, in_high, in_low, column,
    relay, local_sem, send_sem, recv_sem, x_send, x_recv, y_send, y_recv, relay_in, relay_out,
):
    nx, ny, nz = sizes
    tall = pads.shape[1]
    x, y, z = lax.axis_index("gx"), lax.axis_index("gy"), lax.axis_index("gz")
    barrier = pltpu.get_barrier_semaphore()

    def neighbour(axis, sign):
        here = (x, y, z)[axis]
        to = [x, y, z]
        to[axis] = here + sign
        back = [x, y, z]
        back[axis] = here - sign
        below, above = here > 0, here < sizes[axis] - 1
        return (tuple(to), below if sign < 0 else above, tuple(back), above if sign < 0 else below)

    halos = [neighbour(axis, sign) for axis in range(3) for sign in (-1, 1)]
    always = x >= 0

    def offset(dx, dy):
        ok_to = (x + dx > 0) & (x + dx < nx)
        ok_from = (x > 0) & (x - dx >= 0) & (x - dx < nx)
        if dy > 0:
            ok_to, ok_from = ok_to & (y + dy < ny), ok_from & (y >= dy)
        if dy < 0:
            ok_to, ok_from = ok_to & (y + dy >= 0), ok_from & (y - dy < ny)
        return ((x + dx, y + dy, z), ok_to, (x - dx, y - dy, z), ok_from)

    carries = [offset(dx, dy) + (dx, dy) for dx, dy in CARRIES]
    columns = []
    for r in range(1, nz):
        source = lax.rem(z - r + nz, nz)
        columns.append(((x, y, lax.rem(z + r, nz)), always, (x, y, source), always, source))

    def diagonal(offset):
        here = (x, y, z)
        to = tuple(h + d for h, d in zip(here, offset))
        back = tuple(h - d for h, d in zip(here, offset))
        ok_to, ok_from = always, always
        for axis, d in enumerate(offset):
            low, high = here[axis] >= abs(d), here[axis] + abs(d) < sizes[axis]
            if d > 0:
                ok_to, ok_from = ok_to & high, ok_from & low
            elif d < 0:
                ok_to, ok_from = ok_to & low, ok_from & high
        return (to, ok_to, back, ok_from)

    diagonals = [diagonal(offset) for offset in DIAGONALS]

    def diagonal_refs(offset):
        dx, dy, dz = offset
        if dy:
            return order_line.at[0 if dy < 0 else 1], order_xy.at[(1 + dx) // 2, (1 + dy) // 2]
        if dz:
            return orders_ref.at[0], order_xz.at[(1 + dx) // 2, (1 + dz) // 2]
        return orders_ref.at[0], order_far.at[(2 + dx) // 4]

    odd = lax.rem(x, 2) == 1
    even = jnp.logical_not(odd)
    relays = (
        ((x - 2, y, z), even & (x >= 2), (x + 2, y, z), even & (x + 2 < nx), (x + 1, y, z)),
        ((x + 2, y, z), odd & (x + 2 < nx), (x - 2, y, z), odd & (x >= 3), (x - 1, y, z)),
    )

    expected = jnp.int32(0)
    for entry in halos[:4] + columns + diagonals + carries[:1]:
        to, ok_to, back, ok_from = entry[:4]

        @pl.when(ok_from)
        def _(back=back):
            pl.semaphore_signal(barrier, inc=1, device_id=back, device_id_type=MESH)

        expected = expected + jnp.where(ok_to, 1, 0).astype(jnp.int32)

    loads = [
        pltpu.make_async_copy(orders_hbm, orders_ref, local_sem.at[MODES]),
        pltpu.make_async_copy(table_hbm, table_ref, local_sem.at[MODES + 1]),
    ]
    for copy in loads:
        copy.start()

    def rhs_load(b):
        return pltpu.make_async_copy(rhs_hbm.at[:, b], rhs.at[:, b], local_sem.at[b])

    for b in range(MODES):
        rhs_load(b).start()

    def remote(src, dst, slot, to):
        if isinstance(slot, tuple):
            return pltpu.make_async_remote_copy(
                src_ref=src, dst_ref=dst, send_sem=y_send.at[slot], recv_sem=y_recv.at[slot],
                device_id=to, device_id_type=MESH,
            )
        return pltpu.make_async_remote_copy(
            src_ref=src, dst_ref=dst, send_sem=send_sem.at[slot], recv_sem=recv_sem.at[slot],
            device_id=to, device_id_type=MESH,
        )

    def start(entry, slot, src, dst):
        to, ok_to = entry[:2]

        @pl.when(ok_to)
        def _():
            remote(src, dst, slot, to).start()

    def receive(entry, slot, src, dst):
        to, _, _, ok_from = entry[:4]

        @pl.when(ok_from)
        def _():
            remote(src, dst, slot, to).wait_recv()

    def finish(entry, slot, src, dst):
        to, ok_to = entry[:2]

        @pl.when(ok_to)
        def _():
            remote(src, dst, slot, to).wait_send()

    stages = (
        ((xs, xr), (ys, yr), (zs, zr)),
        ((orders_ref, order_x), (order_line, order_y), (orders_ref, order_z)),
    )

    def over(action, stage, axis):
        src, dst = stages[stage][axis]
        for side in range(2):
            index = 2 * axis + side
            action(halos[index], 6 * stage + index, src.at[0 if src is orders_ref else side], dst.at[side])

    for stage, empty in ((0, 0.0), (1, -1)):
        for axis in range(3):
            for side in range(2):
                dst = stages[stage][axis][1]

                @pl.when(jnp.logical_not(halos[2 * axis + side][3]))
                def _(dst=dst, side=side, empty=empty):
                    dst[side] = jnp.full(dst.shape[1:], empty, dst.dtype)

    pads[...] = jnp.zeros(pads.shape, jnp.float32)
    order_tile[...] = jnp.full(order_tile.shape, -1, jnp.int32)
    for offset, entry in zip(DIAGONALS, diagonals):

        @pl.when(jnp.logical_not(entry[3]))
        def _(offset=offset):
            dst = diagonal_refs(offset)[1]
            dst[...] = jnp.full(dst.shape, -1, jnp.int32)

    targets = {0: (out_mid, in_mid), 1: (out_high, in_high), -1: (out_low, in_low)}

    def carry_refs(dx, dy):
        src, dst = targets[dy]
        at = dx + 1 if dy < 0 else dx + 2
        return src.at[at], dst.at[at]

    for _, _, _, ok_from, dx, dy in carries:

        @pl.when(jnp.logical_not(ok_from))
        def _(dx=dx, dy=dy):
            dst = carry_refs(dx, dy)[1]
            dst[...] = jnp.zeros(dst.shape, jnp.float32)

    for copy in loads:
        copy.wait()
    orders = orders_ref[0]
    order_line[0] = orders[0:1]
    order_line[1] = orders[cells_y - 1 : cells_y]
    tile = (MODES, cells_y, cells_z)
    last_mode = lax.broadcasted_iota(jnp.int32, tile, 0)
    lane = lax.broadcasted_iota(jnp.int32, (1, 1, cells_z), 2)

    def active(a, b):
        return jnp.maximum(jnp.maximum(a, b), last_mode) <= orders[None]

    def loop(body, low=0, high=MODES):
        def step(index, carry):
            body(index)
            return carry

        lax.fori_loop(low, high, step, 0)

    def x_copy(side, b, to):
        return pltpu.make_async_remote_copy(
            src_ref=xs.at[side, b], dst_ref=xr.at[side, b],
            send_sem=x_send.at[side, b], recv_sem=x_recv.at[side, b],
            device_id=to, device_id_type=MESH,
        )

    def to_relay(side, b, to):
        return pltpu.make_async_remote_copy(
            src_ref=xs.at[side, b], dst_ref=relay.at[side, b],
            send_sem=x_send.at[side, b], recv_sem=relay_in.at[side, b],
            device_id=to, device_id_type=MESH,
        )

    def from_relay(side, b, to):
        return pltpu.make_async_remote_copy(
            src_ref=relay.at[side, b], dst_ref=xr.at[side, b],
            send_sem=relay_out.at[side, b], recv_sem=x_recv.at[side, b],
            device_id=to, device_id_type=MESH,
        )

    def forward(number):
        for side in range(2):
            back, relaying, target = relays[side][2:]

            @pl.when(relaying)
            def _():
                to_relay(side, number, target).wait_recv()
                from_relay(side, number, target).start()

    def x_receive(number):
        for side in range(2):

            @pl.when(halos[side][3])
            def _():
                x_copy(side, number, halos[side][0]).wait_recv()

    def x_traces(b):
        rhs_load(b).wait()
        values = []
        for a in range(MODES):
            value = jnp.where(active(a, b), table_ref[a, b] * rhs[a, b], 0.0)
            first[a, b] = value
            values.append(value)
        sides = traces(values)
        for side in range(2):
            for kind in range(2):
                xs[side, b, kind] = sides[side][kind]

    def x_start(b):
        for side in range(2):
            to, ok_to = halos[side][:2]
            via, used = relays[side][:2]
            if b < RELAYED:

                @pl.when(used)
                def _():
                    to_relay(side, b, via).start()

                ok_to = ok_to & jnp.logical_not(used)

            @pl.when(ok_to)
            def _():
                x_copy(side, b, to).start()

    def diagonal_over(action):
        for number, (offset, entry) in enumerate(zip(DIAGONALS, diagonals)):
            action(entry, 14 + number, *diagonal_refs(offset))

    def y_over(action, part):
        modes = Y_PARTS[part]
        for side in range(2):
            at = (side, slice(None)) + modes
            action(halos[2 + side], (side, part), ys.at[at], yr.at[at])

    loop(x_traces, 0, 2)
    pl.semaphore_wait(barrier, expected)
    over(start, 1, 0)
    diagonal_over(start)
    x_start(0)
    x_start(1)
    over(start, 1, 1)
    over(start, 1, 2)
    loop(x_traces, 2)

    def y_faces(a, values, send, up_buf, down_buf):
        down, up = traces(values)
        for kind in range(2):
            up_buf[kind, a, :, 0:cells_y, :] = down[kind]
            down_buf[kind, a, :, 1 : cells_y + 1, :] = up[kind]
            send[0, kind, a] = down[kind][:, 0:1, :]
            send[1, kind, a] = up[kind][:, cells_y - 1 : cells_y, :]

    def y_neighbours(a, received, up_buf, down_buf, part=slice(0, MODES)):
        for kind in range(2):
            up_buf[kind, a, part, cells_y : cells_y + 1, :] = received[0, kind, a, part]
            down_buf[kind, a, part, 0:1, :] = received[1, kind, a, part]
        return (
            [up_buf[kind, a, part, 1 : cells_y + 1, :] for kind in range(2)],
            [down_buf[kind, a, part, 0:cells_y, :] for kind in range(2)],
        )

    def z_faces(a, values, send):
        sides = traces(values)
        for side in range(2):
            for kind in range(2):
                send[side, kind, a] = sides[side][kind]

    def z_neighbours(a, send, received, part=slice(0, MODES)):
        def moved(side, kind, edge, amount):
            picked = jnp.where(lane == edge, received[side, kind, a, part], send[side, kind, a, part])
            return pltpu.roll(picked, amount, 2)

        return (
            [moved(0, kind, 0, cells_z - 1) for kind in range(2)],
            [moved(1, kind, cells_z - 1, 1) for kind in range(2)],
        )

    def narrow(pair):
        return [[value[0:2] for value in side] for side in pair]

    def y_traces(a):
        y_faces(a, [first[a, b] for b in range(MODES)], ys, y_up, y_down)

    loop(y_traces, 0, 2)
    y_over(start, 0)
    loop(y_traces, 2)
    y_over(start, 1)
    y_over(start, 2)
    x_start(2)
    loop(lambda a: z_faces(a, [first[a, :, e] for e in range(MODES)], zs))
    over(start, 0, 2)
    x_start(3)

    few = slice(0, 2)

    def predict(a, b, part, total):
        right = rhs[a, b, part]
        modes = jnp.maximum(last_mode[part], jnp.maximum(a, b))
        scale = jnp.where(modes <= orders[None], table_ref[a, b, part], 0.0)
        return scale * (KEEP * right + STEP * (right - total)), scale * (-STEP)

    for b in range(2):
        values = [first[a, b] for a in range(MODES)]
        for a in range(2):
            lead[a, b] = own_row(a, values)
        values = [value[0:2] for value in values]
        for a in range(2, MODES):
            lead[a, b, few] = own_row(a, values)

    def lead_x(b):
        values = [first[a, b, few] for a in range(MODES)]
        for a in range(2):
            lead[a, b, few] = own_row(a, values)

    def lead_y(a):
        values = [first[a, b, few] for b in range(MODES)]
        for b in range(2):
            lead[a, b, few] += own_row(b, values)

    def lead_z(a):
        values = [first[a, few, e] for e in range(MODES)]
        for e in range(2):
            lead[a, few, e] += own_row(e, values)

    loop(lead_x, 2)
    for a in range(2):
        values = [first[a, b] for b in range(MODES)]
        for b in range(2):
            lead[a, b] += own_row(b, values)
        values = [value[0:2] for value in values]
        for b in range(2, MODES):
            lead[a, b, few] += own_row(b, values)
    loop(lead_y, 2)
    for a in range(2):
        values = [first[a, :, e] for e in range(MODES)]
        for e in range(2):
            lead[a, :, e] += own_row(e, values)
        values = [value[0:2] for value in values]
        for e in range(2, MODES):
            lead[a, few, e] += own_row(e, values)
    loop(lead_z, 2)
    over(receive, 0, 2)

    def lead_z_flux(a):
        term = face_terms(*z_neighbours(a, zs, zr, few))
        for e in range(2):
            lead[a, few, e] += term(e)

    for a in range(2):
        pair = z_neighbours(a, zs, zr)
        term = face_terms(*pair)
        for e in range(2):
            lead[a, :, e] += term(e)
        term = face_terms(*narrow(pair))
        for e in range(2, MODES):
            lead[a, few, e] += term(e)
    loop(lead_z_flux, 2)

    slots = iter(range(pads.shape[0]))

    def padded(value, at):
        slot = next(slots)
        pads[slot, at : at + cells_y, :] = value
        return pads[slot]

    near, border, layers = {}, {}, {}

    def gather_into(where_to, key, value):
        where_to[key] = where_to[key] + value if key in where_to else value

    def spread(values, shift, forced, tile_orders, low_orders, high_orders, edge_orders):
        centre, edge, x_low, x_high, y_low, y_high = {}, {}, {}, {}, {}, {}
        for b in range(2):
            line = [values[a, b, 0:2] for a in range(MODES)]
            down, up = traces(line)
            for a in range(2):
                own = own_row(a, line)
                below, above = one_sided(down, a, False), one_sided(up, a, True)
                for e in range(2):
                    centre[a, b, e] = forced[a, b, e] - own[e] if forced is not None else -own[e]
                    x_low[a, b, e] = jnp.where(low_orders >= max(a, b, e), -below[e], 0.0)
                    x_high[a, b, e] = jnp.where(high_orders >= max(a, b, e), -above[e], 0.0)
        for a in range(2):
            line = [values[a, b, 0:2] for b in range(MODES)]
            down, up = traces(line)
            for b in range(2):
                own = own_row(b, line)
                below, above = one_sided(down, b, False), one_sided(up, b, True)
                for e in range(2):
                    centre[a, b, e] = centre[a, b, e] - own[e]
                    y_low[a, b, e], y_high[a, b, e] = below[e], above[e]
            line = [values[a, 0:2, e] for e in range(MODES)]
            down, up = traces(line)
            for e in range(2):
                below = pltpu.roll(one_sided(down, e, False), cells_z - 1, 2)
                above = pltpu.roll(one_sided(up, e, True), 1, 2)
                inner = jnp.where(lane == cells_z - 1, 0.0, below) + jnp.where(lane == 0, 0.0, above)
                outer = jnp.where(lane == cells_z - 1, below, jnp.where(lane == 0, above, 0.0))
                own = own_row(e, line) + inner
                for b in range(2):
                    centre[a, b, e] = centre[a, b, e] - own[b]
                    edge[a, b, e] = jnp.where(edge_orders >= max(a, b, e), -outer[b], 0.0)
        resid = {}
        for key in OCTET:
            total = padded(centre[key], 1) - padded(y_low[key], 0) - padded(y_high[key], 2)
            resid[key] = jnp.where(tile_orders >= max(key), total, 0.0)
        resid, edge, x_low, x_high = corners(resid), corners(edge), corners(x_low), corners(x_high)
        for i, j, k in OCTET:
            moved = pltpu.roll(resid[i, j, k], 1, 0) if j else resid[i, j, k]
            gather_into(layers, (shift + i, k), moved)
            gather_into(border, (shift + i, j, k), edge[i, j, k])
            gather_into(near, (shift - 1 + i, j, k), x_low[i, j, k])
            gather_into(near, (shift + 1 + i, j, k), x_high[i, j, k])

    def ghost(values, side, other_orders):
        def put(a, b, high):
            part = slice(0, high)
            data = [xs[side, b, kind, part] for kind in range(2)]
            modes = jnp.maximum(last_mode[part], max(a, b))
            scale = jnp.where(modes <= other_orders[None], table_ref[a, b, part], 0.0) * (-STEP)
            values[a, b, part] = scale * one_sided(data, a, side == 1)

        for b in range(2):
            for a in range(MODES):
                put(a, b, MODES if a < 2 else 2)
        for b in range(2, MODES):
            for a in range(2):
                put(a, b, 2)

    for axis in range(3):
        over(receive, 1, axis)
    diagonal_over(receive)
    edges = []
    rows_of = (orders, order_x[0], order_x[1])
    lines_of = (order_y, order_xy.at[0], order_xy.at[1])
    sides_of = (order_z, order_xz.at[0], order_xz.at[1])
    for at in range(3):
        order_tile[at, 1 : cells_y + 1] = rows_of[at]
        order_tile[at, 0:1] = lines_of[at][1]
        order_tile[at, cells_y + 1 : cells_y + 2] = lines_of[at][0]
        edges.append(jnp.where(lane[0] == cells_z - 1, sides_of[at][1], sides_of[at][0]))
    ghost(ghost_up, 1, order_x[0])
    ghost(ghost_down, 0, order_x[1])
    spread(ghost_up, 1, None, order_tile[1], orders, order_far[0], edges[1])
    x_start(4)
    spread(ghost_down, -1, None, order_tile[2], order_far[1], orders, edges[2])
    forward(0)
    y_over(receive, 0)
    y_over(receive, 1)

    def lead_y_flux(a):
        term = face_terms(*y_neighbours(a, yr, y_up, y_down, few))
        for b in range(2):
            lead[a, b, few] = predict(a, b, few, lead[a, b, few] + term(b))[0]

    for a in range(2):
        pair = y_neighbours(a, yr, y_up, y_down)
        term = face_terms(*pair)
        for b in range(2):
            lead[a, b] = predict(a, b, slice(0, MODES), lead[a, b] + term(b))[0]
        term = face_terms(*narrow(pair))
        for b in range(2, MODES):
            lead[a, b, few] = predict(a, b, few, lead[a, b, few] + term(b))[0]
    loop(lead_y_flux, 2)
    spread(lead, 0, rhs, order_tile[0], order_x[1], order_x[0], edges[0])

    row_lane = lane[0]
    sums = {}
    for dx in REACH:
        pair = []
        for k in range(2):
            parts = [layers[dx, k]] if (dx, k) in layers else []
            parts += [padded(near[dx, j, k], 1 + j) for j in range(2)]
            pair.append(functools.reduce(lambda p, q: p + q, parts))
        moved = pltpu.roll(pair[1], 1, 1)
        if (dx, 0, 0) in border:
            outer = [padded(border[dx, 0, k], 1) + padded(border[dx, 1, k], 2) for k in range(2)]
            outer_moved = pltpu.roll(outer[1], 1, 1)
            inside = pair[0] + jnp.where(row_lane == 0, outer_moved, moved)
            beyond = jnp.where(row_lane == 0, moved, outer_moved) + outer[0]
        else:
            inside = pair[0] + jnp.where(row_lane == 0, 0.0, moved)
            beyond = jnp.where(row_lane == 0, moved, 0.0)
        for part, value in enumerate((inside, beyond)):
            if dx == 0:
                sums[part] = value[1 : cells_y + 1]
            else:
                out_mid[dx + 2, part] = value[1 : cells_y + 1]
            out_high[dx + 2, part] = value[cells_y + 1 : cells_y + 3]
            if -1 <= dx <= 2:
                out_low[dx + 1, part] = value[0:1]

    for number, entry in enumerate(carries):
        start(entry, 24 + number, *carry_refs(*entry[4:]))
    x_start(5)
    forward(1)

    def x_own(b):
        values = [first[a, b] for a in range(MODES)]
        for a in range(MODES):
            acc[a, b] = own_row(a, values)

    def y_own(a):
        values = [first[a, b] for b in range(MODES)]
        for b in range(MODES):
            acc[a, b] += own_row(b, values)

    def z_own(a):
        values = [first[a, :, e] for e in range(MODES)]
        for e in range(MODES):
            acc[a, :, e] += own_row(e, values)

    def z_flux(a):
        term = face_terms(*z_neighbours(a, zs, zr))
        for e in range(MODES):
            acc[a, :, e] += term(e)

    def y_flux(a):
        term = face_terms(*y_neighbours(a, yr, y_up, y_down))
        for b in range(MODES):
            acc[a, b], coef[a, b] = predict(a, b, slice(0, MODES), acc[a, b] + term(b))

    loop(x_own)
    x_start(6)
    forward(2)
    loop(y_own)
    forward(3)
    loop(z_own)
    loop(z_flux)
    y_over(receive, 2)
    loop(y_flux)

    def x_flux(b):
        x_receive(b)
        term = face_terms(
            [xr[0, b, kind] for kind in range(2)], [xr[1, b, kind] for kind in range(2)]
        )
        for a in range(MODES):
            smooth[a, b] = acc[a, b] + coef[a, b] * term(a)

    loop(x_flux, RELAYED)

    for number, entry in enumerate(carries):
        receive(entry, 24 + number, *carry_refs(*entry[4:]))

    for part in range(2):
        value = sums[part]
        for dx in REACH:
            if dx:
                value = value + in_mid[dx + 2, part]
        high = functools.reduce(lambda p, q: p + q, [in_high[at, part] for at in range(6)])
        low = functools.reduce(lambda p, q: p + q, [in_low[at, part] for at in range(4)])
        column[pl.ds(z, 1), part] = value[None]
        column[pl.ds(z, 1), part, 0:2] += high[None]
        column[pl.ds(z, 1), part, cells_y - 1 : cells_y] += low[None]

    def gather(number, arriving):
        entry = columns[number]
        at = entry[4] if arriving else z
        return remote(column.at[at], column.at[at], 24 + len(carries) + number, entry[0])

    for number in range(len(columns)):
        gather(number, False).start()
    loop(x_flux, 0, RELAYED)
    for number in range(len(columns)):
        gather(number, True).wait_recv()

    row = lax.broadcasted_iota(jnp.int32, (cells_y, cells_z), 0)
    spot = lax.broadcasted_iota(jnp.int32, (cells_y, cells_z), 1)
    for zz in range(nz):
        total = column[zz, 0]
        if zz > 0:
            total = total + jnp.where(spot < 2, column[zz - 1, 1], 0.0)
        if zz < nz - 1:
            total = total + jnp.where(spot == cells_z - 1, column[zz + 1, 1], 0.0)
        inside = (x > 0) & ((row > 0) | (y > 0))
        if zz == 0:
            inside = inside & (spot > 0)
        coarse_ref[0, :, zz * cells_z : (zz + 1) * cells_z] = jnp.where(inside, total, 0.0)

    for stage, axis in ((0, 2), (1, 0), (1, 1), (1, 2)):
        over(finish, stage, axis)
    for part in range(3):
        y_over(finish, part)
    diagonal_over(finish)
    for b in range(MODES):
        for side in range(2):

            @pl.when(halos[side][1])
            def _():
                x_copy(side, b, halos[side][0]).wait_send()

    for b in range(RELAYED):
        for side in range(2):

            @pl.when(relays[side][3])
            def _():
                from_relay(side, b, relays[side][4]).wait_send()

    for number, entry in enumerate(carries):
        finish(entry, 24 + number, *carry_refs(*entry[4:]))
    for number in range(len(columns)):
        gather(number, False).wait_send()


def drain(smooth, coarse, smooth_hbm, coarse_hbm, sem):
    copies = [
        pltpu.make_async_copy(smooth.at[a], smooth_hbm.at[a], sem.at[a]) for a in range(MODES)
    ]
    copies.append(pltpu.make_async_copy(coarse, coarse_hbm, sem.at[MODES]))
    for copy in copies:
        copy.start()
    for copy in copies:
        copy.wait()


def per_device(sizes, rhs, orders):
    _, cells_y, cells_z = orders.shape
    nz = sizes[2]
    table = jnp.asarray(
        np.broadcast_to(
            (1.0 / (DIAGONAL * THETA))[:, :, :, None, None], DIAGONAL.shape + (1, cells_z)
        ),
        jnp.float32,
    )
    field = rhs.reshape(rhs.shape[:3] + rhs.shape[4:])
    cells = (cells_y, cells_z)
    rows = 8 * ((cells_y + 8) // 8)
    tall = 8 * ((cells_y + 10) // 8)
    line = (2, 2, MODES, MODES)

    def buf(*shape):
        return pltpu.VMEM(shape, jnp.float32)

    def whole(*shape):
        return pltpu.VMEM(shape, jnp.int32)

    slots = 24 + len(CARRIES) + nz - 1
    coarse_shape = (1, cells_y, nz * cells_z)
    vmem = pl.BlockSpec(memory_space=pltpu.VMEM)
    hbm = pl.BlockSpec(memory_space=pltpu.HBM)
    smoothed, coarse = pl.pallas_call(
        functools.partial(kernel, sizes, cells_y, cells_z),
        out_shape=(pltpu.VMEM(field.shape, jnp.float32), pltpu.VMEM(coarse_shape, jnp.float32)),
        in_specs=[hbm, hbm, hbm],
        out_specs=(vmem, vmem),
        scratch_shapes=[buf(*field.shape)] * 7
        + [
            whole(*orders.shape), buf(*table.shape),
            buf(2, MODES, 2, MODES, *cells), buf(2, MODES, 2, MODES, *cells),
            buf(*line, 1, cells_z), buf(*line, 1, cells_z),
            buf(*line, *cells), buf(*line, *cells),
            buf(2, MODES, MODES, rows, cells_z), buf(2, MODES, MODES, rows, cells_z),
            whole(2, 1, cells_z), whole(2, *cells), whole(2, 1, cells_z), whole(2, *cells),
            whole(2, 2, 1, cells_z), whole(2, 2, *cells), whole(2, *cells), whole(3, tall, cells_z),
            buf(112, tall, cells_z),
            buf(6, 2, *cells), buf(6, 2, 2, cells_z), buf(4, 2, 1, cells_z),
            buf(6, 2, *cells), buf(6, 2, 2, cells_z), buf(4, 2, 1, cells_z),
            buf(nz, 2, *cells),
            buf(2, RELAYED, 2, MODES, *cells),
            pltpu.SemaphoreType.DMA((MODES + 2,)),
            pltpu.SemaphoreType.DMA((slots,)),
            pltpu.SemaphoreType.DMA((slots,)),
            pltpu.SemaphoreType.DMA((2, MODES)),
            pltpu.SemaphoreType.DMA((2, MODES)),
            pltpu.SemaphoreType.DMA((2, 3)),
            pltpu.SemaphoreType.DMA((2, 3)),
            pltpu.SemaphoreType.DMA((2, RELAYED)),
            pltpu.SemaphoreType.DMA((2, RELAYED)),
        ],
        compiler_params=pltpu.CompilerParams(collective_id=0, has_side_effects=True),
        name="smoother",
    )(field, orders, table)
    smoothed, coarse = pl.pallas_call(
        drain,
        out_shape=(
            jax.ShapeDtypeStruct(field.shape, jnp.float32),
            jax.ShapeDtypeStruct(coarse_shape, jnp.float32),
        ),
        in_specs=[vmem, vmem],
        out_specs=(hbm, hbm),
        scratch_shapes=[pltpu.SemaphoreType.DMA((MODES + 1,))],
        name="drain",
    )(
        pltpu.with_memory_space_constraint(smoothed, pltpu.VMEM),
        pltpu.with_memory_space_constraint(coarse, pltpu.VMEM),
    )
    return smoothed.reshape(rhs.shape), coarse


def solution(mesh):
    sizes = tuple(mesh.shape[axis] for axis in ("gx", "gy", "gz"))
    return jax.shard_map(
        functools.partial(per_device, sizes),
        mesh=mesh,
        in_specs=(P(None, None, None, "gx", "gy", "gz"), P("gx", "gy", "gz")),
        out_specs=(P(None, None, None, "gx", "gy", "gz"), P("gx", "gy", None)),
        check_vma=False,
    )
```

```python
import functools

import jax
import jax.numpy as jnp
import numpy as np
from jax import lax
from jax.experimental import pallas as pl
from jax.experimental.pallas import tpu as pltpu
from jax.sharding import PartitionSpec as P

PENALTY = 49.0
EIGEN_HIGH = 2.4
EIGEN_LOW = 0.24
MODES = 7
MESH = pl.DeviceIdType.MESH


def tables():
    degree = np.arange(MODES)
    normed = np.sqrt((2.0 * degree + 1.0) / 2.0)
    smaller = np.minimum(degree[:, None], degree[None, :])
    parity = (degree[:, None] + degree[None, :]) % 2 == 0
    stiffness = np.where(parity, normed[:, None] * normed[None, :] * smaller * (smaller + 1), 0.0)
    signs = (-1.0) ** degree
    slope = normed * degree * (degree + 1) / 2.0
    low, low_slope = normed * signs, -slope * signs
    own = stiffness + np.outer(normed, PENALTY * normed - 0.5 * slope) - 0.5 * np.outer(slope, normed)
    own = own + np.outer(low, PENALTY * low + 0.5 * low_slope) + 0.5 * np.outer(low_slope, low)
    one_axis = normed * normed * degree * (degree + 1) + 2.0 * (
        PENALTY * normed * normed - normed * slope
    )
    diagonal = (
        one_axis[:, None, None] + one_axis[None, :, None] + one_axis[None, None, :]
    ) / PENALTY
    return (
        own / PENALTY,
        0.5 * slope - PENALTY * normed,
        0.5 * normed,
        normed / PENALTY,
        slope / PENALTY,
        diagonal,
    )


OWN, JUMP, HALF, VALUE, SLOPE, DIAGONAL = tables()
THETA = 0.5 * (EIGEN_HIGH + EIGEN_LOW)
DELTA = 0.5 * (EIGEN_HIGH - EIGEN_LOW)
RHO_FIRST = DELTA / THETA
RHO_SECOND = 1.0 / (2.0 * THETA / DELTA - RHO_FIRST)
KEEP = 1.0 + RHO_SECOND * RHO_FIRST
STEP = 2.0 * RHO_SECOND / DELTA * THETA


def combine(weights, values):
    total = None
    for weight, value in zip(weights, values):
        term = value * float(weight)
        total = term if total is None else total + term
    return total


def traces(values):
    even, odd = values[0::2], values[1::2]
    jump_even, jump_odd = combine(JUMP[0::2], even), combine(JUMP[1::2], odd)
    half_even, half_odd = combine(HALF[0::2], even), combine(HALF[1::2], odd)
    down = (jump_even - jump_odd, half_even - half_odd)
    up = (jump_even + jump_odd, half_even + half_odd)
    return down, up


def own_row(row, values):
    start = row % 2
    return combine(OWN[row, start::2], values[start::2])


def face_terms(from_up, from_down):
    both = (from_up[0] + from_down[0], from_up[1] + from_down[1])
    apart = (from_up[0] - from_down[0], from_up[1] - from_down[1])

    def term(mode):
        pair = both if mode % 2 == 0 else apart
        if mode == 0:
            return pair[0] * float(VALUE[0])
        return pair[0] * float(VALUE[mode]) + pair[1] * float(SLOPE[mode])

    return term


def vertex_pair(zero, one):
    flat, tilt = np.sqrt(0.5) * zero, (np.sqrt(1.5) / 3.0) * one
    return flat - tilt, flat + tilt


def one_sided(data, mode, from_below):
    if mode == 0:
        return data[0] * float(VALUE[0])
    sign = -1.0 if from_below and mode % 2 else 1.0
    return data[0] * (sign * float(VALUE[mode])) + data[1] * (sign * float(SLOPE[mode]))


def corners(values):
    for axis in range(3):
        done = {}
        for key in values:
            if key[axis] == 0:
                other = tuple(1 if n == axis else key[n] for n in range(3))
                done[key], done[other] = vertex_pair(values[key], values[other])
        values = done
    return values


OCTET = [(a, b, e) for a in range(2) for b in range(2) for e in range(2)]
RELAYED = 4
SIGNS = (1, -1)
DIAGONALS = (
    [(dx, dy, 0) for dx in SIGNS for dy in SIGNS]
    + [(dx, 0, dz) for dx in SIGNS for dz in SIGNS]
    + [(2 * dx, 0, 0) for dx in SIGNS]
)
Y_PARTS = ((slice(0, 2), slice(0, MODES)), (slice(2, MODES), slice(0, 2)), (slice(2, MODES), slice(2, MODES)))
REACH = range(-2, 4)
CARRIES = (
    (3, 1), (2, 1), (-2, 1), (1, 1), (-1, 1), (2, -1), (1, -1), (-1, -1),
    (3, 0), (2, 0), (-2, 0), (1, 0), (-1, 0), (0, 1), (0, -1),
)


def kernel(
    sizes, cells_y, cells_z, rhs_hbm, orders_hbm, table_hbm, smooth, coarse_ref,
    rhs, first, acc, coef, ghost_up, ghost_down, orders_ref, table_ref,
    xs, xr, ys, yr, zs, zr, y_up, y_down,
    order_line, order_x, order_y, order_z, order_xy, order_xz, order_far, order_tile, pads,
    out_mid, out_high, out_low, in_mid, in_high, in_low, column,
    relay, local_sem, send_sem, recv_sem, x_send, x_recv, y_send, y_recv, relay_in, relay_out, met,
):
    nx, ny, nz = sizes
    tall = pads.shape[1]
    x, y, z = lax.axis_index("gx"), lax.axis_index("gy"), lax.axis_index("gz")
    barrier = pltpu.get_barrier_semaphore()

    def neighbour(axis, sign):
        here = (x, y, z)[axis]
        to = [x, y, z]
        to[axis] = here + sign
        back = [x, y, z]
        back[axis] = here - sign
        below, above = here > 0, here < sizes[axis] - 1
        return (tuple(to), below if sign < 0 else above, tuple(back), above if sign < 0 else below)

    halos = [neighbour(axis, sign) for axis in range(3) for sign in (-1, 1)]
    always = x >= 0

    def offset(dx, dy):
        ok_to = (x + dx > 0) & (x + dx < nx)
        ok_from = (x > 0) & (x - dx >= 0) & (x - dx < nx)
        if dy > 0:
            ok_to, ok_from = ok_to & (y + dy < ny), ok_from & (y >= dy)
        if dy < 0:
            ok_to, ok_from = ok_to & (y + dy >= 0), ok_from & (y - dy < ny)
        return ((x + dx, y + dy, z), ok_to, (x - dx, y - dy, z), ok_from)

    carries = [offset(dx, dy) + (dx, dy) for dx, dy in CARRIES]
    columns = []
    for r in range(1, nz):
        source = lax.rem(z - r + nz, nz)
        columns.append(((x, y, lax.rem(z + r, nz)), always, (x, y, source), always, source))

    def diagonal(offset):
        here = (x, y, z)
        to = tuple(h + d for h, d in zip(here, offset))
        back = tuple(h - d for h, d in zip(here, offset))
        ok_to, ok_from = always, always
        for axis, d in enumerate(offset):
            low, high = here[axis] >= abs(d), here[axis] + abs(d) < sizes[axis]
            if d > 0:
                ok_to, ok_from = ok_to & high, ok_from & low
            elif d < 0:
                ok_to, ok_from = ok_to & low, ok_from & high
        return (to, ok_to, back, ok_from)

    diagonals = [diagonal(offset) for offset in DIAGONALS]

    def diagonal_refs(offset):
        dx, dy, dz = offset
        if dy:
            return order_line.at[0 if dy < 0 else 1], order_xy.at[(1 + dx) // 2, (1 + dy) // 2]
        if dz:
            return orders_ref.at[0], order_xz.at[(1 + dx) // 2, (1 + dz) // 2]
        return orders_ref.at[0], order_far.at[(2 + dx) // 4]

    odd = lax.rem(x, 2) == 1
    even = jnp.logical_not(odd)
    relays = (
        ((x - 2, y, z), even & (x >= 2), (x + 2, y, z), even & (x + 2 < nx), (x + 1, y, z)),
        ((x + 2, y, z), odd & (x + 2 < nx), (x - 2, y, z), odd & (x >= 3), (x - 1, y, z)),
    )

    expected = jnp.int32(0)
    for entry in halos[:4] + columns + list(relays):
        to, ok_to, back, ok_from = entry[:4]

        @pl.when(ok_from)
        def _(back=back):
            pl.semaphore_signal(barrier, inc=1, device_id=back, device_id_type=MESH)

        expected = expected + jnp.where(ok_to, 1, 0).astype(jnp.int32)

    loads = [
        pltpu.make_async_copy(orders_hbm, orders_ref, local_sem.at[MODES]),
        pltpu.make_async_copy(table_hbm, table_ref, local_sem.at[MODES + 1]),
    ]
    for copy in loads:
        copy.start()

    def rhs_load(b):
        return pltpu.make_async_copy(rhs_hbm.at[:, b], rhs.at[:, b], local_sem.at[b])

    for b in range(MODES):
        rhs_load(b).start()

    def remote(src, dst, slot, to):
        if isinstance(slot, tuple):
            return pltpu.make_async_remote_copy(
                src_ref=src, dst_ref=dst, send_sem=y_send.at[slot], recv_sem=y_recv.at[slot],
                device_id=to, device_id_type=MESH,
            )
        return pltpu.make_async_remote_copy(
            src_ref=src, dst_ref=dst, send_sem=send_sem.at[slot], recv_sem=recv_sem.at[slot],
            device_id=to, device_id_type=MESH,
        )

    def start(entry, slot, src, dst):
        to, ok_to = entry[:2]

        @pl.when(ok_to)
        def _():
            remote(src, dst, slot, to).start()

    def receive(entry, slot, src, dst):
        to, _, _, ok_from = entry[:4]

        @pl.when(ok_from)
        def _():
            remote(src, dst, slot, to).wait_recv()

    def finish(entry, slot, src, dst):
        to, ok_to = entry[:2]

        @pl.when(ok_to)
        def _():
            remote(src, dst, slot, to).wait_send()

    stages = (
        ((xs, xr), (ys, yr), (zs, zr)),
        ((orders_ref, order_x), (order_line, order_y), (orders_ref, order_z)),
    )

    def over(action, stage, axis):
        src, dst = stages[stage][axis]
        for side in range(2):
            index = 2 * axis + side
            action(halos[index], 6 * stage + index, src.at[0 if src is orders_ref else side], dst.at[side])

    for stage, empty in ((0, 0.0), (1, -1)):
        for axis in range(3):
            for side in range(2):
                dst = stages[stage][axis][1]

                @pl.when(jnp.logical_not(halos[2 * axis + side][3]))
                def _(dst=dst, side=side, empty=empty):
                    dst[side] = jnp.full(dst.shape[1:], empty, dst.dtype)

    pads[...] = jnp.zeros(pads.shape, jnp.float32)
    order_tile[...] = jnp.full(order_tile.shape, -1, jnp.int32)
    for offset, entry in zip(DIAGONALS, diagonals):

        @pl.when(jnp.logical_not(entry[3]))
        def _(offset=offset):
            dst = diagonal_refs(offset)[1]
            dst[...] = jnp.full(dst.shape, -1, jnp.int32)

    targets = {0: (out_mid, in_mid), 1: (out_high, in_high), -1: (out_low, in_low)}

    def carry_refs(dx, dy):
        src, dst = targets[dy]
        at = dx + 1 if dy < 0 else dx + 2
        return src.at[at], dst.at[at]

    for _, _, _, ok_from, dx, dy in carries:

        @pl.when(jnp.logical_not(ok_from))
        def _(dx=dx, dy=dy):
            dst = carry_refs(dx, dy)[1]
            dst[...] = jnp.zeros(dst.shape, jnp.float32)

    for copy in loads:
        copy.wait()
    orders = orders_ref[0]
    order_line[0] = orders[0:1]
    order_line[1] = orders[cells_y - 1 : cells_y]
    tile = (MODES, cells_y, cells_z)
    last_mode = lax.broadcasted_iota(jnp.int32, tile, 0)
    lane = lax.broadcasted_iota(jnp.int32, (1, 1, cells_z), 2)

    def active(a, b):
        return jnp.maximum(jnp.maximum(a, b), last_mode) <= orders[None]

    def loop(body, low=0, high=MODES):
        def step(index, carry):
            body(index)
            return carry

        lax.fori_loop(low, high, step, 0)

    def x_copy(side, b, to):
        return pltpu.make_async_remote_copy(
            src_ref=xs.at[side, b], dst_ref=xr.at[side, b],
            send_sem=x_send.at[side, b], recv_sem=x_recv.at[side, b],
            device_id=to, device_id_type=MESH,
        )

    def to_relay(side, b, to):
        return pltpu.make_async_remote_copy(
            src_ref=xs.at[side, b], dst_ref=relay.at[side, b],
            send_sem=x_send.at[side, b], recv_sem=relay_in.at[side, b],
            device_id=to, device_id_type=MESH,
        )

    def from_relay(side, b, to):
        return pltpu.make_async_remote_copy(
            src_ref=relay.at[side, b], dst_ref=xr.at[side, b],
            send_sem=relay_out.at[side, b], recv_sem=x_recv.at[side, b],
            device_id=to, device_id_type=MESH,
        )

    def forward(number):
        for side in range(2):
            back, relaying, target = relays[side][2:]

            @pl.when(relaying)
            def _():
                to_relay(side, number, target).wait_recv()
                from_relay(side, number, target).start()

    def x_receive(number):
        for side in range(2):

            @pl.when(halos[side][3])
            def _():
                x_copy(side, number, halos[side][0]).wait_recv()

    def x_traces(b):
        rhs_load(b).wait()
        values = []
        for a in range(MODES):
            value = jnp.where(active(a, b), table_ref[a, b] * rhs[a, b], 0.0)
            first[a, b] = value
            values.append(value)
        sides = traces(values)
        for side in range(2):
            for kind in range(2):
                xs[side, b, kind] = sides[side][kind]

    def x_start(b):
        for side in range(2):
            to, ok_to = halos[side][:2]
            via, used = relays[side][:2]
            if b < RELAYED:

                @pl.when(used)
                def _():
                    to_relay(side, b, via).start()

                ok_to = ok_to & jnp.logical_not(used)

            @pl.when(ok_to)
            def _():
                x_copy(side, b, to).start()

    def diagonal_over(action):
        for number, (offset, entry) in enumerate(zip(DIAGONALS, diagonals)):
            action(entry, 14 + number, *diagonal_refs(offset))

    def y_over(action, part):
        modes = Y_PARTS[part]
        for side in range(2):
            at = (side, slice(None)) + modes
            action(halos[2 + side], (side, part), ys.at[at], yr.at[at])

    def meet(action):
        for side in range(2):
            to, ok_to, _, ok_from = halos[side]

            @pl.when(ok_to if action == "tell" else ok_from)
            def _():
                if action == "tell":
                    pl.semaphore_signal(met.at[side], inc=1, device_id=to, device_id_type=MESH)
                else:
                    pl.semaphore_wait(met.at[side], 1)

    loop(x_traces, 0, 2)
    pl.semaphore_wait(barrier, expected)
    meet("tell")
    over(start, 1, 0)
    x_start(0)
    x_start(1)
    loop(x_traces, 2)

    def y_faces(a, values, send, up_buf, down_buf):
        down, up = traces(values)
        for kind in range(2):
            up_buf[kind, a, :, 0:cells_y, :] = down[kind]
            down_buf[kind, a, :, 1 : cells_y + 1, :] = up[kind]
            send[0, kind, a] = down[kind][:, 0:1, :]
            send[1, kind, a] = up[kind][:, cells_y - 1 : cells_y, :]

    def y_neighbours(a, received, up_buf, down_buf, part=slice(0, MODES)):
        for kind in range(2):
            up_buf[kind, a, part, cells_y : cells_y + 1, :] = received[0, kind, a, part]
            down_buf[kind, a, part, 0:1, :] = received[1, kind, a, part]
        return (
            [up_buf[kind, a, part, 1 : cells_y + 1, :] for kind in range(2)],
            [down_buf[kind, a, part, 0:cells_y, :] for kind in range(2)],
        )

    def z_faces(a, values, send):
        sides = traces(values)
        for side in range(2):
            for kind in range(2):
                send[side, kind, a] = sides[side][kind]

    def z_neighbours(a, send, received, part=slice(0, MODES)):
        def moved(side, kind, edge, amount):
            picked = jnp.where(lane == edge, received[side, kind, a, part], send[side, kind, a, part])
            return pltpu.roll(picked, amount, 2)

        return (
            [moved(0, kind, 0, cells_z - 1) for kind in range(2)],
            [moved(1, kind, cells_z - 1, 1) for kind in range(2)],
        )

    def y_traces(a):
        y_faces(a, [first[a, b] for b in range(MODES)], ys, y_up, y_down)

    loop(y_traces, 0, 2)
    y_over(start, 0)
    loop(y_traces, 2)
    y_over(start, 1)
    over(start, 1, 1)
    meet("hear")
    diagonal_over(start)
    x_start(2)
    over(start, 1, 2)
    y_over(start, 2)
    loop(lambda a: z_faces(a, [first[a, :, e] for e in range(MODES)], zs))
    over(start, 0, 2)
    x_start(3)

    def predict(a, b, part, total):
        right = rhs[a, b, part]
        modes = jnp.maximum(last_mode[part], jnp.maximum(a, b))
        scale = jnp.where(modes <= orders[None], table_ref[a, b, part], 0.0)
        return scale * (KEEP * right + STEP * (right - total)), scale * (-STEP)

    def x_own(b):
        values = [first[a, b] for a in range(MODES)]
        for a in range(MODES):
            acc[a, b] = own_row(a, values)

    def y_own(a):
        values = [first[a, b] for b in range(MODES)]
        for b in range(MODES):
            acc[a, b] += own_row(b, values)

    def z_own(a):
        values = [first[a, :, e] for e in range(MODES)]
        for e in range(MODES):
            acc[a, :, e] += own_row(e, values)

    def z_flux(a):
        term = face_terms(*z_neighbours(a, zs, zr))
        for e in range(MODES):
            acc[a, :, e] += term(e)

    def y_flux(a):
        term = face_terms(*y_neighbours(a, yr, y_up, y_down))
        for b in range(MODES):
            acc[a, b], coef[a, b] = predict(a, b, slice(0, MODES), acc[a, b] + term(b))

    def y_flux_part(part):
        def step(a):
            term = face_terms(*y_neighbours(a, yr, y_up, y_down, part))
            for b in range(MODES):
                acc[a, b, part], coef[a, b, part] = predict(a, b, part, acc[a, b, part] + term(b))

        loop(step, 2)

    loop(x_own)
    x_start(4)
    x_start(5)
    loop(y_own)
    x_start(6)
    loop(z_own)
    over(receive, 0, 2)
    loop(z_flux)
    forward(0)

    slots = iter(range(pads.shape[0]))

    def padded(value, at):
        slot = next(slots)
        pads[slot, at : at + cells_y, :] = value
        return pads[slot]

    near, border, layers = {}, {}, {}

    def gather_into(where_to, key, value):
        where_to[key] = where_to[key] + value if key in where_to else value

    def spread(values, shift, forced, tile_orders, low_orders, high_orders, edge_orders):
        centre, edge, x_low, x_high, y_low, y_high = {}, {}, {}, {}, {}, {}
        for b in range(2):
            line = [values[a, b, 0:2] for a in range(MODES)]
            down, up = traces(line)
            for a in range(2):
                own = own_row(a, line)
                below, above = one_sided(down, a, False), one_sided(up, a, True)
                for e in range(2):
                    centre[a, b, e] = forced[a, b, e] - own[e] if forced is not None else -own[e]
                    x_low[a, b, e] = jnp.where(low_orders >= max(a, b, e), -below[e], 0.0)
                    x_high[a, b, e] = jnp.where(high_orders >= max(a, b, e), -above[e], 0.0)
        for a in range(2):
            line = [values[a, b, 0:2] for b in range(MODES)]
            down, up = traces(line)
            for b in range(2):
                own = own_row(b, line)
                below, above = one_sided(down, b, False), one_sided(up, b, True)
                for e in range(2):
                    centre[a, b, e] = centre[a, b, e] - own[e]
                    y_low[a, b, e], y_high[a, b, e] = below[e], above[e]
            line = [values[a, 0:2, e] for e in range(MODES)]
            down, up = traces(line)
            for e in range(2):
                below = pltpu.roll(one_sided(down, e, False), cells_z - 1, 2)
                above = pltpu.roll(one_sided(up, e, True), 1, 2)
                inner = jnp.where(lane == cells_z - 1, 0.0, below) + jnp.where(lane == 0, 0.0, above)
                outer = jnp.where(lane == cells_z - 1, below, jnp.where(lane == 0, above, 0.0))
                own = own_row(e, line) + inner
                for b in range(2):
                    centre[a, b, e] = centre[a, b, e] - own[b]
                    edge[a, b, e] = jnp.where(edge_orders >= max(a, b, e), -outer[b], 0.0)
        resid = {}
        for key in OCTET:
            total = padded(centre[key], 1) - padded(y_low[key], 0) - padded(y_high[key], 2)
            resid[key] = jnp.where(tile_orders >= max(key), total, 0.0)
        resid, edge, x_low, x_high = corners(resid), corners(edge), corners(x_low), corners(x_high)
        for i, j, k in OCTET:
            moved = pltpu.roll(resid[i, j, k], 1, 0) if j else resid[i, j, k]
            gather_into(layers, (shift + i, k), moved)
            gather_into(border, (shift + i, j, k), edge[i, j, k])
            gather_into(near, (shift - 1 + i, j, k), x_low[i, j, k])
            gather_into(near, (shift + 1 + i, j, k), x_high[i, j, k])

    def ghost(values, side, other_orders):
        def put(a, b, high):
            part = slice(0, high)
            data = [xs[side, b, kind, part] for kind in range(2)]
            modes = jnp.maximum(last_mode[part], max(a, b))
            scale = jnp.where(modes <= other_orders[None], table_ref[a, b, part], 0.0) * (-STEP)
            values[a, b, part] = scale * one_sided(data, a, side == 1)

        for b in range(2):
            for a in range(MODES):
                put(a, b, MODES if a < 2 else 2)
        for b in range(2, MODES):
            for a in range(2):
                put(a, b, 2)

    for axis in range(3):
        over(receive, 1, axis)
    rows_of = (orders, order_x[0], order_x[1])
    lines_of = (order_y, order_xy.at[0], order_xy.at[1])
    sides_of = (order_z, order_xz.at[0], order_xz.at[1])

    def surroundings(at):
        order_tile[at, 1 : cells_y + 1] = rows_of[at]
        order_tile[at, 0:1] = lines_of[at][1]
        order_tile[at, cells_y + 1 : cells_y + 2] = lines_of[at][0]
        edge_orders = jnp.where(lane[0] == cells_z - 1, sides_of[at][1], sides_of[at][0])
        return order_tile[at], edge_orders

    ghost(ghost_up, 1, order_x[0])
    ghost(ghost_down, 0, order_x[1])
    y_over(receive, 0)
    loop(y_flux, 0, 2)
    y_over(receive, 1)
    y_flux_part(slice(0, 2))
    forward(1)
    tile_orders, edge_orders = surroundings(0)
    spread(acc, 0, rhs, tile_orders, order_x[1], order_x[0], edge_orders)
    diagonal_over(receive)
    forward(2)
    tile_orders, edge_orders = surroundings(1)
    spread(ghost_up, 1, None, tile_orders, orders, order_far[0], edge_orders)
    tile_orders, edge_orders = surroundings(2)
    spread(ghost_down, -1, None, tile_orders, order_far[1], orders, edge_orders)

    row_lane = lane[0]
    sums = {}
    for dx in REACH:
        pair = []
        for k in range(2):
            parts = [layers[dx, k]] if (dx, k) in layers else []
            parts += [padded(near[dx, j, k], 1 + j) for j in range(2)]
            pair.append(functools.reduce(lambda p, q: p + q, parts))
        moved = pltpu.roll(pair[1], 1, 1)
        if (dx, 0, 0) in border:
            outer = [padded(border[dx, 0, k], 1) + padded(border[dx, 1, k], 2) for k in range(2)]
            outer_moved = pltpu.roll(outer[1], 1, 1)
            inside = pair[0] + jnp.where(row_lane == 0, outer_moved, moved)
            beyond = jnp.where(row_lane == 0, moved, outer_moved) + outer[0]
        else:
            inside = pair[0] + jnp.where(row_lane == 0, 0.0, moved)
            beyond = jnp.where(row_lane == 0, moved, 0.0)
        for part, value in enumerate((inside, beyond)):
            if dx == 0:
                sums[part] = value[1 : cells_y + 1]
            else:
                out_mid[dx + 2, part] = value[1 : cells_y + 1]
            out_high[dx + 2, part] = value[cells_y + 1 : cells_y + 3]
            if -1 <= dx <= 2:
                out_low[dx + 1, part] = value[0:1]

    for number, entry in enumerate(carries):
        start(entry, 24 + number, *carry_refs(*entry[4:]))
    forward(3)
    y_over(receive, 2)
    y_flux_part(slice(2, MODES))

    def x_flux(b):
        x_receive(b)
        term = face_terms(
            [xr[0, b, kind] for kind in range(2)], [xr[1, b, kind] for kind in range(2)]
        )
        for a in range(MODES):
            smooth[a, b] = acc[a, b] + coef[a, b] * term(a)

    loop(x_flux, RELAYED)

    for stage, axis in ((0, 2), (1, 0), (1, 1), (1, 2)):
        over(finish, stage, axis)
    for part in range(3):
        y_over(finish, part)
    diagonal_over(finish)
    for b in range(MODES):
        for side in range(2):

            @pl.when(halos[side][1])
            def _():
                x_copy(side, b, halos[side][0]).wait_send()

    for b in range(RELAYED):
        for side in range(2):

            @pl.when(relays[side][3])
            def _():
                from_relay(side, b, relays[side][4]).wait_send()

    for number, entry in enumerate(carries):
        receive(entry, 24 + number, *carry_refs(*entry[4:]))

    for part in range(2):
        value = sums[part]
        for dx in REACH:
            if dx:
                value = value + in_mid[dx + 2, part]
        high = functools.reduce(lambda p, q: p + q, [in_high[at, part] for at in range(6)])
        low = functools.reduce(lambda p, q: p + q, [in_low[at, part] for at in range(4)])
        column[pl.ds(z, 1), part] = value[None]
        column[pl.ds(z, 1), part, 0:2] += high[None]
        column[pl.ds(z, 1), part, cells_y - 1 : cells_y] += low[None]

    def gather(number, arriving):
        entry = columns[number]
        at = entry[4] if arriving else z
        return remote(column.at[at], column.at[at], 24 + len(carries) + number, entry[0])

    for number in range(len(columns)):
        gather(number, False).start()
    loop(x_flux, 0, RELAYED)
    for number, entry in enumerate(carries):
        finish(entry, 24 + number, *carry_refs(*entry[4:]))
    for number in range(len(columns)):
        gather(number, True).wait_recv()
    for number in range(len(columns)):
        gather(number, False).wait_send()

    row = lax.broadcasted_iota(jnp.int32, (cells_y, cells_z), 0)
    spot = lax.broadcasted_iota(jnp.int32, (cells_y, cells_z), 1)
    for zz in range(nz):
        total = column[zz, 0]
        if zz > 0:
            total = total + jnp.where(spot < 2, column[zz - 1, 1], 0.0)
        if zz < nz - 1:
            total = total + jnp.where(spot == cells_z - 1, column[zz + 1, 1], 0.0)
        inside = (x > 0) & ((row > 0) | (y > 0))
        if zz == 0:
            inside = inside & (spot > 0)
        coarse_ref[0, :, zz * cells_z : (zz + 1) * cells_z] = jnp.where(inside, total, 0.0)


def drain(smooth, coarse, smooth_hbm, coarse_hbm, sem):
    copies = [
        pltpu.make_async_copy(smooth.at[a], smooth_hbm.at[a], sem.at[a]) for a in range(MODES)
    ]
    copies.append(pltpu.make_async_copy(coarse, coarse_hbm, sem.at[MODES]))
    for copy in copies:
        copy.start()
    for copy in copies:
        copy.wait()


def per_device(sizes, rhs, orders):
    _, cells_y, cells_z = orders.shape
    nz = sizes[2]
    table = jnp.asarray(
        np.broadcast_to(
            (1.0 / (DIAGONAL * THETA))[:, :, :, None, None], DIAGONAL.shape + (1, cells_z)
        ),
        jnp.float32,
    )
    field = rhs.reshape(rhs.shape[:3] + rhs.shape[4:])
    cells = (cells_y, cells_z)
    rows = 8 * ((cells_y + 8) // 8)
    tall = 8 * ((cells_y + 10) // 8)
    line = (2, 2, MODES, MODES)

    def buf(*shape):
        return pltpu.VMEM(shape, jnp.float32)

    def whole(*shape):
        return pltpu.VMEM(shape, jnp.int32)

    slots = 24 + len(CARRIES) + nz - 1
    coarse_shape = (1, cells_y, nz * cells_z)
    vmem = pl.BlockSpec(memory_space=pltpu.VMEM)
    hbm = pl.BlockSpec(memory_space=pltpu.HBM)
    smoothed, coarse = pl.pallas_call(
        functools.partial(kernel, sizes, cells_y, cells_z),
        out_shape=(pltpu.VMEM(field.shape, jnp.float32), pltpu.VMEM(coarse_shape, jnp.float32)),
        in_specs=[hbm, hbm, hbm],
        out_specs=(vmem, vmem),
        scratch_shapes=[buf(*field.shape)] * 6
        + [
            whole(*orders.shape), buf(*table.shape),
            buf(2, MODES, 2, MODES, *cells), buf(2, MODES, 2, MODES, *cells),
            buf(*line, 1, cells_z), buf(*line, 1, cells_z),
            buf(*line, *cells), buf(*line, *cells),
            buf(2, MODES, MODES, rows, cells_z), buf(2, MODES, MODES, rows, cells_z),
            whole(2, 1, cells_z), whole(2, *cells), whole(2, 1, cells_z), whole(2, *cells),
            whole(2, 2, 1, cells_z), whole(2, 2, *cells), whole(2, *cells), whole(3, tall, cells_z),
            buf(112, tall, cells_z),
            buf(6, 2, *cells), buf(6, 2, 2, cells_z), buf(4, 2, 1, cells_z),
            buf(6, 2, *cells), buf(6, 2, 2, cells_z), buf(4, 2, 1, cells_z),
            buf(nz, 2, *cells),
            buf(2, RELAYED, 2, MODES, *cells),
            pltpu.SemaphoreType.DMA((MODES + 2,)),
            pltpu.SemaphoreType.DMA((slots,)),
            pltpu.SemaphoreType.DMA((slots,)),
            pltpu.SemaphoreType.DMA((2, MODES)),
            pltpu.SemaphoreType.DMA((2, MODES)),
            pltpu.SemaphoreType.DMA((2, 3)),
            pltpu.SemaphoreType.DMA((2, 3)),
            pltpu.SemaphoreType.DMA((2, RELAYED)),
            pltpu.SemaphoreType.DMA((2, RELAYED)),
            pltpu.SemaphoreType.REGULAR((2,)),
        ],
        compiler_params=pltpu.CompilerParams(collective_id=0, has_side_effects=True),
        name="smoother",
    )(field, orders, table)
    smoothed, coarse = pl.pallas_call(
        drain,
        out_shape=(
            jax.ShapeDtypeStruct(field.shape, jnp.float32),
            jax.ShapeDtypeStruct(coarse_shape, jnp.float32),
        ),
        in_specs=[vmem, vmem],
        out_specs=(hbm, hbm),
        scratch_shapes=[pltpu.SemaphoreType.DMA((MODES + 1,))],
        name="drain",
    )(
        pltpu.with_memory_space_constraint(smoothed, pltpu.VMEM),
        pltpu.with_memory_space_constraint(coarse, pltpu.VMEM),
    )
    return smoothed.reshape(rhs.shape), coarse


def solution(mesh):
    sizes = tuple(mesh.shape[axis] for axis in ("gx", "gy", "gz"))
    return jax.shard_map(
        functools.partial(per_device, sizes),
        mesh=mesh,
        in_specs=(P(None, None, None, "gx", "gy", "gz"), P("gx", "gy", "gz")),
        out_specs=(P(None, None, None, "gx", "gy", "gz"), P("gx", "gy", None)),
        check_vma=False,
    )
```

```python
import functools

import jax
import jax.numpy as jnp
import numpy as np
from jax import lax
from jax.experimental import pallas as pl
from jax.experimental.pallas import tpu as pltpu
from jax.sharding import PartitionSpec as P

PENALTY = 49.0
EIGEN_HIGH = 2.4
EIGEN_LOW = 0.24
MODES = 7
MESH = pl.DeviceIdType.MESH


def tables():
    degree = np.arange(MODES)
    normed = np.sqrt((2.0 * degree + 1.0) / 2.0)
    smaller = np.minimum(degree[:, None], degree[None, :])
    parity = (degree[:, None] + degree[None, :]) % 2 == 0
    stiffness = np.where(parity, normed[:, None] * normed[None, :] * smaller * (smaller + 1), 0.0)
    signs = (-1.0) ** degree
    slope = normed * degree * (degree + 1) / 2.0
    low, low_slope = normed * signs, -slope * signs
    own = stiffness + np.outer(normed, PENALTY * normed - 0.5 * slope) - 0.5 * np.outer(slope, normed)
    own = own + np.outer(low, PENALTY * low + 0.5 * low_slope) + 0.5 * np.outer(low_slope, low)
    one_axis = normed * normed * degree * (degree + 1) + 2.0 * (
        PENALTY * normed * normed - normed * slope
    )
    diagonal = (
        one_axis[:, None, None] + one_axis[None, :, None] + one_axis[None, None, :]
    ) / PENALTY
    return (
        own / PENALTY,
        0.5 * slope - PENALTY * normed,
        0.5 * normed,
        normed / PENALTY,
        slope / PENALTY,
        diagonal,
    )


OWN, JUMP, HALF, VALUE, SLOPE, DIAGONAL = tables()
THETA = 0.5 * (EIGEN_HIGH + EIGEN_LOW)
DELTA = 0.5 * (EIGEN_HIGH - EIGEN_LOW)
RHO_FIRST = DELTA / THETA
RHO_SECOND = 1.0 / (2.0 * THETA / DELTA - RHO_FIRST)
KEEP = 1.0 + RHO_SECOND * RHO_FIRST
STEP = 2.0 * RHO_SECOND / DELTA * THETA


def combine(weights, values):
    total = None
    for weight, value in zip(weights, values):
        term = value * float(weight)
        total = term if total is None else total + term
    return total


def traces(values):
    even, odd = values[0::2], values[1::2]
    jump_even, jump_odd = combine(JUMP[0::2], even), combine(JUMP[1::2], odd)
    half_even, half_odd = combine(HALF[0::2], even), combine(HALF[1::2], odd)
    down = (jump_even - jump_odd, half_even - half_odd)
    up = (jump_even + jump_odd, half_even + half_odd)
    return down, up


def own_row(row, values):
    start = row % 2
    return combine(OWN[row, start::2], values[start::2])


def face_terms(from_up, from_down):
    both = (from_up[0] + from_down[0], from_up[1] + from_down[1])
    apart = (from_up[0] - from_down[0], from_up[1] - from_down[1])

    def term(mode):
        pair = both if mode % 2 == 0 else apart
        if mode == 0:
            return pair[0] * float(VALUE[0])
        return pair[0] * float(VALUE[mode]) + pair[1] * float(SLOPE[mode])

    return term


def vertex_pair(zero, one):
    flat, tilt = np.sqrt(0.5) * zero, (np.sqrt(1.5) / 3.0) * one
    return flat - tilt, flat + tilt


def one_sided(data, mode, from_below):
    if mode == 0:
        return data[0] * float(VALUE[0])
    sign = -1.0 if from_below and mode % 2 else 1.0
    return data[0] * (sign * float(VALUE[mode])) + data[1] * (sign * float(SLOPE[mode]))


def corners(values):
    for axis in range(3):
        done = {}
        for key in values:
            if key[axis] == 0:
                other = tuple(1 if n == axis else key[n] for n in range(3))
                done[key], done[other] = vertex_pair(values[key], values[other])
        values = done
    return values


OCTET = [(a, b, e) for a in range(2) for b in range(2) for e in range(2)]
RELAYED = 4
SIGNS = (1, -1)
DIAGONALS = (
    [(dx, dy, 0) for dx in SIGNS for dy in SIGNS]
    + [(dx, 0, dz) for dx in SIGNS for dz in SIGNS]
    + [(2 * dx, 0, 0) for dx in SIGNS]
)
Y_PARTS = ((slice(0, 2), slice(0, MODES)), (slice(2, MODES), slice(0, 2)), (slice(2, MODES), slice(2, MODES)))
REACH = range(-2, 4)
CARRIES = (
    (1, 1), (-1, 1), (1, -1), (-1, -1), (3, 1), (2, 1), (-2, 1), (2, -1),
    (3, 0), (2, 0), (-2, 0), (1, 0), (-1, 0), (0, 1), (0, -1),
)


def kernel(
    sizes, cells_y, cells_z, rhs_hbm, orders_hbm, table_hbm, smooth, coarse_ref,
    rhs, first, acc, coef, ghost_up, ghost_down, orders_ref, table_ref,
    xs, xr, ys, yr, zs, zr, y_up, y_down,
    order_line, order_x, order_y, order_z, order_xy, order_xz, order_far, order_tile, pads,
    out_mid, out_high, out_low, in_mid, in_high, in_low, far_mid, far_high, far_low, column,
    relay, local_sem, send_sem, recv_sem, x_send, x_recv, y_send, y_recv, relay_in, relay_out, met,
):
    nx, ny, nz = sizes
    tall = pads.shape[1]
    x, y, z = lax.axis_index("gx"), lax.axis_index("gy"), lax.axis_index("gz")
    barrier = pltpu.get_barrier_semaphore()

    def neighbour(axis, sign):
        here = (x, y, z)[axis]
        to = [x, y, z]
        to[axis] = here + sign
        back = [x, y, z]
        back[axis] = here - sign
        below, above = here > 0, here < sizes[axis] - 1
        return (tuple(to), below if sign < 0 else above, tuple(back), above if sign < 0 else below)

    halos = [neighbour(axis, sign) for axis in range(3) for sign in (-1, 1)]
    always = x >= 0

    def offset(dx, dy):
        ok_to = (x + dx > 0) & (x + dx < nx)
        ok_from = (x > 0) & (x - dx >= 0) & (x - dx < nx)
        if dy > 0:
            ok_to, ok_from = ok_to & (y + dy < ny), ok_from & (y >= dy)
        if dy < 0:
            ok_to, ok_from = ok_to & (y + dy >= 0), ok_from & (y - dy < ny)
        return ((x + dx, y + dy, z), ok_to, (x - dx, y - dy, z), ok_from)

    carries = [offset(dx, dy) + (dx, dy) for dx, dy in CARRIES]
    collects = z == nz - 1
    direct = []
    for dx, dy in CARRIES + ((0, 0),):
        to, ok_to, back, ok_from = offset(dx, dy)
        to = to[:2] + (nz - 1,)
        direct.append((to, ok_to & jnp.logical_not(collects), back, ok_from, dx, dy))
    columns = []
    for r in range(1, nz):
        source = lax.rem(z - r + nz, nz)
        columns.append(((x, y, lax.rem(z + r, nz)), always, (x, y, source), always, source))

    def diagonal(offset):
        here = (x, y, z)
        to = tuple(h + d for h, d in zip(here, offset))
        back = tuple(h - d for h, d in zip(here, offset))
        ok_to, ok_from = always, always
        for axis, d in enumerate(offset):
            low, high = here[axis] >= abs(d), here[axis] + abs(d) < sizes[axis]
            if d > 0:
                ok_to, ok_from = ok_to & high, ok_from & low
            elif d < 0:
                ok_to, ok_from = ok_to & low, ok_from & high
        return (to, ok_to, back, ok_from)

    diagonals = [diagonal(offset) for offset in DIAGONALS]

    def diagonal_refs(offset):
        dx, dy, dz = offset
        if dy:
            return order_line.at[0 if dy < 0 else 1], order_xy.at[(1 + dx) // 2, (1 + dy) // 2]
        if dz:
            return orders_ref.at[0], order_xz.at[(1 + dx) // 2, (1 + dz) // 2]
        return orders_ref.at[0], order_far.at[(2 + dx) // 4]

    odd = lax.rem(x, 2) == 1
    even = jnp.logical_not(odd)
    relays = (
        ((x - 2, y, z), even & (x >= 2), (x + 2, y, z), even & (x + 2 < nx), (x + 1, y, z)),
        ((x + 2, y, z), odd & (x + 2 < nx), (x - 2, y, z), odd & (x >= 3), (x - 1, y, z)),
    )

    expected = jnp.int32(0)
    for entry in halos[:4] + columns + list(relays):
        to, ok_to, back, ok_from = entry[:4]

        @pl.when(ok_from)
        def _(back=back):
            pl.semaphore_signal(barrier, inc=1, device_id=back, device_id_type=MESH)

        expected = expected + jnp.where(ok_to, 1, 0).astype(jnp.int32)

    loads = [
        pltpu.make_async_copy(orders_hbm, orders_ref, local_sem.at[MODES]),
        pltpu.make_async_copy(table_hbm, table_ref, local_sem.at[MODES + 1]),
    ]
    for copy in loads:
        copy.start()

    def rhs_load(b):
        return pltpu.make_async_copy(rhs_hbm.at[:, b], rhs.at[:, b], local_sem.at[b])

    for b in range(MODES):
        rhs_load(b).start()

    def remote(src, dst, slot, to):
        if isinstance(slot, tuple):
            return pltpu.make_async_remote_copy(
                src_ref=src, dst_ref=dst, send_sem=y_send.at[slot], recv_sem=y_recv.at[slot],
                device_id=to, device_id_type=MESH,
            )
        return pltpu.make_async_remote_copy(
            src_ref=src, dst_ref=dst, send_sem=send_sem.at[slot], recv_sem=recv_sem.at[slot],
            device_id=to, device_id_type=MESH,
        )

    def start(entry, slot, src, dst):
        to, ok_to = entry[:2]

        @pl.when(ok_to)
        def _():
            remote(src, dst, slot, to).start()

    def receive(entry, slot, src, dst):
        to, _, _, ok_from = entry[:4]

        @pl.when(ok_from)
        def _():
            remote(src, dst, slot, to).wait_recv()

    def finish(entry, slot, src, dst):
        to, ok_to = entry[:2]

        @pl.when(ok_to)
        def _():
            remote(src, dst, slot, to).wait_send()

    stages = (
        ((xs, xr), (ys, yr), (zs, zr)),
        ((orders_ref, order_x), (order_line, order_y), (orders_ref, order_z)),
    )

    def over(action, stage, axis):
        src, dst = stages[stage][axis]
        for side in range(2):
            index = 2 * axis + side
            action(halos[index], 6 * stage + index, src.at[0 if src is orders_ref else side], dst.at[side])

    for stage, empty in ((0, 0.0), (1, -1)):
        for axis in range(3):
            for side in range(2):
                dst = stages[stage][axis][1]

                @pl.when(jnp.logical_not(halos[2 * axis + side][3]))
                def _(dst=dst, side=side, empty=empty):
                    dst[side] = jnp.full(dst.shape[1:], empty, dst.dtype)

    pads[...] = jnp.zeros(pads.shape, jnp.float32)
    order_tile[...] = jnp.full(order_tile.shape, -1, jnp.int32)
    for offset, entry in zip(DIAGONALS, diagonals):

        @pl.when(jnp.logical_not(entry[3]))
        def _(offset=offset):
            dst = diagonal_refs(offset)[1]
            dst[...] = jnp.full(dst.shape, -1, jnp.int32)

    targets = {0: (out_mid, in_mid), 1: (out_high, in_high), -1: (out_low, in_low)}

    def carry_refs(dx, dy):
        src, dst = targets[dy]
        at = dx + 1 if dy < 0 else dx + 2
        return src.at[at], dst.at[at]

    far_of = {0: far_mid, 1: far_high, -1: far_low}

    def direct_refs(dx, dy, source):
        at = dx + 1 if dy < 0 else dx + 2
        return targets[dy][0].at[at], far_of[dy].at[at, source]

    for _, _, _, ok_from, dx, dy in direct:

        @pl.when(jnp.logical_not(ok_from))
        def _(dx=dx, dy=dy):
            dst = far_of[dy].at[dx + 1 if dy < 0 else dx + 2]
            dst[...] = jnp.zeros(dst.shape, jnp.float32)

    for _, _, _, ok_from, dx, dy in carries:

        @pl.when(jnp.logical_not(ok_from))
        def _(dx=dx, dy=dy):
            dst = carry_refs(dx, dy)[1]
            dst[...] = jnp.zeros(dst.shape, jnp.float32)

    for copy in loads:
        copy.wait()
    orders = orders_ref[0]
    order_line[0] = orders[0:1]
    order_line[1] = orders[cells_y - 1 : cells_y]
    tile = (MODES, cells_y, cells_z)
    last_mode = lax.broadcasted_iota(jnp.int32, tile, 0)
    lane = lax.broadcasted_iota(jnp.int32, (1, 1, cells_z), 2)

    def active(a, b):
        return jnp.maximum(jnp.maximum(a, b), last_mode) <= orders[None]

    def loop(body, low=0, high=MODES):
        def step(index, carry):
            body(index)
            return carry

        lax.fori_loop(low, high, step, 0)

    def x_copy(side, b, to):
        return pltpu.make_async_remote_copy(
            src_ref=xs.at[side, b], dst_ref=xr.at[side, b],
            send_sem=x_send.at[side, b], recv_sem=x_recv.at[side, b],
            device_id=to, device_id_type=MESH,
        )

    def to_relay(side, b, to):
        return pltpu.make_async_remote_copy(
            src_ref=xs.at[side, b], dst_ref=relay.at[side, b],
            send_sem=x_send.at[side, b], recv_sem=relay_in.at[side, b],
            device_id=to, device_id_type=MESH,
        )

    def from_relay(side, b, to):
        return pltpu.make_async_remote_copy(
            src_ref=relay.at[side, b], dst_ref=xr.at[side, b],
            send_sem=relay_out.at[side, b], recv_sem=x_recv.at[side, b],
            device_id=to, device_id_type=MESH,
        )

    def forward(number):
        for side in range(2):
            back, relaying, target = relays[side][2:]

            @pl.when(relaying)
            def _():
                to_relay(side, number, target).wait_recv()
                from_relay(side, number, target).start()

    def x_receive(number):
        for side in range(2):

            @pl.when(halos[side][3])
            def _():
                x_copy(side, number, halos[side][0]).wait_recv()

    def x_traces(b):
        rhs_load(b).wait()
        values = []
        for a in range(MODES):
            value = jnp.where(active(a, b), table_ref[a, b] * rhs[a, b], 0.0)
            first[a, b] = value
            values.append(value)
        sides = traces(values)
        for side in range(2):
            for kind in range(2):
                xs[side, b, kind] = sides[side][kind]

    def x_start(b):
        for side in range(2):
            to, ok_to = halos[side][:2]
            via, used = relays[side][:2]
            if b < RELAYED:

                @pl.when(used)
                def _():
                    to_relay(side, b, via).start()

                ok_to = ok_to & jnp.logical_not(used)

            @pl.when(ok_to)
            def _():
                x_copy(side, b, to).start()

    def diagonal_over(action):
        for number, (offset, entry) in enumerate(zip(DIAGONALS, diagonals)):
            action(entry, 14 + number, *diagonal_refs(offset))

    def y_over(action, part):
        modes = Y_PARTS[part]
        for side in range(2):
            at = (side, slice(None)) + modes
            action(halos[2 + side], (side, part), ys.at[at], yr.at[at])

    def meet(action):
        for side in range(2):
            to, ok_to, _, ok_from = halos[side]

            @pl.when(ok_to if action == "tell" else ok_from)
            def _():
                if action == "tell":
                    pl.semaphore_signal(met.at[side], inc=1, device_id=to, device_id_type=MESH)
                else:
                    pl.semaphore_wait(met.at[side], 1)

    loop(x_traces, 0, 2)
    pl.semaphore_wait(barrier, expected)
    meet("tell")
    over(start, 1, 0)
    x_start(0)
    x_start(1)
    loop(x_traces, 2)

    def y_faces(a, values, send, up_buf, down_buf):
        down, up = traces(values)
        for kind in range(2):
            up_buf[kind, a, :, 0:cells_y, :] = down[kind]
            down_buf[kind, a, :, 1 : cells_y + 1, :] = up[kind]
            send[0, kind, a] = down[kind][:, 0:1, :]
            send[1, kind, a] = up[kind][:, cells_y - 1 : cells_y, :]

    def y_neighbours(a, received, up_buf, down_buf, part=slice(0, MODES)):
        for kind in range(2):
            up_buf[kind, a, part, cells_y : cells_y + 1, :] = received[0, kind, a, part]
            down_buf[kind, a, part, 0:1, :] = received[1, kind, a, part]
        return (
            [up_buf[kind, a, part, 1 : cells_y + 1, :] for kind in range(2)],
            [down_buf[kind, a, part, 0:cells_y, :] for kind in range(2)],
        )

    def z_faces(a, values, send):
        sides = traces(values)
        for side in range(2):
            for kind in range(2):
                send[side, kind, a] = sides[side][kind]

    def z_neighbours(a, send, received, part=slice(0, MODES)):
        def moved(side, kind, edge, amount):
            picked = jnp.where(lane == edge, received[side, kind, a, part], send[side, kind, a, part])
            return pltpu.roll(picked, amount, 2)

        return (
            [moved(0, kind, 0, cells_z - 1) for kind in range(2)],
            [moved(1, kind, cells_z - 1, 1) for kind in range(2)],
        )

    def y_traces(a):
        y_faces(a, [first[a, b] for b in range(MODES)], ys, y_up, y_down)

    loop(y_traces, 0, 2)
    y_over(start, 0)
    loop(y_traces, 2)
    y_over(start, 1)
    over(start, 1, 1)
    meet("hear")
    diagonal_over(start)
    x_start(2)
    over(start, 1, 2)
    y_over(start, 2)
    loop(lambda a: z_faces(a, [first[a, :, e] for e in range(MODES)], zs))
    over(start, 0, 2)
    x_start(3)

    def predict(a, b, part, total):
        right = rhs[a, b, part]
        modes = jnp.maximum(last_mode[part], jnp.maximum(a, b))
        scale = jnp.where(modes <= orders[None], table_ref[a, b, part], 0.0)
        return scale * (KEEP * right + STEP * (right - total)), scale * (-STEP)

    def x_own(b):
        values = [first[a, b] for a in range(MODES)]
        for a in range(MODES):
            acc[a, b] = own_row(a, values)

    def y_own(a):
        values = [first[a, b] for b in range(MODES)]
        for b in range(MODES):
            acc[a, b] += own_row(b, values)

    def z_own(a):
        values = [first[a, :, e] for e in range(MODES)]
        for e in range(MODES):
            acc[a, :, e] += own_row(e, values)

    def z_flux(a):
        term = face_terms(*z_neighbours(a, zs, zr))
        for e in range(MODES):
            acc[a, :, e] += term(e)

    def y_flux(a):
        term = face_terms(*y_neighbours(a, yr, y_up, y_down))
        for b in range(MODES):
            acc[a, b], coef[a, b] = predict(a, b, slice(0, MODES), acc[a, b] + term(b))

    def y_flux_part(part):
        def step(a):
            term = face_terms(*y_neighbours(a, yr, y_up, y_down, part))
            for b in range(MODES):
                acc[a, b, part], coef[a, b, part] = predict(a, b, part, acc[a, b, part] + term(b))

        loop(step, 2)

    loop(x_own)
    x_start(4)
    x_start(5)
    loop(y_own)
    x_start(6)
    loop(z_own)
    over(receive, 0, 2)
    loop(z_flux)
    forward(0)

    slots = iter(range(pads.shape[0]))

    def padded(value, at):
        slot = next(slots)
        pads[slot, at : at + cells_y, :] = value
        return pads[slot]

    near, border, layers = {}, {}, {}

    def gather_into(where_to, key, value):
        where_to[key] = where_to[key] + value if key in where_to else value

    def spread(values, shift, forced, tile_orders, low_orders, high_orders, edge_orders):
        centre, edge, x_low, x_high, y_low, y_high = {}, {}, {}, {}, {}, {}
        for b in range(2):
            line = [values[a, b, 0:2] for a in range(MODES)]
            down, up = traces(line)
            for a in range(2):
                own = own_row(a, line)
                below, above = one_sided(down, a, False), one_sided(up, a, True)
                for e in range(2):
                    centre[a, b, e] = forced[a, b, e] - own[e] if forced is not None else -own[e]
                    x_low[a, b, e] = jnp.where(low_orders >= max(a, b, e), -below[e], 0.0)
                    x_high[a, b, e] = jnp.where(high_orders >= max(a, b, e), -above[e], 0.0)
        for a in range(2):
            line = [values[a, b, 0:2] for b in range(MODES)]
            down, up = traces(line)
            for b in range(2):
                own = own_row(b, line)
                below, above = one_sided(down, b, False), one_sided(up, b, True)
                for e in range(2):
                    centre[a, b, e] = centre[a, b, e] - own[e]
                    y_low[a, b, e], y_high[a, b, e] = below[e], above[e]
            line = [values[a, 0:2, e] for e in range(MODES)]
            down, up = traces(line)
            for e in range(2):
                below = pltpu.roll(one_sided(down, e, False), cells_z - 1, 2)
                above = pltpu.roll(one_sided(up, e, True), 1, 2)
                inner = jnp.where(lane == cells_z - 1, 0.0, below) + jnp.where(lane == 0, 0.0, above)
                outer = jnp.where(lane == cells_z - 1, below, jnp.where(lane == 0, above, 0.0))
                own = own_row(e, line) + inner
                for b in range(2):
                    centre[a, b, e] = centre[a, b, e] - own[b]
                    edge[a, b, e] = jnp.where(edge_orders >= max(a, b, e), -outer[b], 0.0)
        resid = {}
        for key in OCTET:
            total = padded(centre[key], 1) - padded(y_low[key], 0) - padded(y_high[key], 2)
            resid[key] = jnp.where(tile_orders >= max(key), total, 0.0)
        resid, edge, x_low, x_high = corners(resid), corners(edge), corners(x_low), corners(x_high)
        for i, j, k in OCTET:
            moved = pltpu.roll(resid[i, j, k], 1, 0) if j else resid[i, j, k]
            gather_into(layers, (shift + i, k), moved)
            gather_into(border, (shift + i, j, k), edge[i, j, k])
            gather_into(near, (shift - 1 + i, j, k), x_low[i, j, k])
            gather_into(near, (shift + 1 + i, j, k), x_high[i, j, k])

    def ghost(values, side, other_orders):
        def put(a, b, high):
            part = slice(0, high)
            data = [xs[side, b, kind, part] for kind in range(2)]
            modes = jnp.maximum(last_mode[part], max(a, b))
            scale = jnp.where(modes <= other_orders[None], table_ref[a, b, part], 0.0) * (-STEP)
            values[a, b, part] = scale * one_sided(data, a, side == 1)

        for b in range(2):
            for a in range(MODES):
                put(a, b, MODES if a < 2 else 2)
        for b in range(2, MODES):
            for a in range(2):
                put(a, b, 2)

    for axis in range(3):
        over(receive, 1, axis)
    rows_of = (orders, order_x[0], order_x[1])
    lines_of = (order_y, order_xy.at[0], order_xy.at[1])
    sides_of = (order_z, order_xz.at[0], order_xz.at[1])

    def surroundings(at):
        order_tile[at, 1 : cells_y + 1] = rows_of[at]
        order_tile[at, 0:1] = lines_of[at][1]
        order_tile[at, cells_y + 1 : cells_y + 2] = lines_of[at][0]
        edge_orders = jnp.where(lane[0] == cells_z - 1, sides_of[at][1], sides_of[at][0])
        return order_tile[at], edge_orders

    ghost(ghost_up, 1, order_x[0])
    ghost(ghost_down, 0, order_x[1])
    y_over(receive, 0)
    loop(y_flux, 0, 2)
    y_over(receive, 1)
    y_flux_part(slice(0, 2))
    forward(1)
    tile_orders, edge_orders = surroundings(0)
    spread(acc, 0, rhs, tile_orders, order_x[1], order_x[0], edge_orders)
    diagonal_over(receive)

    @pl.when(collects)
    def _():
        for zz in range(nz - 1):
            pl.semaphore_signal(met.at[2], inc=1, device_id=(x, y, zz), device_id_type=MESH)

    forward(2)
    tile_orders, edge_orders = surroundings(1)
    spread(ghost_up, 1, None, tile_orders, orders, order_far[0], edge_orders)
    tile_orders, edge_orders = surroundings(2)
    spread(ghost_down, -1, None, tile_orders, order_far[1], orders, edge_orders)

    row_lane = lane[0]
    sums = {}
    def carries_of(dx):
        for number, entry in enumerate(carries):
            if entry[4] == dx:
                start(entry, 24 + number, *carry_refs(*entry[4:]))

    for dx in (1, -1, 2, 3, -2, 0):
        pair = []
        for k in range(2):
            parts = [layers[dx, k]] if (dx, k) in layers else []
            parts += [padded(near[dx, j, k], 1 + j) for j in range(2)]
            pair.append(functools.reduce(lambda p, q: p + q, parts))
        moved = pltpu.roll(pair[1], 1, 1)
        if (dx, 0, 0) in border:
            outer = [padded(border[dx, 0, k], 1) + padded(border[dx, 1, k], 2) for k in range(2)]
            outer_moved = pltpu.roll(outer[1], 1, 1)
            inside = pair[0] + jnp.where(row_lane == 0, outer_moved, moved)
            beyond = jnp.where(row_lane == 0, moved, outer_moved) + outer[0]
        else:
            inside = pair[0] + jnp.where(row_lane == 0, 0.0, moved)
            beyond = jnp.where(row_lane == 0, moved, 0.0)
        for part, value in enumerate((inside, beyond)):
            if dx == 0:
                sums[part] = value[1 : cells_y + 1]
            out_mid[dx + 2, part] = value[1 : cells_y + 1]
            out_high[dx + 2, part] = value[cells_y + 1 : cells_y + 3]
            if -1 <= dx <= 2:
                out_low[dx + 1, part] = value[0:1]
        carries_of(dx)

    direct_slot = 24 + len(carries) + len(columns)

    @pl.when(jnp.logical_not(collects))
    def _():
        pl.semaphore_wait(met.at[2], 1)

    for number, entry in enumerate(direct):
        start(entry, direct_slot + number * nz + z, *direct_refs(*entry[4:], z))

    forward(3)
    y_over(receive, 2)
    y_flux_part(slice(2, MODES))

    def x_flux(b):
        x_receive(b)
        term = face_terms(
            [xr[0, b, kind] for kind in range(2)], [xr[1, b, kind] for kind in range(2)]
        )
        for a in range(MODES):
            smooth[a, b] = acc[a, b] + coef[a, b] * term(a)

    for stage, axis in ((0, 2), (1, 0), (1, 1), (1, 2)):
        over(finish, stage, axis)
    for part in range(3):
        y_over(finish, part)
    diagonal_over(finish)
    for b in range(MODES):
        for side in range(2):

            @pl.when(halos[side][1])
            def _():
                x_copy(side, b, halos[side][0]).wait_send()

    for b in range(RELAYED):
        for side in range(2):

            @pl.when(relays[side][3])
            def _():
                from_relay(side, b, relays[side][4]).wait_send()

    loop(x_flux, RELAYED)
    loop(x_flux, 0, RELAYED)

    for number, entry in enumerate(carries):
        receive(entry, 24 + number, *carry_refs(*entry[4:]))

    for part in range(2):
        value = sums[part]
        for dx in REACH:
            if dx:
                value = value + in_mid[dx + 2, part]
        high = functools.reduce(lambda p, q: p + q, [in_high[at, part] for at in range(6)])
        low = functools.reduce(lambda p, q: p + q, [in_low[at, part] for at in range(4)])
        column[pl.ds(z, 1), part] = value[None]
        column[pl.ds(z, 1), part, 0:2] += high[None]
        column[pl.ds(z, 1), part, cells_y - 1 : cells_y] += low[None]

    def gather(number, arriving):
        entry = columns[number]
        at = entry[4] if arriving else z
        return remote(column.at[at], column.at[at], 24 + len(carries) + number, entry[0])

    def columns_over(action, arriving):
        for number, entry in enumerate(columns):
            to_collector = collects if arriving else entry[0][2] == nz - 1

            @pl.when((x > 0) & jnp.logical_not(to_collector))
            def _(number=number):
                action(number)

    columns_over(lambda number: gather(number, False).start(), False)
    for number, entry in enumerate(carries):
        finish(entry, 24 + number, *carry_refs(*entry[4:]))
    for number, entry in enumerate(direct):
        finish(entry, direct_slot + number * nz + z, *direct_refs(*entry[4:], z))
    @pl.when(collects)
    def _():
        for number, (to, _, back, ok_from, dx, dy) in enumerate(direct):
            for zz in range(nz - 1):
                slot = direct_slot + number * nz + zz
                receive((to, None, back, ok_from), slot, *direct_refs(dx, dy, zz))
        for zz in range(nz - 1):
            for part in range(2):
                column[zz, part] = functools.reduce(
                    lambda p, q: p + q, [far_mid[at, zz, part] for at in range(6)]
                )
                column[zz, part, 0:2] += functools.reduce(
                    lambda p, q: p + q, [far_high[at, zz, part] for at in range(6)]
                )
                column[zz, part, cells_y - 1 : cells_y] += functools.reduce(
                    lambda p, q: p + q, [far_low[at, zz, part] for at in range(4)]
                )

    columns_over(lambda number: gather(number, True).wait_recv(), True)
    columns_over(lambda number: gather(number, False).wait_send(), False)

    row = lax.broadcasted_iota(jnp.int32, (cells_y, cells_z), 0)
    spot = lax.broadcasted_iota(jnp.int32, (cells_y, cells_z), 1)
    for zz in range(nz):
        total = column[zz, 0]
        if zz > 0:
            total = total + jnp.where(spot < 2, column[zz - 1, 1], 0.0)
        if zz < nz - 1:
            total = total + jnp.where(spot == cells_z - 1, column[zz + 1, 1], 0.0)
        inside = (x > 0) & ((row > 0) | (y > 0))
        if zz == 0:
            inside = inside & (spot > 0)
        coarse_ref[0, :, zz * cells_z : (zz + 1) * cells_z] = jnp.where(inside, total, 0.0)


def drain(smooth, coarse, smooth_hbm, coarse_hbm, sem):
    copies = [
        pltpu.make_async_copy(smooth.at[a], smooth_hbm.at[a], sem.at[a]) for a in range(MODES)
    ]
    copies.append(pltpu.make_async_copy(coarse, coarse_hbm, sem.at[MODES]))
    for copy in copies:
        copy.start()
    for copy in copies:
        copy.wait()


def per_device(sizes, rhs, orders):
    _, cells_y, cells_z = orders.shape
    nz = sizes[2]
    table = jnp.asarray(
        np.broadcast_to(
            (1.0 / (DIAGONAL * THETA))[:, :, :, None, None], DIAGONAL.shape + (1, cells_z)
        ),
        jnp.float32,
    )
    field = rhs.reshape(rhs.shape[:3] + rhs.shape[4:])
    cells = (cells_y, cells_z)
    rows = 8 * ((cells_y + 8) // 8)
    tall = 8 * ((cells_y + 10) // 8)
    line = (2, 2, MODES, MODES)

    def buf(*shape):
        return pltpu.VMEM(shape, jnp.float32)

    def whole(*shape):
        return pltpu.VMEM(shape, jnp.int32)

    slots = 24 + len(CARRIES) + nz - 1 + (len(CARRIES) + 1) * nz
    coarse_shape = (1, cells_y, nz * cells_z)
    vmem = pl.BlockSpec(memory_space=pltpu.VMEM)
    hbm = pl.BlockSpec(memory_space=pltpu.HBM)
    smoothed, coarse = pl.pallas_call(
        functools.partial(kernel, sizes, cells_y, cells_z),
        out_shape=(pltpu.VMEM(field.shape, jnp.float32), pltpu.VMEM(coarse_shape, jnp.float32)),
        in_specs=[hbm, hbm, hbm],
        out_specs=(vmem, vmem),
        scratch_shapes=[buf(*field.shape)] * 6
        + [
            whole(*orders.shape), buf(*table.shape),
            buf(2, MODES, 2, MODES, *cells), buf(2, MODES, 2, MODES, *cells),
            buf(*line, 1, cells_z), buf(*line, 1, cells_z),
            buf(*line, *cells), buf(*line, *cells),
            buf(2, MODES, MODES, rows, cells_z), buf(2, MODES, MODES, rows, cells_z),
            whole(2, 1, cells_z), whole(2, *cells), whole(2, 1, cells_z), whole(2, *cells),
            whole(2, 2, 1, cells_z), whole(2, 2, *cells), whole(2, *cells), whole(3, tall, cells_z),
            buf(112, tall, cells_z),
            buf(6, 2, *cells), buf(6, 2, 2, cells_z), buf(4, 2, 1, cells_z),
            buf(6, 2, *cells), buf(6, 2, 2, cells_z), buf(4, 2, 1, cells_z),
            buf(6, nz, 2, *cells), buf(6, nz, 2, 2, cells_z), buf(4, nz, 2, 1, cells_z),
            buf(nz, 2, *cells),
            buf(2, RELAYED, 2, MODES, *cells),
            pltpu.SemaphoreType.DMA((MODES + 2,)),
            pltpu.SemaphoreType.DMA((slots,)),
            pltpu.SemaphoreType.DMA((slots,)),
            pltpu.SemaphoreType.DMA((2, MODES)),
            pltpu.SemaphoreType.DMA((2, MODES)),
            pltpu.SemaphoreType.DMA((2, 3)),
            pltpu.SemaphoreType.DMA((2, 3)),
            pltpu.SemaphoreType.DMA((2, RELAYED)),
            pltpu.SemaphoreType.DMA((2, RELAYED)),
            pltpu.SemaphoreType.REGULAR((3,)),
        ],
        compiler_params=pltpu.CompilerParams(collective_id=0, has_side_effects=True),
        name="smoother",
    )(field, orders, table)
    smoothed, coarse = pl.pallas_call(
        drain,
        out_shape=(
            jax.ShapeDtypeStruct(field.shape, jnp.float32),
            jax.ShapeDtypeStruct(coarse_shape, jnp.float32),
        ),
        in_specs=[vmem, vmem],
        out_specs=(hbm, hbm),
        scratch_shapes=[pltpu.SemaphoreType.DMA((MODES + 1,))],
        name="drain",
    )(
        pltpu.with_memory_space_constraint(smoothed, pltpu.VMEM),
        pltpu.with_memory_space_constraint(coarse, pltpu.VMEM),
    )
    return smoothed.reshape(rhs.shape), coarse


def solution(mesh):
    sizes = tuple(mesh.shape[axis] for axis in ("gx", "gy", "gz"))
    return jax.shard_map(
        functools.partial(per_device, sizes),
        mesh=mesh,
        in_specs=(P(None, None, None, "gx", "gy", "gz"), P("gx", "gy", "gz")),
        out_specs=(P(None, None, None, "gx", "gy", "gz"), P("gx", "gy", None)),
        check_vma=False,
    )
```

```python
import functools

import jax
import jax.numpy as jnp
import numpy as np
from jax import lax
from jax.experimental import pallas as pl
from jax.experimental.pallas import tpu as pltpu
from jax.sharding import PartitionSpec as P

PENALTY = 49.0
EIGEN_HIGH = 2.4
EIGEN_LOW = 0.24
MODES = 7
MESH = pl.DeviceIdType.MESH


def tables():
    degree = np.arange(MODES)
    normed = np.sqrt((2.0 * degree + 1.0) / 2.0)
    smaller = np.minimum(degree[:, None], degree[None, :])
    parity = (degree[:, None] + degree[None, :]) % 2 == 0
    stiffness = np.where(parity, normed[:, None] * normed[None, :] * smaller * (smaller + 1), 0.0)
    signs = (-1.0) ** degree
    slope = normed * degree * (degree + 1) / 2.0
    low, low_slope = normed * signs, -slope * signs
    own = stiffness + np.outer(normed, PENALTY * normed - 0.5 * slope) - 0.5 * np.outer(slope, normed)
    own = own + np.outer(low, PENALTY * low + 0.5 * low_slope) + 0.5 * np.outer(low_slope, low)
    one_axis = normed * normed * degree * (degree + 1) + 2.0 * (
        PENALTY * normed * normed - normed * slope
    )
    diagonal = (
        one_axis[:, None, None] + one_axis[None, :, None] + one_axis[None, None, :]
    ) / PENALTY
    return (
        own / PENALTY,
        0.5 * slope - PENALTY * normed,
        0.5 * normed,
        normed / PENALTY,
        slope / PENALTY,
        diagonal,
    )


OWN, JUMP, HALF, VALUE, SLOPE, DIAGONAL = tables()
THETA = 0.5 * (EIGEN_HIGH + EIGEN_LOW)
DELTA = 0.5 * (EIGEN_HIGH - EIGEN_LOW)
RHO_FIRST = DELTA / THETA
RHO_SECOND = 1.0 / (2.0 * THETA / DELTA - RHO_FIRST)
KEEP = 1.0 + RHO_SECOND * RHO_FIRST
STEP = 2.0 * RHO_SECOND / DELTA * THETA


def combine(weights, values):
    total = None
    for weight, value in zip(weights, values):
        term = value * float(weight)
        total = term if total is None else total + term
    return total


def traces(values):
    even, odd = values[0::2], values[1::2]
    jump_even, jump_odd = combine(JUMP[0::2], even), combine(JUMP[1::2], odd)
    half_even, half_odd = combine(HALF[0::2], even), combine(HALF[1::2], odd)
    down = (jump_even - jump_odd, half_even - half_odd)
    up = (jump_even + jump_odd, half_even + half_odd)
    return down, up


def own_row(row, values):
    start = row % 2
    return combine(OWN[row, start::2], values[start::2])


def face_terms(from_up, from_down):
    both = (from_up[0] + from_down[0], from_up[1] + from_down[1])
    apart = (from_up[0] - from_down[0], from_up[1] - from_down[1])

    def term(mode):
        pair = both if mode % 2 == 0 else apart
        if mode == 0:
            return pair[0] * float(VALUE[0])
        return pair[0] * float(VALUE[mode]) + pair[1] * float(SLOPE[mode])

    return term


def vertex_pair(zero, one):
    flat, tilt = np.sqrt(0.5) * zero, (np.sqrt(1.5) / 3.0) * one
    return flat - tilt, flat + tilt


def one_sided(data, mode, from_below):
    if mode == 0:
        return data[0] * float(VALUE[0])
    sign = -1.0 if from_below and mode % 2 else 1.0
    return data[0] * (sign * float(VALUE[mode])) + data[1] * (sign * float(SLOPE[mode]))


def corners(values):
    for axis in range(3):
        done = {}
        for key in values:
            if key[axis] == 0:
                other = tuple(1 if n == axis else key[n] for n in range(3))
                done[key], done[other] = vertex_pair(values[key], values[other])
        values = done
    return values


OCTET = [(a, b, e) for a in range(2) for b in range(2) for e in range(2)]
RELAYED = 4
SIGNS = (1, -1)
DIAGONALS = (
    [(dx, dy, 0) for dx in SIGNS for dy in SIGNS]
    + [(dx, 0, dz) for dx in SIGNS for dz in SIGNS]
    + [(2 * dx, 0, 0) for dx in SIGNS]
)
Y_PARTS = ((slice(0, 2), slice(0, MODES)), (slice(2, MODES), slice(0, 2)), (slice(2, MODES), slice(2, MODES)))
REACH = range(-2, 4)
CARRIES = (
    (1, 1), (-1, 1), (1, -1), (-1, -1), (3, 1), (2, 1), (-2, 1), (2, -1),
    (3, 0), (2, 0), (-2, 0), (1, 0), (-1, 0), (0, 1), (0, -1),
)


def kernel(
    sizes, cells_y, cells_z, rhs_hbm, orders_hbm, table_hbm, smooth, coarse_ref,
    rhs, first, acc, coef, ghost_up, ghost_down, orders_ref, table_ref,
    xs, xr, ys, yr, zs, zr, y_up, y_down,
    order_line, order_x, order_y, order_z, order_xy, order_xz, order_far, order_tile, pads,
    out_mid, out_high, out_low, in_mid, in_high, in_low, far_mid, far_high, far_low, column,
    relay, local_sem, send_sem, recv_sem, x_send, x_recv, y_send, y_recv, relay_in, relay_out, met,
):
    nx, ny, nz = sizes
    tall = pads.shape[1]
    x, y, z = lax.axis_index("gx"), lax.axis_index("gy"), lax.axis_index("gz")
    barrier = pltpu.get_barrier_semaphore()

    def neighbour(axis, sign):
        here = (x, y, z)[axis]
        to = [x, y, z]
        to[axis] = here + sign
        back = [x, y, z]
        back[axis] = here - sign
        below, above = here > 0, here < sizes[axis] - 1
        return (tuple(to), below if sign < 0 else above, tuple(back), above if sign < 0 else below)

    halos = [neighbour(axis, sign) for axis in range(3) for sign in (-1, 1)]
    always = x >= 0

    def offset(dx, dy):
        ok_to = (x + dx > 0) & (x + dx < nx)
        ok_from = (x > 0) & (x - dx >= 0) & (x - dx < nx)
        if dy > 0:
            ok_to, ok_from = ok_to & (y + dy < ny), ok_from & (y >= dy)
        if dy < 0:
            ok_to, ok_from = ok_to & (y + dy >= 0), ok_from & (y - dy < ny)
        return ((x + dx, y + dy, z), ok_to, (x - dx, y - dy, z), ok_from)

    carries = [offset(dx, dy) + (dx, dy) for dx, dy in CARRIES]
    collects = z == nz - 1
    direct = []
    for dx, dy in CARRIES + ((0, 0),):
        to, ok_to, back, ok_from = offset(dx, dy)
        to = to[:2] + (nz - 1,)
        direct.append((to, ok_to & jnp.logical_not(collects), back, ok_from, dx, dy))
    columns = []
    for r in range(1, nz):
        source = lax.rem(z - r + nz, nz)
        columns.append(((x, y, lax.rem(z + r, nz)), always, (x, y, source), always, source))

    def diagonal(offset):
        here = (x, y, z)
        to = tuple(h + d for h, d in zip(here, offset))
        back = tuple(h - d for h, d in zip(here, offset))
        ok_to, ok_from = always, always
        for axis, d in enumerate(offset):
            low, high = here[axis] >= abs(d), here[axis] + abs(d) < sizes[axis]
            if d > 0:
                ok_to, ok_from = ok_to & high, ok_from & low
            elif d < 0:
                ok_to, ok_from = ok_to & low, ok_from & high
        return (to, ok_to, back, ok_from)

    diagonals = [diagonal(offset) for offset in DIAGONALS]

    def diagonal_refs(offset):
        dx, dy, dz = offset
        if dy:
            return order_line.at[0 if dy < 0 else 1], order_xy.at[(1 + dx) // 2, (1 + dy) // 2]
        if dz:
            return orders_ref.at[0], order_xz.at[(1 + dx) // 2, (1 + dz) // 2]
        return orders_ref.at[0], order_far.at[(2 + dx) // 4]

    odd = lax.rem(x, 2) == 1
    even = jnp.logical_not(odd)
    relays = (
        ((x - 2, y, z), even & (x >= 2), (x + 2, y, z), even & (x + 2 < nx), (x + 1, y, z)),
        ((x + 2, y, z), odd & (x + 2 < nx), (x - 2, y, z), odd & (x >= 3), (x - 1, y, z)),
    )

    expected = jnp.int32(0)
    for entry in halos[:4] + columns + list(relays):
        to, ok_to, back, ok_from = entry[:4]

        @pl.when(ok_from)
        def _(back=back):
            pl.semaphore_signal(barrier, inc=1, device_id=back, device_id_type=MESH)

        expected = expected + jnp.where(ok_to, 1, 0).astype(jnp.int32)

    loads = [
        pltpu.make_async_copy(orders_hbm, orders_ref, local_sem.at[MODES]),
        pltpu.make_async_copy(table_hbm, table_ref, local_sem.at[MODES + 1]),
    ]
    for copy in loads:
        copy.start()

    def rhs_load(b):
        return pltpu.make_async_copy(rhs_hbm.at[:, b], rhs.at[:, b], local_sem.at[b])

    for b in range(MODES):
        rhs_load(b).start()

    def remote(src, dst, slot, to):
        if isinstance(slot, tuple):
            return pltpu.make_async_remote_copy(
                src_ref=src, dst_ref=dst, send_sem=y_send.at[slot], recv_sem=y_recv.at[slot],
                device_id=to, device_id_type=MESH,
            )
        return pltpu.make_async_remote_copy(
            src_ref=src, dst_ref=dst, send_sem=send_sem.at[slot], recv_sem=recv_sem.at[slot],
            device_id=to, device_id_type=MESH,
        )

    def start(entry, slot, src, dst):
        to, ok_to = entry[:2]

        @pl.when(ok_to)
        def _():
            remote(src, dst, slot, to).start()

    def receive(entry, slot, src, dst):
        to, _, _, ok_from = entry[:4]

        @pl.when(ok_from)
        def _():
            remote(src, dst, slot, to).wait_recv()

    def finish(entry, slot, src, dst):
        to, ok_to = entry[:2]

        @pl.when(ok_to)
        def _():
            remote(src, dst, slot, to).wait_send()

    stages = (
        ((xs, xr), (ys, yr), (zs, zr)),
        ((orders_ref, order_x), (order_line, order_y), (orders_ref, order_z)),
    )

    def over(action, stage, axis):
        src, dst = stages[stage][axis]
        for side in range(2):
            index = 2 * axis + side
            action(halos[index], 6 * stage + index, src.at[0 if src is orders_ref else side], dst.at[side])

    for stage, empty in ((0, 0.0), (1, -1)):
        for axis in range(3):
            for side in range(2):
                dst = stages[stage][axis][1]

                @pl.when(jnp.logical_not(halos[2 * axis + side][3]))
                def _(dst=dst, side=side, empty=empty):
                    dst[side] = jnp.full(dst.shape[1:], empty, dst.dtype)

    pads[...] = jnp.zeros(pads.shape, jnp.float32)
    order_tile[...] = jnp.full(order_tile.shape, -1, jnp.int32)
    for offset, entry in zip(DIAGONALS, diagonals):

        @pl.when(jnp.logical_not(entry[3]))
        def _(offset=offset):
            dst = diagonal_refs(offset)[1]
            dst[...] = jnp.full(dst.shape, -1, jnp.int32)

    targets = {0: (out_mid, in_mid), 1: (out_high, in_high), -1: (out_low, in_low)}

    def carry_refs(dx, dy):
        src, dst = targets[dy]
        at = dx + 1 if dy < 0 else dx + 2
        return src.at[at], dst.at[at]

    far_of = {0: far_mid, 1: far_high, -1: far_low}

    def direct_refs(dx, dy, source):
        at = dx + 1 if dy < 0 else dx + 2
        return targets[dy][0].at[at], far_of[dy].at[at, source]

    for _, _, _, ok_from, dx, dy in direct:

        @pl.when(jnp.logical_not(ok_from))
        def _(dx=dx, dy=dy):
            dst = far_of[dy].at[dx + 1 if dy < 0 else dx + 2]
            dst[...] = jnp.zeros(dst.shape, jnp.float32)

    for _, _, _, ok_from, dx, dy in carries:

        @pl.when(jnp.logical_not(ok_from))
        def _(dx=dx, dy=dy):
            dst = carry_refs(dx, dy)[1]
            dst[...] = jnp.zeros(dst.shape, jnp.float32)

    for copy in loads:
        copy.wait()
    orders = orders_ref[0]
    order_line[0] = orders[0:1]
    order_line[1] = orders[cells_y - 1 : cells_y]
    tile = (MODES, cells_y, cells_z)
    last_mode = lax.broadcasted_iota(jnp.int32, tile, 0)
    lane = lax.broadcasted_iota(jnp.int32, (1, 1, cells_z), 2)

    def active(a, b):
        return jnp.maximum(jnp.maximum(a, b), last_mode) <= orders[None]

    def loop(body, low=0, high=MODES):
        def step(index, carry):
            body(index)
            return carry

        lax.fori_loop(low, high, step, 0)

    def x_copy(side, b, to):
        return pltpu.make_async_remote_copy(
            src_ref=xs.at[side, b], dst_ref=xr.at[side, b],
            send_sem=x_send.at[side, b], recv_sem=x_recv.at[side, b],
            device_id=to, device_id_type=MESH,
        )

    def to_relay(side, b, to):
        return pltpu.make_async_remote_copy(
            src_ref=xs.at[side, b], dst_ref=relay.at[side, b],
            send_sem=x_send.at[side, b], recv_sem=relay_in.at[side, b],
            device_id=to, device_id_type=MESH,
        )

    def from_relay(side, b, to):
        return pltpu.make_async_remote_copy(
            src_ref=relay.at[side, b], dst_ref=xr.at[side, b],
            send_sem=relay_out.at[side, b], recv_sem=x_recv.at[side, b],
            device_id=to, device_id_type=MESH,
        )

    def forward(number):
        for side in range(2):
            back, relaying, target = relays[side][2:]

            @pl.when(relaying)
            def _():
                to_relay(side, number, target).wait_recv()
                from_relay(side, number, target).start()

    def x_receive(number):
        for side in range(2):

            @pl.when(halos[side][3])
            def _():
                x_copy(side, number, halos[side][0]).wait_recv()

    def x_traces(b):
        rhs_load(b).wait()
        values = []
        for a in range(MODES):
            value = jnp.where(active(a, b), table_ref[a, b] * rhs[a, b], 0.0)
            first[a, b] = value
            values.append(value)
        sides = traces(values)
        for side in range(2):
            for kind in range(2):
                xs[side, b, kind] = sides[side][kind]

    def x_start(b):
        for side in range(2):
            to, ok_to = halos[side][:2]
            via, used = relays[side][:2]
            if b < RELAYED:

                @pl.when(used)
                def _():
                    to_relay(side, b, via).start()

                ok_to = ok_to & jnp.logical_not(used)

            @pl.when(ok_to)
            def _():
                x_copy(side, b, to).start()

    def diagonal_over(action):
        for number, (offset, entry) in enumerate(zip(DIAGONALS, diagonals)):
            action(entry, 14 + number, *diagonal_refs(offset))

    def y_over(action, part):
        modes = Y_PARTS[part]
        for side in range(2):
            at = (side, slice(None)) + modes
            action(halos[2 + side], (side, part), ys.at[at], yr.at[at])

    def meet(action):
        for side in range(2):
            to, ok_to, _, ok_from = halos[side]

            @pl.when(ok_to if action == "tell" else ok_from)
            def _():
                if action == "tell":
                    pl.semaphore_signal(met.at[side], inc=1, device_id=to, device_id_type=MESH)
                else:
                    pl.semaphore_wait(met.at[side], 1)

    loop(x_traces, 0, 5)
    pl.semaphore_wait(barrier, expected)
    meet("tell")
    over(start, 1, 0)
    over(start, 1, 1)
    over(start, 1, 2)
    x_start(0)
    x_start(1)
    x_start(2)
    loop(x_traces, 5)

    def y_faces(a, values, send, up_buf, down_buf):
        down, up = traces(values)
        for kind in range(2):
            up_buf[kind, a, :, 0:cells_y, :] = down[kind]
            down_buf[kind, a, :, 1 : cells_y + 1, :] = up[kind]
            send[0, kind, a] = down[kind][:, 0:1, :]
            send[1, kind, a] = up[kind][:, cells_y - 1 : cells_y, :]

    def y_neighbours(a, received, up_buf, down_buf, part=slice(0, MODES)):
        for kind in range(2):
            up_buf[kind, a, part, cells_y : cells_y + 1, :] = received[0, kind, a, part]
            down_buf[kind, a, part, 0:1, :] = received[1, kind, a, part]
        return (
            [up_buf[kind, a, part, 1 : cells_y + 1, :] for kind in range(2)],
            [down_buf[kind, a, part, 0:cells_y, :] for kind in range(2)],
        )

    def z_faces(a, values, send):
        sides = traces(values)
        for side in range(2):
            for kind in range(2):
                send[side, kind, a] = sides[side][kind]

    def z_neighbours(a, send, received, part=slice(0, MODES)):
        def moved(side, kind, edge, amount):
            picked = jnp.where(lane == edge, received[side, kind, a, part], send[side, kind, a, part])
            return pltpu.roll(picked, amount, 2)

        return (
            [moved(0, kind, 0, cells_z - 1) for kind in range(2)],
            [moved(1, kind, cells_z - 1, 1) for kind in range(2)],
        )

    def y_traces(a):
        y_faces(a, [first[a, b] for b in range(MODES)], ys, y_up, y_down)

    loop(y_traces, 0, 2)
    y_over(start, 0)
    loop(y_traces, 2)
    y_over(start, 1)
    meet("hear")
    diagonal_over(start)
    x_start(3)
    y_over(start, 2)
    loop(lambda a: z_faces(a, [first[a, :, e] for e in range(MODES)], zs))
    over(start, 0, 2)

    def predict(a, b, part, total):
        right = rhs[a, b, part]
        modes = jnp.maximum(last_mode[part], jnp.maximum(a, b))
        scale = jnp.where(modes <= orders[None], table_ref[a, b, part], 0.0)
        return scale * (KEEP * right + STEP * (right - total)), scale * (-STEP)

    def x_own(b):
        values = [first[a, b] for a in range(MODES)]
        for a in range(MODES):
            acc[a, b] = own_row(a, values)

    def y_own(a):
        values = [first[a, b] for b in range(MODES)]
        for b in range(MODES):
            acc[a, b] += own_row(b, values)

    def z_own(a):
        values = [first[a, :, e] for e in range(MODES)]
        for e in range(MODES):
            acc[a, :, e] += own_row(e, values)

    def z_flux(a):
        term = face_terms(*z_neighbours(a, zs, zr))
        for e in range(MODES):
            acc[a, :, e] += term(e)

    def y_flux(a):
        term = face_terms(*y_neighbours(a, yr, y_up, y_down))
        for b in range(MODES):
            acc[a, b], coef[a, b] = predict(a, b, slice(0, MODES), acc[a, b] + term(b))

    def y_flux_part(part):
        def step(a):
            term = face_terms(*y_neighbours(a, yr, y_up, y_down, part))
            for b in range(MODES):
                acc[a, b, part], coef[a, b, part] = predict(a, b, part, acc[a, b, part] + term(b))

        loop(step, 2)

    loop(x_own)
    x_start(4)
    x_start(5)
    loop(y_own)
    x_start(6)
    loop(z_own)
    over(receive, 0, 2)
    loop(z_flux)
    forward(0)

    slots = iter(range(pads.shape[0]))

    def padded(value, at):
        slot = next(slots)
        pads[slot, at : at + cells_y, :] = value
        return pads[slot]

    near, border, layers = {}, {}, {}

    def gather_into(where_to, key, value):
        where_to[key] = where_to[key] + value if key in where_to else value

    def spread(values, shift, forced, tile_orders, low_orders, high_orders, edge_orders):
        centre, edge, x_low, x_high, y_low, y_high = {}, {}, {}, {}, {}, {}
        for b in range(2):
            line = [values[a, b, 0:2] for a in range(MODES)]
            down, up = traces(line)
            for a in range(2):
                own = own_row(a, line)
                below, above = one_sided(down, a, False), one_sided(up, a, True)
                for e in range(2):
                    centre[a, b, e] = forced[a, b, e] - own[e] if forced is not None else -own[e]
                    x_low[a, b, e] = jnp.where(low_orders >= max(a, b, e), -below[e], 0.0)
                    x_high[a, b, e] = jnp.where(high_orders >= max(a, b, e), -above[e], 0.0)
        for a in range(2):
            line = [values[a, b, 0:2] for b in range(MODES)]
            down, up = traces(line)
            for b in range(2):
                own = own_row(b, line)
                below, above = one_sided(down, b, False), one_sided(up, b, True)
                for e in range(2):
                    centre[a, b, e] = centre[a, b, e] - own[e]
                    y_low[a, b, e], y_high[a, b, e] = below[e], above[e]
            line = [values[a, 0:2, e] for e in range(MODES)]
            down, up = traces(line)
            for e in range(2):
                below = pltpu.roll(one_sided(down, e, False), cells_z - 1, 2)
                above = pltpu.roll(one_sided(up, e, True), 1, 2)
                inner = jnp.where(lane == cells_z - 1, 0.0, below) + jnp.where(lane == 0, 0.0, above)
                outer = jnp.where(lane == cells_z - 1, below, jnp.where(lane == 0, above, 0.0))
                own = own_row(e, line) + inner
                for b in range(2):
                    centre[a, b, e] = centre[a, b, e] - own[b]
                    edge[a, b, e] = jnp.where(edge_orders >= max(a, b, e), -outer[b], 0.0)
        resid = {}
        for key in OCTET:
            total = padded(centre[key], 1) - padded(y_low[key], 0) - padded(y_high[key], 2)
            resid[key] = jnp.where(tile_orders >= max(key), total, 0.0)
        resid, edge, x_low, x_high = corners(resid), corners(edge), corners(x_low), corners(x_high)
        for i, j, k in OCTET:
            moved = pltpu.roll(resid[i, j, k], 1, 0) if j else resid[i, j, k]
            gather_into(layers, (shift + i, k), moved)
            gather_into(border, (shift + i, j, k), edge[i, j, k])
            gather_into(near, (shift - 1 + i, j, k), x_low[i, j, k])
            gather_into(near, (shift + 1 + i, j, k), x_high[i, j, k])

    def ghost(values, side, other_orders):
        def put(a, b, high):
            part = slice(0, high)
            data = [xs[side, b, kind, part] for kind in range(2)]
            modes = jnp.maximum(last_mode[part], max(a, b))
            scale = jnp.where(modes <= other_orders[None], table_ref[a, b, part], 0.0) * (-STEP)
            values[a, b, part] = scale * one_sided(data, a, side == 1)

        for b in range(2):
            for a in range(MODES):
                put(a, b, MODES if a < 2 else 2)
        for b in range(2, MODES):
            for a in range(2):
                put(a, b, 2)

    for axis in range(3):
        over(receive, 1, axis)
    rows_of = (orders, order_x[0], order_x[1])
    lines_of = (order_y, order_xy.at[0], order_xy.at[1])
    sides_of = (order_z, order_xz.at[0], order_xz.at[1])

    def surroundings(at):
        order_tile[at, 1 : cells_y + 1] = rows_of[at]
        order_tile[at, 0:1] = lines_of[at][1]
        order_tile[at, cells_y + 1 : cells_y + 2] = lines_of[at][0]
        edge_orders = jnp.where(lane[0] == cells_z - 1, sides_of[at][1], sides_of[at][0])
        return order_tile[at], edge_orders

    ghost(ghost_up, 1, order_x[0])
    ghost(ghost_down, 0, order_x[1])
    y_over(receive, 0)
    loop(y_flux, 0, 2)
    y_over(receive, 1)
    y_flux_part(slice(0, 2))
    forward(1)
    tile_orders, edge_orders = surroundings(0)
    spread(acc, 0, rhs, tile_orders, order_x[1], order_x[0], edge_orders)
    diagonal_over(receive)

    @pl.when(collects)
    def _():
        for zz in range(nz - 1):
            pl.semaphore_signal(met.at[2], inc=1, device_id=(x, y, zz), device_id_type=MESH)

    forward(2)
    tile_orders, edge_orders = surroundings(1)
    spread(ghost_up, 1, None, tile_orders, orders, order_far[0], edge_orders)
    tile_orders, edge_orders = surroundings(2)
    spread(ghost_down, -1, None, tile_orders, order_far[1], orders, edge_orders)

    row_lane = lane[0]
    sums = {}
    def carries_of(dx):
        for number, entry in enumerate(carries):
            if entry[4] == dx:
                start(entry, 24 + number, *carry_refs(*entry[4:]))

    for dx in (1, -1, 2, 3, -2, 0):
        pair = []
        for k in range(2):
            parts = [layers[dx, k]] if (dx, k) in layers else []
            parts += [padded(near[dx, j, k], 1 + j) for j in range(2)]
            pair.append(functools.reduce(lambda p, q: p + q, parts))
        moved = pltpu.roll(pair[1], 1, 1)
        if (dx, 0, 0) in border:
            outer = [padded(border[dx, 0, k], 1) + padded(border[dx, 1, k], 2) for k in range(2)]
            outer_moved = pltpu.roll(outer[1], 1, 1)
            inside = pair[0] + jnp.where(row_lane == 0, outer_moved, moved)
            beyond = jnp.where(row_lane == 0, moved, outer_moved) + outer[0]
        else:
            inside = pair[0] + jnp.where(row_lane == 0, 0.0, moved)
            beyond = jnp.where(row_lane == 0, moved, 0.0)
        for part, value in enumerate((inside, beyond)):
            if dx == 0:
                sums[part] = value[1 : cells_y + 1]
            out_mid[dx + 2, part] = value[1 : cells_y + 1]
            out_high[dx + 2, part] = value[cells_y + 1 : cells_y + 3]
            if -1 <= dx <= 2:
                out_low[dx + 1, part] = value[0:1]
        carries_of(dx)

    direct_slot = 24 + len(carries) + len(columns)

    @pl.when(jnp.logical_not(collects))
    def _():
        pl.semaphore_wait(met.at[2], 1)

    for number, entry in enumerate(direct):
        start(entry, direct_slot + number * nz + z, *direct_refs(*entry[4:], z))

    forward(3)
    y_over(receive, 2)
    y_flux_part(slice(2, MODES))

    def x_flux(b):
        x_receive(b)
        term = face_terms(
            [xr[0, b, kind] for kind in range(2)], [xr[1, b, kind] for kind in range(2)]
        )
        for a in range(MODES):
            smooth[a, b] = acc[a, b] + coef[a, b] * term(a)

    for stage, axis in ((0, 2), (1, 0), (1, 1), (1, 2)):
        over(finish, stage, axis)
    for part in range(3):
        y_over(finish, part)
    diagonal_over(finish)
    for b in range(MODES):
        for side in range(2):

            @pl.when(halos[side][1])
            def _():
                x_copy(side, b, halos[side][0]).wait_send()

    for b in range(RELAYED):
        for side in range(2):

            @pl.when(relays[side][3])
            def _():
                from_relay(side, b, relays[side][4]).wait_send()

    loop(x_flux, RELAYED)
    loop(x_flux, 0, RELAYED)

    for number, entry in enumerate(carries):
        receive(entry, 24 + number, *carry_refs(*entry[4:]))

    for part in range(2):
        value = sums[part]
        for dx in REACH:
            if dx:
                value = value + in_mid[dx + 2, part]
        high = functools.reduce(lambda p, q: p + q, [in_high[at, part] for at in range(6)])
        low = functools.reduce(lambda p, q: p + q, [in_low[at, part] for at in range(4)])
        column[pl.ds(z, 1), part] = value[None]
        column[pl.ds(z, 1), part, 0:2] += high[None]
        column[pl.ds(z, 1), part, cells_y - 1 : cells_y] += low[None]

    def gather(number, arriving):
        entry = columns[number]
        at = entry[4] if arriving else z
        return remote(column.at[at], column.at[at], 24 + len(carries) + number, entry[0])

    def columns_over(action, arriving):
        for number, entry in enumerate(columns):
            to_collector = collects if arriving else entry[0][2] == nz - 1

            @pl.when((x > 0) & jnp.logical_not(to_collector))
            def _(number=number):
                action(number)

    columns_over(lambda number: gather(number, False).start(), False)
    for number, entry in enumerate(carries):
        finish(entry, 24 + number, *carry_refs(*entry[4:]))
    for number, entry in enumerate(direct):
        finish(entry, direct_slot + number * nz + z, *direct_refs(*entry[4:], z))
    @pl.when(collects)
    def _():
        for number, (to, _, back, ok_from, dx, dy) in enumerate(direct):
            for zz in range(nz - 1):
                slot = direct_slot + number * nz + zz
                receive((to, None, back, ok_from), slot, *direct_refs(dx, dy, zz))
        for zz in range(nz - 1):
            for part in range(2):
                column[zz, part] = functools.reduce(
                    lambda p, q: p + q, [far_mid[at, zz, part] for at in range(6)]
                )
                column[zz, part, 0:2] += functools.reduce(
                    lambda p, q: p + q, [far_high[at, zz, part] for at in range(6)]
                )
                column[zz, part, cells_y - 1 : cells_y] += functools.reduce(
                    lambda p, q: p + q, [far_low[at, zz, part] for at in range(4)]
                )

    columns_over(lambda number: gather(number, True).wait_recv(), True)
    columns_over(lambda number: gather(number, False).wait_send(), False)

    row = lax.broadcasted_iota(jnp.int32, (cells_y, cells_z), 0)
    spot = lax.broadcasted_iota(jnp.int32, (cells_y, cells_z), 1)
    for zz in range(nz):
        total = column[zz, 0]
        if zz > 0:
            total = total + jnp.where(spot < 2, column[zz - 1, 1], 0.0)
        if zz < nz - 1:
            total = total + jnp.where(spot == cells_z - 1, column[zz + 1, 1], 0.0)
        inside = (x > 0) & ((row > 0) | (y > 0))
        if zz == 0:
            inside = inside & (spot > 0)
        coarse_ref[0, :, zz * cells_z : (zz + 1) * cells_z] = jnp.where(inside, total, 0.0)


def drain(smooth, coarse, smooth_hbm, coarse_hbm, sem):
    copies = [
        pltpu.make_async_copy(smooth.at[a], smooth_hbm.at[a], sem.at[a]) for a in range(MODES)
    ]
    copies.append(pltpu.make_async_copy(coarse, coarse_hbm, sem.at[MODES]))
    for copy in copies:
        copy.start()
    for copy in copies:
        copy.wait()


def per_device(sizes, rhs, orders):
    _, cells_y, cells_z = orders.shape
    nz = sizes[2]
    table = jnp.asarray(
        np.broadcast_to(
            (1.0 / (DIAGONAL * THETA))[:, :, :, None, None], DIAGONAL.shape + (1, cells_z)
        ),
        jnp.float32,
    )
    field = rhs.reshape(rhs.shape[:3] + rhs.shape[4:])
    cells = (cells_y, cells_z)
    rows = 8 * ((cells_y + 8) // 8)
    tall = 8 * ((cells_y + 10) // 8)
    line = (2, 2, MODES, MODES)

    def buf(*shape):
        return pltpu.VMEM(shape, jnp.float32)

    def whole(*shape):
        return pltpu.VMEM(shape, jnp.int32)

    slots = 24 + len(CARRIES) + nz - 1 + (len(CARRIES) + 1) * nz
    coarse_shape = (1, cells_y, nz * cells_z)
    vmem = pl.BlockSpec(memory_space=pltpu.VMEM)
    hbm = pl.BlockSpec(memory_space=pltpu.HBM)
    smoothed, coarse = pl.pallas_call(
        functools.partial(kernel, sizes, cells_y, cells_z),
        out_shape=(pltpu.VMEM(field.shape, jnp.float32), pltpu.VMEM(coarse_shape, jnp.float32)),
        in_specs=[hbm, hbm, hbm],
        out_specs=(vmem, vmem),
        scratch_shapes=[buf(*field.shape)] * 6
        + [
            whole(*orders.shape), buf(*table.shape),
            buf(2, MODES, 2, MODES, *cells), buf(2, MODES, 2, MODES, *cells),
            buf(*line, 1, cells_z), buf(*line, 1, cells_z),
            buf(*line, *cells), buf(*line, *cells),
            buf(2, MODES, MODES, rows, cells_z), buf(2, MODES, MODES, rows, cells_z),
            whole(2, 1, cells_z), whole(2, *cells), whole(2, 1, cells_z), whole(2, *cells),
            whole(2, 2, 1, cells_z), whole(2, 2, *cells), whole(2, *cells), whole(3, tall, cells_z),
            buf(112, tall, cells_z),
            buf(6, 2, *cells), buf(6, 2, 2, cells_z), buf(4, 2, 1, cells_z),
            buf(6, 2, *cells), buf(6, 2, 2, cells_z), buf(4, 2, 1, cells_z),
            buf(6, nz, 2, *cells), buf(6, nz, 2, 2, cells_z), buf(4, nz, 2, 1, cells_z),
            buf(nz, 2, *cells),
            buf(2, RELAYED, 2, MODES, *cells),
            pltpu.SemaphoreType.DMA((MODES + 2,)),
            pltpu.SemaphoreType.DMA((slots,)),
            pltpu.SemaphoreType.DMA((slots,)),
            pltpu.SemaphoreType.DMA((2, MODES)),
            pltpu.SemaphoreType.DMA((2, MODES)),
            pltpu.SemaphoreType.DMA((2, 3)),
            pltpu.SemaphoreType.DMA((2, 3)),
            pltpu.SemaphoreType.DMA((2, RELAYED)),
            pltpu.SemaphoreType.DMA((2, RELAYED)),
            pltpu.SemaphoreType.REGULAR((3,)),
        ],
        compiler_params=pltpu.CompilerParams(collective_id=0, has_side_effects=True),
        name="smoother",
    )(field, orders, table)
    smoothed, coarse = pl.pallas_call(
        drain,
        out_shape=(
            jax.ShapeDtypeStruct(field.shape, jnp.float32),
            jax.ShapeDtypeStruct(coarse_shape, jnp.float32),
        ),
        in_specs=[vmem, vmem],
        out_specs=(hbm, hbm),
        scratch_shapes=[pltpu.SemaphoreType.DMA((MODES + 1,))],
        name="drain",
    )(
        pltpu.with_memory_space_constraint(smoothed, pltpu.VMEM),
        pltpu.with_memory_space_constraint(coarse, pltpu.VMEM),
    )
    return smoothed.reshape(rhs.shape), coarse


def solution(mesh):
    sizes = tuple(mesh.shape[axis] for axis in ("gx", "gy", "gz"))
    return jax.shard_map(
        functools.partial(per_device, sizes),
        mesh=mesh,
        in_specs=(P(None, None, None, "gx", "gy", "gz"), P("gx", "gy", "gz")),
        out_specs=(P(None, None, None, "gx", "gy", "gz"), P("gx", "gy", None)),
        check_vma=False,
    )
```

```python
import functools

import jax
import jax.numpy as jnp
import numpy as np
from jax import lax
from jax.experimental import pallas as pl
from jax.experimental.pallas import tpu as pltpu
from jax.sharding import PartitionSpec as P

PENALTY = 49.0
EIGEN_HIGH = 2.4
EIGEN_LOW = 0.24
MODES = 7
MESH = pl.DeviceIdType.MESH


def tables():
    degree = np.arange(MODES)
    normed = np.sqrt((2.0 * degree + 1.0) / 2.0)
    smaller = np.minimum(degree[:, None], degree[None, :])
    parity = (degree[:, None] + degree[None, :]) % 2 == 0
    stiffness = np.where(parity, normed[:, None] * normed[None, :] * smaller * (smaller + 1), 0.0)
    signs = (-1.0) ** degree
    slope = normed * degree * (degree + 1) / 2.0
    low, low_slope = normed * signs, -slope * signs
    own = stiffness + np.outer(normed, PENALTY * normed - 0.5 * slope) - 0.5 * np.outer(slope, normed)
    own = own + np.outer(low, PENALTY * low + 0.5 * low_slope) + 0.5 * np.outer(low_slope, low)
    one_axis = normed * normed * degree * (degree + 1) + 2.0 * (
        PENALTY * normed * normed - normed * slope
    )
    diagonal = (
        one_axis[:, None, None] + one_axis[None, :, None] + one_axis[None, None, :]
    ) / PENALTY
    return (
        own / PENALTY,
        0.5 * slope - PENALTY * normed,
        0.5 * normed,
        normed / PENALTY,
        slope / PENALTY,
        diagonal,
    )


OWN, JUMP, HALF, VALUE, SLOPE, DIAGONAL = tables()
THETA = 0.5 * (EIGEN_HIGH + EIGEN_LOW)
DELTA = 0.5 * (EIGEN_HIGH - EIGEN_LOW)
RHO_FIRST = DELTA / THETA
RHO_SECOND = 1.0 / (2.0 * THETA / DELTA - RHO_FIRST)
KEEP = 1.0 + RHO_SECOND * RHO_FIRST
STEP = 2.0 * RHO_SECOND / DELTA * THETA


def combine(weights, values):
    total = None
    for weight, value in zip(weights, values):
        term = value * float(weight)
        total = term if total is None else total + term
    return total


def traces(values):
    even, odd = values[0::2], values[1::2]
    jump_even, jump_odd = combine(JUMP[0::2], even), combine(JUMP[1::2], odd)
    half_even, half_odd = combine(HALF[0::2], even), combine(HALF[1::2], odd)
    down = (jump_even - jump_odd, half_even - half_odd)
    up = (jump_even + jump_odd, half_even + half_odd)
    return down, up


def own_row(row, values):
    start = row % 2
    return combine(OWN[row, start::2], values[start::2])


def face_terms(from_up, from_down):
    both = (from_up[0] + from_down[0], from_up[1] + from_down[1])
    apart = (from_up[0] - from_down[0], from_up[1] - from_down[1])

    def term(mode):
        pair = both if mode % 2 == 0 else apart
        if mode == 0:
            return pair[0] * float(VALUE[0])
        return pair[0] * float(VALUE[mode]) + pair[1] * float(SLOPE[mode])

    return term


def vertex_pair(zero, one):
    flat, tilt = np.sqrt(0.5) * zero, (np.sqrt(1.5) / 3.0) * one
    return flat - tilt, flat + tilt


def one_sided(data, mode, from_below):
    if mode == 0:
        return data[0] * float(VALUE[0])
    sign = -1.0 if from_below and mode % 2 else 1.0
    return data[0] * (sign * float(VALUE[mode])) + data[1] * (sign * float(SLOPE[mode]))


def corners(values):
    for axis in range(3):
        done = {}
        for key in values:
            if key[axis] == 0:
                other = tuple(1 if n == axis else key[n] for n in range(3))
                done[key], done[other] = vertex_pair(values[key], values[other])
        values = done
    return values


OCTET = [(a, b, e) for a in range(2) for b in range(2) for e in range(2)]
RELAYED = 4
SIGNS = (1, -1)
DIAGONALS = (
    [(dx, dy, 0) for dx in SIGNS for dy in SIGNS]
    + [(dx, 0, dz) for dx in SIGNS for dz in SIGNS]
    + [(2 * dx, 0, 0) for dx in SIGNS]
)
Y_PARTS = ((slice(0, 2), slice(0, MODES)), (slice(2, MODES), slice(0, 2)), (slice(2, MODES), slice(2, MODES)))
REACH = range(-2, 4)
CARRIES = (
    (1, 1), (-1, 1), (1, -1), (-1, -1), (3, 1), (2, 1), (-2, 1), (2, -1),
    (3, 0), (2, 0), (-2, 0), (1, 0), (-1, 0), (0, 1), (0, -1),
)


def kernel(
    sizes, cells_y, cells_z, rhs_hbm, orders_hbm, table_hbm, smooth, coarse_ref,
    rhs, first, acc, coef, ghost_up, ghost_down, orders_ref, table_ref,
    xs, xr, ys, yr, zs, zr, y_up, y_down,
    order_line, order_x, order_y, order_z, order_xy, order_xz, order_far, order_tile, pads,
    out_mid, out_high, out_low, in_mid, in_high, in_low, far_mid, far_high, far_low, column,
    relay, local_sem, send_sem, recv_sem, x_send, x_recv, y_send, y_recv, relay_in, relay_out, met,
):
    nx, ny, nz = sizes
    tall = pads.shape[1]
    x, y, z = lax.axis_index("gx"), lax.axis_index("gy"), lax.axis_index("gz")
    barrier = pltpu.get_barrier_semaphore()

    def neighbour(axis, sign):
        here = (x, y, z)[axis]
        to = [x, y, z]
        to[axis] = here + sign
        back = [x, y, z]
        back[axis] = here - sign
        below, above = here > 0, here < sizes[axis] - 1
        return (tuple(to), below if sign < 0 else above, tuple(back), above if sign < 0 else below)

    halos = [neighbour(axis, sign) for axis in range(3) for sign in (-1, 1)]
    always = x >= 0

    def offset(dx, dy):
        ok_to = (x + dx > 0) & (x + dx < nx)
        ok_from = (x > 0) & (x - dx >= 0) & (x - dx < nx)
        if dy > 0:
            ok_to, ok_from = ok_to & (y + dy < ny), ok_from & (y >= dy)
        if dy < 0:
            ok_to, ok_from = ok_to & (y + dy >= 0), ok_from & (y - dy < ny)
        return ((x + dx, y + dy, z), ok_to, (x - dx, y - dy, z), ok_from)

    carries = [offset(dx, dy) + (dx, dy) for dx, dy in CARRIES]
    collects = z == nz - 1
    direct = []
    for dx, dy in CARRIES + ((0, 0),):
        to, ok_to, back, ok_from = offset(dx, dy)
        to = to[:2] + (nz - 1,)
        direct.append((to, ok_to & jnp.logical_not(collects), back, ok_from, dx, dy))
    columns = []
    for r in range(1, nz):
        source = lax.rem(z - r + nz, nz)
        columns.append(((x, y, lax.rem(z + r, nz)), always, (x, y, source), always, source))

    def diagonal(offset):
        here = (x, y, z)
        to = tuple(h + d for h, d in zip(here, offset))
        back = tuple(h - d for h, d in zip(here, offset))
        ok_to, ok_from = always, always
        for axis, d in enumerate(offset):
            low, high = here[axis] >= abs(d), here[axis] + abs(d) < sizes[axis]
            if d > 0:
                ok_to, ok_from = ok_to & high, ok_from & low
            elif d < 0:
                ok_to, ok_from = ok_to & low, ok_from & high
        return (to, ok_to, back, ok_from)

    diagonals = [diagonal(offset) for offset in DIAGONALS]

    def diagonal_refs(offset):
        dx, dy, dz = offset
        if dy:
            return order_line.at[0 if dy < 0 else 1], order_xy.at[(1 + dx) // 2, (1 + dy) // 2]
        if dz:
            return orders_ref.at[0], order_xz.at[(1 + dx) // 2, (1 + dz) // 2]
        return orders_ref.at[0], order_far.at[(2 + dx) // 4]

    odd = lax.rem(x, 2) == 1
    even = jnp.logical_not(odd)
    relays = (
        ((x - 2, y, z), even & (x >= 2), (x + 2, y, z), even & (x + 2 < nx), (x + 1, y, z)),
        ((x + 2, y, z), odd & (x + 2 < nx), (x - 2, y, z), odd & (x >= 3), (x - 1, y, z)),
    )

    expected = jnp.int32(0)
    for entry in halos[:4] + columns + list(relays):
        to, ok_to, back, ok_from = entry[:4]

        @pl.when(ok_from)
        def _(back=back):
            pl.semaphore_signal(barrier, inc=1, device_id=back, device_id_type=MESH)

        expected = expected + jnp.where(ok_to, 1, 0).astype(jnp.int32)

    loads = [
        pltpu.make_async_copy(orders_hbm, orders_ref, local_sem.at[MODES]),
        pltpu.make_async_copy(table_hbm, table_ref, local_sem.at[MODES + 1]),
    ]
    for copy in loads:
        copy.start()

    def rhs_load(b):
        return pltpu.make_async_copy(rhs_hbm.at[:, b], rhs.at[:, b], local_sem.at[b])

    for b in range(MODES):
        rhs_load(b).start()

    def remote(src, dst, slot, to):
        if isinstance(slot, tuple):
            return pltpu.make_async_remote_copy(
                src_ref=src, dst_ref=dst, send_sem=y_send.at[slot], recv_sem=y_recv.at[slot],
                device_id=to, device_id_type=MESH,
            )
        return pltpu.make_async_remote_copy(
            src_ref=src, dst_ref=dst, send_sem=send_sem.at[slot], recv_sem=recv_sem.at[slot],
            device_id=to, device_id_type=MESH,
        )

    def start(entry, slot, src, dst):
        to, ok_to = entry[:2]

        @pl.when(ok_to)
        def _():
            remote(src, dst, slot, to).start()

    def receive(entry, slot, src, dst):
        to, _, _, ok_from = entry[:4]

        @pl.when(ok_from)
        def _():
            remote(src, dst, slot, to).wait_recv()

    def finish(entry, slot, src, dst):
        to, ok_to = entry[:2]

        @pl.when(ok_to)
        def _():
            remote(src, dst, slot, to).wait_send()

    stages = (
        ((xs, xr), (ys, yr), (zs, zr)),
        ((orders_ref, order_x), (order_line, order_y), (orders_ref, order_z)),
    )

    def over(action, stage, axis):
        src, dst = stages[stage][axis]
        for side in range(2):
            index = 2 * axis + side
            action(halos[index], 6 * stage + index, src.at[0 if src is orders_ref else side], dst.at[side])

    for stage, empty in ((0, 0.0), (1, -1)):
        for axis in range(3):
            for side in range(2):
                dst = stages[stage][axis][1]

                @pl.when(jnp.logical_not(halos[2 * axis + side][3]))
                def _(dst=dst, side=side, empty=empty):
                    dst[side] = jnp.full(dst.shape[1:], empty, dst.dtype)

    pads[...] = jnp.zeros(pads.shape, jnp.float32)
    order_tile[...] = jnp.full(order_tile.shape, -1, jnp.int32)
    for offset, entry in zip(DIAGONALS, diagonals):

        @pl.when(jnp.logical_not(entry[3]))
        def _(offset=offset):
            dst = diagonal_refs(offset)[1]
            dst[...] = jnp.full(dst.shape, -1, jnp.int32)

    targets = {0: (out_mid, in_mid), 1: (out_high, in_high), -1: (out_low, in_low)}

    def carry_refs(dx, dy):
        src, dst = targets[dy]
        at = dx + 1 if dy < 0 else dx + 2
        return src.at[at], dst.at[at]

    far_of = {0: far_mid, 1: far_high, -1: far_low}

    def direct_refs(dx, dy, source):
        at = dx + 1 if dy < 0 else dx + 2
        return targets[dy][0].at[at], far_of[dy].at[at, source]

    for _, _, _, ok_from, dx, dy in direct:

        @pl.when(jnp.logical_not(ok_from))
        def _(dx=dx, dy=dy):
            dst = far_of[dy].at[dx + 1 if dy < 0 else dx + 2]
            dst[...] = jnp.zeros(dst.shape, jnp.float32)

    for _, _, _, ok_from, dx, dy in carries:

        @pl.when(jnp.logical_not(ok_from))
        def _(dx=dx, dy=dy):
            dst = carry_refs(dx, dy)[1]
            dst[...] = jnp.zeros(dst.shape, jnp.float32)

    for copy in loads:
        copy.wait()
    orders = orders_ref[0]
    order_line[0] = orders[0:1]
    order_line[1] = orders[cells_y - 1 : cells_y]
    tile = (MODES, cells_y, cells_z)
    last_mode = lax.broadcasted_iota(jnp.int32, tile, 0)
    lane = lax.broadcasted_iota(jnp.int32, (1, 1, cells_z), 2)

    def active(a, b):
        return jnp.maximum(jnp.maximum(a, b), last_mode) <= orders[None]

    def loop(body, low=0, high=MODES):
        def step(index, carry):
            body(index)
            return carry

        lax.fori_loop(low, high, step, 0)

    def x_copy(side, b, to):
        return pltpu.make_async_remote_copy(
            src_ref=xs.at[side, b], dst_ref=xr.at[side, b],
            send_sem=x_send.at[side, b], recv_sem=x_recv.at[side, b],
            device_id=to, device_id_type=MESH,
        )

    def to_relay(side, b, to):
        return pltpu.make_async_remote_copy(
            src_ref=xs.at[side, b], dst_ref=relay.at[side, b],
            send_sem=x_send.at[side, b], recv_sem=relay_in.at[side, b],
            device_id=to, device_id_type=MESH,
        )

    def from_relay(side, b, to):
        return pltpu.make_async_remote_copy(
            src_ref=relay.at[side, b], dst_ref=xr.at[side, b],
            send_sem=relay_out.at[side, b], recv_sem=x_recv.at[side, b],
            device_id=to, device_id_type=MESH,
        )

    def forward(number):
        for side in range(2):
            back, relaying, target = relays[side][2:]

            @pl.when(relaying)
            def _():
                to_relay(side, number, target).wait_recv()
                from_relay(side, number, target).start()

    def x_receive(number):
        for side in range(2):

            @pl.when(halos[side][3])
            def _():
                x_copy(side, number, halos[side][0]).wait_recv()

    def x_traces(b):
        rhs_load(b).wait()
        values = []
        for a in range(MODES):
            value = jnp.where(active(a, b), table_ref[a, b] * rhs[a, b], 0.0)
            first[a, b] = value
            values.append(value)
        sides = traces(values)
        for side in range(2):
            for kind in range(2):
                xs[side, b, kind] = sides[side][kind]

    def x_start(b):
        for side in range(2):
            to, ok_to = halos[side][:2]
            via, used = relays[side][:2]
            if b < RELAYED:

                @pl.when(used)
                def _():
                    to_relay(side, b, via).start()

                ok_to = ok_to & jnp.logical_not(used)

            @pl.when(ok_to)
            def _():
                x_copy(side, b, to).start()

    def diagonal_over(action):
        for number, (offset, entry) in enumerate(zip(DIAGONALS, diagonals)):
            action(entry, 14 + number, *diagonal_refs(offset))

    def y_over(action, part):
        modes = Y_PARTS[part]
        for side in range(2):
            at = (side, slice(None)) + modes
            action(halos[2 + side], (side, part), ys.at[at], yr.at[at])

    def meet(action):
        for side in range(2):
            to, ok_to, _, ok_from = halos[side]

            @pl.when(ok_to if action == "tell" else ok_from)
            def _():
                if action == "tell":
                    pl.semaphore_signal(met.at[side], inc=1, device_id=to, device_id_type=MESH)
                else:
                    pl.semaphore_wait(met.at[side], 1)

    loop(x_traces, 0, 5)
    pl.semaphore_wait(barrier, expected)
    meet("tell")
    over(start, 1, 0)
    over(start, 1, 1)
    over(start, 1, 2)
    x_start(0)
    x_start(1)
    x_start(2)
    loop(x_traces, 5)

    def y_faces(a, values, send, up_buf, down_buf):
        down, up = traces(values)
        for kind in range(2):
            up_buf[kind, a, :, 0:cells_y, :] = down[kind]
            down_buf[kind, a, :, 1 : cells_y + 1, :] = up[kind]
            send[0, kind, a] = down[kind][:, 0:1, :]
            send[1, kind, a] = up[kind][:, cells_y - 1 : cells_y, :]

    def y_neighbours(a, received, up_buf, down_buf, part=slice(0, MODES)):
        for kind in range(2):
            up_buf[kind, a, part, cells_y : cells_y + 1, :] = received[0, kind, a, part]
            down_buf[kind, a, part, 0:1, :] = received[1, kind, a, part]
        return (
            [up_buf[kind, a, part, 1 : cells_y + 1, :] for kind in range(2)],
            [down_buf[kind, a, part, 0:cells_y, :] for kind in range(2)],
        )

    def z_faces(a, values, send):
        sides = traces(values)
        for side in range(2):
            for kind in range(2):
                send[side, kind, a] = sides[side][kind]

    def z_neighbours(a, send, received, part=slice(0, MODES)):
        def moved(side, kind, edge, amount):
            picked = jnp.where(lane == edge, received[side, kind, a, part], send[side, kind, a, part])
            return pltpu.roll(picked, amount, 2)

        return (
            [moved(0, kind, 0, cells_z - 1) for kind in range(2)],
            [moved(1, kind, cells_z - 1, 1) for kind in range(2)],
        )

    def y_traces(a):
        y_faces(a, [first[a, b] for b in range(MODES)], ys, y_up, y_down)

    loop(y_traces, 0, 2)
    y_over(start, 0)
    loop(y_traces, 2)
    y_over(start, 1)
    meet("hear")
    diagonal_over(start)
    x_start(3)
    y_over(start, 2)
    loop(lambda a: z_faces(a, [first[a, :, e] for e in range(MODES)], zs))
    over(start, 0, 2)

    def predict(a, b, part, total):
        right = rhs[a, b, part]
        modes = jnp.maximum(last_mode[part], jnp.maximum(a, b))
        scale = jnp.where(modes <= orders[None], table_ref[a, b, part], 0.0)
        return scale * (KEEP * right + STEP * (right - total)), scale * (-STEP)

    def x_own(b):
        values = [first[a, b] for a in range(MODES)]
        for a in range(MODES):
            acc[a, b] = own_row(a, values)

    def y_own(a):
        values = [first[a, b] for b in range(MODES)]
        for b in range(MODES):
            acc[a, b] += own_row(b, values)

    def z_own(a):
        values = [first[a, :, e] for e in range(MODES)]
        for e in range(MODES):
            acc[a, :, e] += own_row(e, values)

    def z_flux(a):
        term = face_terms(*z_neighbours(a, zs, zr))
        for e in range(MODES):
            acc[a, :, e] += term(e)

    def y_flux(a):
        term = face_terms(*y_neighbours(a, yr, y_up, y_down))
        for b in range(MODES):
            acc[a, b], coef[a, b] = predict(a, b, slice(0, MODES), acc[a, b] + term(b))

    def y_flux_part(part):
        def step(a):
            term = face_terms(*y_neighbours(a, yr, y_up, y_down, part))
            for b in range(MODES):
                acc[a, b, part], coef[a, b, part] = predict(a, b, part, acc[a, b, part] + term(b))

        loop(step, 2)

    loop(x_own)
    x_start(4)
    x_start(5)
    loop(y_own)
    x_start(6)
    loop(z_own)
    over(receive, 0, 2)
    loop(z_flux)
    forward(0)

    slots = iter(range(pads.shape[0]))

    def padded(value, at):
        slot = next(slots)
        pads[slot, at : at + cells_y, :] = value
        return pads[slot]

    near, border, layers = {}, {}, {}

    def gather_into(where_to, key, value):
        where_to[key] = where_to[key] + value if key in where_to else value

    def spread(values, shift, forced):
        centre, edge, x_low, x_high, y_low, y_high = {}, {}, {}, {}, {}, {}
        for b in range(2):
            line = [values[a, b, 0:2] for a in range(MODES)]
            down, up = traces(line)
            for a in range(2):
                own = own_row(a, line)
                below, above = one_sided(down, a, False), one_sided(up, a, True)
                for e in range(2):
                    centre[a, b, e] = forced[a, b, e] - own[e] if forced is not None else -own[e]
                    x_low[a, b, e] = -below[e]
                    x_high[a, b, e] = -above[e]
        for a in range(2):
            line = [values[a, b, 0:2] for b in range(MODES)]
            down, up = traces(line)
            for b in range(2):
                own = own_row(b, line)
                below, above = one_sided(down, b, False), one_sided(up, b, True)
                for e in range(2):
                    centre[a, b, e] = centre[a, b, e] - own[e]
                    y_low[a, b, e], y_high[a, b, e] = below[e], above[e]
            line = [values[a, 0:2, e] for e in range(MODES)]
            down, up = traces(line)
            for e in range(2):
                below = pltpu.roll(one_sided(down, e, False), cells_z - 1, 2)
                above = pltpu.roll(one_sided(up, e, True), 1, 2)
                inner = jnp.where(lane == cells_z - 1, 0.0, below) + jnp.where(lane == 0, 0.0, above)
                outer = jnp.where(lane == cells_z - 1, below, jnp.where(lane == 0, above, 0.0))
                own = own_row(e, line) + inner
                for b in range(2):
                    centre[a, b, e] = centre[a, b, e] - own[b]
                    edge[a, b, e] = -outer[b]
        resid = {
            key: padded(centre[key], 1) - padded(y_low[key], 0) - padded(y_high[key], 2)
            for key in OCTET
        }

        def masked(parts, degrees):
            return corners(
                {key: jnp.where(degrees >= max(key), parts[key], 0.0) for key in OCTET}
            )

        def settle_sums(tile_orders, low_orders, high_orders, edge_orders):
            cells, rim = masked(resid, tile_orders), masked(edge, edge_orders)
            low, high = masked(x_low, low_orders), masked(x_high, high_orders)
            for i, j, k in OCTET:
                moved = pltpu.roll(cells[i, j, k], 1, 0) if j else cells[i, j, k]
                gather_into(layers, (shift + i, k), moved)
                gather_into(border, (shift + i, j, k), rim[i, j, k])
                gather_into(near, (shift - 1 + i, j, k), low[i, j, k])
                gather_into(near, (shift + 1 + i, j, k), high[i, j, k])

        return settle_sums

    def ghost(values, side, other_orders):
        def put(a, b, high):
            part = slice(0, high)
            data = [xs[side, b, kind, part] for kind in range(2)]
            modes = jnp.maximum(last_mode[part], max(a, b))
            scale = jnp.where(modes <= other_orders[None], table_ref[a, b, part], 0.0) * (-STEP)
            values[a, b, part] = scale * one_sided(data, a, side == 1)

        for b in range(2):
            for a in range(MODES):
                put(a, b, MODES if a < 2 else 2)
        for b in range(2, MODES):
            for a in range(2):
                put(a, b, 2)

    for axis in range(3):
        over(receive, 1, axis)
    rows_of = (orders, order_x[0], order_x[1])
    lines_of = (order_y, order_xy.at[0], order_xy.at[1])
    sides_of = (order_z, order_xz.at[0], order_xz.at[1])

    def surroundings(at):
        order_tile[at, 1 : cells_y + 1] = rows_of[at]
        order_tile[at, 0:1] = lines_of[at][1]
        order_tile[at, cells_y + 1 : cells_y + 2] = lines_of[at][0]
        edge_orders = jnp.where(lane[0] == cells_z - 1, sides_of[at][1], sides_of[at][0])
        return order_tile[at], edge_orders

    ghost(ghost_up, 1, order_x[0])
    ghost(ghost_down, 0, order_x[1])
    y_over(receive, 0)
    loop(y_flux, 0, 2)
    y_over(receive, 1)
    y_flux_part(slice(0, 2))
    forward(1)
    tile_orders, edge_orders = surroundings(0)
    spread(acc, 0, rhs)(tile_orders, order_x[1], order_x[0], edge_orders)
    raised = spread(ghost_up, 1, None)
    lowered = spread(ghost_down, -1, None)
    diagonal_over(receive)

    @pl.when(collects)
    def _():
        for zz in range(nz - 1):
            pl.semaphore_signal(met.at[2], inc=1, device_id=(x, y, zz), device_id_type=MESH)

    forward(2)
    tile_orders, edge_orders = surroundings(1)
    raised(tile_orders, orders, order_far[0], edge_orders)
    tile_orders, edge_orders = surroundings(2)
    lowered(tile_orders, order_far[1], orders, edge_orders)

    row_lane = lane[0]
    sums = {}
    def carries_of(dx):
        for number, entry in enumerate(carries):
            if entry[4] == dx:
                start(entry, 24 + number, *carry_refs(*entry[4:]))

    for dx in (1, -1, 2, 3, -2, 0):
        pair = []
        for k in range(2):
            parts = [layers[dx, k]] if (dx, k) in layers else []
            parts += [padded(near[dx, j, k], 1 + j) for j in range(2)]
            pair.append(functools.reduce(lambda p, q: p + q, parts))
        moved = pltpu.roll(pair[1], 1, 1)
        if (dx, 0, 0) in border:
            outer = [padded(border[dx, 0, k], 1) + padded(border[dx, 1, k], 2) for k in range(2)]
            outer_moved = pltpu.roll(outer[1], 1, 1)
            inside = pair[0] + jnp.where(row_lane == 0, outer_moved, moved)
            beyond = jnp.where(row_lane == 0, moved, outer_moved) + outer[0]
        else:
            inside = pair[0] + jnp.where(row_lane == 0, 0.0, moved)
            beyond = jnp.where(row_lane == 0, moved, 0.0)
        for part, value in enumerate((inside, beyond)):
            if dx == 0:
                sums[part] = value[1 : cells_y + 1]
            out_mid[dx + 2, part] = value[1 : cells_y + 1]
            out_high[dx + 2, part] = value[cells_y + 1 : cells_y + 3]
            if -1 <= dx <= 2:
                out_low[dx + 1, part] = value[0:1]
        carries_of(dx)

    direct_slot = 24 + len(carries) + len(columns)

    @pl.when(jnp.logical_not(collects))
    def _():
        pl.semaphore_wait(met.at[2], 1)

    for number, entry in enumerate(direct):
        start(entry, direct_slot + number * nz + z, *direct_refs(*entry[4:], z))

    forward(3)
    y_over(receive, 2)
    y_flux_part(slice(2, MODES))

    def x_flux(b):
        x_receive(b)
        term = face_terms(
            [xr[0, b, kind] for kind in range(2)], [xr[1, b, kind] for kind in range(2)]
        )
        for a in range(MODES):
            smooth[a, b] = acc[a, b] + coef[a, b] * term(a)

    for stage, axis in ((0, 2), (1, 0), (1, 1), (1, 2)):
        over(finish, stage, axis)
    for part in range(3):
        y_over(finish, part)
    diagonal_over(finish)
    for b in range(MODES):
        for side in range(2):

            @pl.when(halos[side][1])
            def _():
                x_copy(side, b, halos[side][0]).wait_send()

    for b in range(RELAYED):
        for side in range(2):

            @pl.when(relays[side][3])
            def _():
                from_relay(side, b, relays[side][4]).wait_send()

    loop(x_flux, RELAYED)
    loop(x_flux, 0, RELAYED)

    for number, entry in enumerate(carries):
        receive(entry, 24 + number, *carry_refs(*entry[4:]))

    for part in range(2):
        value = sums[part]
        for dx in REACH:
            if dx:
                value = value + in_mid[dx + 2, part]
        high = functools.reduce(lambda p, q: p + q, [in_high[at, part] for at in range(6)])
        low = functools.reduce(lambda p, q: p + q, [in_low[at, part] for at in range(4)])
        column[pl.ds(z, 1), part] = value[None]
        column[pl.ds(z, 1), part, 0:2] += high[None]
        column[pl.ds(z, 1), part, cells_y - 1 : cells_y] += low[None]

    def gather(number, arriving):
        entry = columns[number]
        at = entry[4] if arriving else z
        return remote(column.at[at], column.at[at], 24 + len(carries) + number, entry[0])

    def columns_over(action, arriving):
        for number, entry in enumerate(columns):
            to_collector = collects if arriving else entry[0][2] == nz - 1

            @pl.when((x > 0) & jnp.logical_not(to_collector))
            def _(number=number):
                action(number)

    columns_over(lambda number: gather(number, False).start(), False)
    for number, entry in enumerate(carries):
        finish(entry, 24 + number, *carry_refs(*entry[4:]))
    for number, entry in enumerate(direct):
        finish(entry, direct_slot + number * nz + z, *direct_refs(*entry[4:], z))
    @pl.when(collects)
    def _():
        for number, (to, _, back, ok_from, dx, dy) in enumerate(direct):
            for zz in range(nz - 1):
                slot = direct_slot + number * nz + zz
                receive((to, None, back, ok_from), slot, *direct_refs(dx, dy, zz))
        for zz in range(nz - 1):
            for part in range(2):
                column[zz, part] = functools.reduce(
                    lambda p, q: p + q, [far_mid[at, zz, part] for at in range(6)]
                )
                column[zz, part, 0:2] += functools.reduce(
                    lambda p, q: p + q, [far_high[at, zz, part] for at in range(6)]
                )
                column[zz, part, cells_y - 1 : cells_y] += functools.reduce(
                    lambda p, q: p + q, [far_low[at, zz, part] for at in range(4)]
                )

    columns_over(lambda number: gather(number, True).wait_recv(), True)
    columns_over(lambda number: gather(number, False).wait_send(), False)

    row = lax.broadcasted_iota(jnp.int32, (cells_y, cells_z), 0)
    spot = lax.broadcasted_iota(jnp.int32, (cells_y, cells_z), 1)
    for zz in range(nz):
        total = column[zz, 0]
        if zz > 0:
            total = total + jnp.where(spot < 2, column[zz - 1, 1], 0.0)
        if zz < nz - 1:
            total = total + jnp.where(spot == cells_z - 1, column[zz + 1, 1], 0.0)
        inside = (x > 0) & ((row > 0) | (y > 0))
        if zz == 0:
            inside = inside & (spot > 0)
        coarse_ref[0, :, zz * cells_z : (zz + 1) * cells_z] = jnp.where(inside, total, 0.0)


def drain(smooth, coarse, smooth_hbm, coarse_hbm, sem):
    copies = [
        pltpu.make_async_copy(smooth.at[a], smooth_hbm.at[a], sem.at[a]) for a in range(MODES)
    ]
    copies.append(pltpu.make_async_copy(coarse, coarse_hbm, sem.at[MODES]))
    for copy in copies:
        copy.start()
    for copy in copies:
        copy.wait()


def per_device(sizes, rhs, orders):
    _, cells_y, cells_z = orders.shape
    nz = sizes[2]
    table = jnp.asarray(
        np.broadcast_to(
            (1.0 / (DIAGONAL * THETA))[:, :, :, None, None], DIAGONAL.shape + (1, cells_z)
        ),
        jnp.float32,
    )
    field = rhs.reshape(rhs.shape[:3] + rhs.shape[4:])
    cells = (cells_y, cells_z)
    rows = 8 * ((cells_y + 8) // 8)
    tall = 8 * ((cells_y + 10) // 8)
    line = (2, 2, MODES, MODES)

    def buf(*shape):
        return pltpu.VMEM(shape, jnp.float32)

    def whole(*shape):
        return pltpu.VMEM(shape, jnp.int32)

    slots = 24 + len(CARRIES) + nz - 1 + (len(CARRIES) + 1) * nz
    coarse_shape = (1, cells_y, nz * cells_z)
    vmem = pl.BlockSpec(memory_space=pltpu.VMEM)
    hbm = pl.BlockSpec(memory_space=pltpu.HBM)
    smoothed, coarse = pl.pallas_call(
        functools.partial(kernel, sizes, cells_y, cells_z),
        out_shape=(pltpu.VMEM(field.shape, jnp.float32), pltpu.VMEM(coarse_shape, jnp.float32)),
        in_specs=[hbm, hbm, hbm],
        out_specs=(vmem, vmem),
        scratch_shapes=[buf(*field.shape)] * 6
        + [
            whole(*orders.shape), buf(*table.shape),
            buf(2, MODES, 2, MODES, *cells), buf(2, MODES, 2, MODES, *cells),
            buf(*line, 1, cells_z), buf(*line, 1, cells_z),
            buf(*line, *cells), buf(*line, *cells),
            buf(2, MODES, MODES, rows, cells_z), buf(2, MODES, MODES, rows, cells_z),
            whole(2, 1, cells_z), whole(2, *cells), whole(2, 1, cells_z), whole(2, *cells),
            whole(2, 2, 1, cells_z), whole(2, 2, *cells), whole(2, *cells), whole(3, tall, cells_z),
            buf(112, tall, cells_z),
            buf(6, 2, *cells), buf(6, 2, 2, cells_z), buf(4, 2, 1, cells_z),
            buf(6, 2, *cells), buf(6, 2, 2, cells_z), buf(4, 2, 1, cells_z),
            buf(6, nz, 2, *cells), buf(6, nz, 2, 2, cells_z), buf(4, nz, 2, 1, cells_z),
            buf(nz, 2, *cells),
            buf(2, RELAYED, 2, MODES, *cells),
            pltpu.SemaphoreType.DMA((MODES + 2,)),
            pltpu.SemaphoreType.DMA((slots,)),
            pltpu.SemaphoreType.DMA((slots,)),
            pltpu.SemaphoreType.DMA((2, MODES)),
            pltpu.SemaphoreType.DMA((2, MODES)),
            pltpu.SemaphoreType.DMA((2, 3)),
            pltpu.SemaphoreType.DMA((2, 3)),
            pltpu.SemaphoreType.DMA((2, RELAYED)),
            pltpu.SemaphoreType.DMA((2, RELAYED)),
            pltpu.SemaphoreType.REGULAR((3,)),
        ],
        compiler_params=pltpu.CompilerParams(collective_id=0, has_side_effects=True),
        name="smoother",
    )(field, orders, table)
    smoothed, coarse = pl.pallas_call(
        drain,
        out_shape=(
            jax.ShapeDtypeStruct(field.shape, jnp.float32),
            jax.ShapeDtypeStruct(coarse_shape, jnp.float32),
        ),
        in_specs=[vmem, vmem],
        out_specs=(hbm, hbm),
        scratch_shapes=[pltpu.SemaphoreType.DMA((MODES + 1,))],
        name="drain",
    )(
        pltpu.with_memory_space_constraint(smoothed, pltpu.VMEM),
        pltpu.with_memory_space_constraint(coarse, pltpu.VMEM),
    )
    return smoothed.reshape(rhs.shape), coarse


def solution(mesh):
    sizes = tuple(mesh.shape[axis] for axis in ("gx", "gy", "gz"))
    return jax.shard_map(
        functools.partial(per_device, sizes),
        mesh=mesh,
        in_specs=(P(None, None, None, "gx", "gy", "gz"), P("gx", "gy", "gz")),
        out_specs=(P(None, None, None, "gx", "gy", "gz"), P("gx", "gy", None)),
        check_vma=False,
    )
```

```python
import functools

import jax
import jax.numpy as jnp
import numpy as np
from jax import lax
from jax.experimental import pallas as pl
from jax.experimental.pallas import tpu as pltpu
from jax.sharding import PartitionSpec as P

PENALTY = 49.0
EIGEN_HIGH = 2.4
EIGEN_LOW = 0.24
MODES = 7
MESH = pl.DeviceIdType.MESH


def tables():
    degree = np.arange(MODES)
    normed = np.sqrt((2.0 * degree + 1.0) / 2.0)
    smaller = np.minimum(degree[:, None], degree[None, :])
    parity = (degree[:, None] + degree[None, :]) % 2 == 0
    stiffness = np.where(parity, normed[:, None] * normed[None, :] * smaller * (smaller + 1), 0.0)
    signs = (-1.0) ** degree
    slope = normed * degree * (degree + 1) / 2.0
    low, low_slope = normed * signs, -slope * signs
    own = stiffness + np.outer(normed, PENALTY * normed - 0.5 * slope) - 0.5 * np.outer(slope, normed)
    own = own + np.outer(low, PENALTY * low + 0.5 * low_slope) + 0.5 * np.outer(low_slope, low)
    one_axis = normed * normed * degree * (degree + 1) + 2.0 * (
        PENALTY * normed * normed - normed * slope
    )
    diagonal = (
        one_axis[:, None, None] + one_axis[None, :, None] + one_axis[None, None, :]
    ) / PENALTY
    return (
        own / PENALTY,
        0.5 * slope - PENALTY * normed,
        0.5 * normed,
        normed / PENALTY,
        slope / PENALTY,
        diagonal,
    )


OWN, JUMP, HALF, VALUE, SLOPE, DIAGONAL = tables()
THETA = 0.5 * (EIGEN_HIGH + EIGEN_LOW)
DELTA = 0.5 * (EIGEN_HIGH - EIGEN_LOW)
RHO_FIRST = DELTA / THETA
RHO_SECOND = 1.0 / (2.0 * THETA / DELTA - RHO_FIRST)
KEEP = 1.0 + RHO_SECOND * RHO_FIRST
STEP = 2.0 * RHO_SECOND / DELTA * THETA


def combine(weights, values):
    total = None
    for weight, value in zip(weights, values):
        term = value * float(weight)
        total = term if total is None else total + term
    return total


def traces(values):
    even, odd = values[0::2], values[1::2]
    jump_even, jump_odd = combine(JUMP[0::2], even), combine(JUMP[1::2], odd)
    half_even, half_odd = combine(HALF[0::2], even), combine(HALF[1::2], odd)
    down = (jump_even - jump_odd, half_even - half_odd)
    up = (jump_even + jump_odd, half_even + half_odd)
    return down, up


def own_row(row, values):
    start = row % 2
    return combine(OWN[row, start::2], values[start::2])


def face_terms(from_up, from_down):
    both = (from_up[0] + from_down[0], from_up[1] + from_down[1])
    apart = (from_up[0] - from_down[0], from_up[1] - from_down[1])

    def term(mode):
        pair = both if mode % 2 == 0 else apart
        if mode == 0:
            return pair[0] * float(VALUE[0])
        return pair[0] * float(VALUE[mode]) + pair[1] * float(SLOPE[mode])

    return term


def vertex_pair(zero, one):
    flat, tilt = np.sqrt(0.5) * zero, (np.sqrt(1.5) / 3.0) * one
    return flat - tilt, flat + tilt


def one_sided(data, mode, from_below):
    if mode == 0:
        return data[0] * float(VALUE[0])
    sign = -1.0 if from_below and mode % 2 else 1.0
    return data[0] * (sign * float(VALUE[mode])) + data[1] * (sign * float(SLOPE[mode]))


def corners(values):
    for axis in range(3):
        done = {}
        for key in values:
            if key[axis] == 0:
                other = tuple(1 if n == axis else key[n] for n in range(3))
                done[key], done[other] = vertex_pair(values[key], values[other])
        values = done
    return values


OCTET = [(a, b, e) for a in range(2) for b in range(2) for e in range(2)]
RELAYED = 4
SIGNS = (1, -1)
DIAGONALS = (
    [(dx, dy, 0) for dx in SIGNS for dy in SIGNS]
    + [(dx, 0, dz) for dx in SIGNS for dz in SIGNS]
    + [(2 * dx, 0, 0) for dx in SIGNS]
)
Y_PARTS = ((slice(0, 2), slice(0, MODES)), (slice(2, MODES), slice(0, 2)), (slice(2, MODES), slice(2, MODES)))
REACH = range(-2, 4)
CARRIES = (
    (1, 1), (-1, 1), (1, -1), (-1, -1), (3, 1), (2, 1), (-2, 1), (2, -1),
    (3, 0), (2, 0), (-2, 0), (1, 0), (-1, 0), (0, 1), (0, -1),
)


def kernel(
    sizes, cells_y, cells_z, rhs_hbm, orders_hbm, table_hbm, smooth, coarse_ref,
    rhs, first, acc, coef, ghost_up, ghost_down, orders_ref, table_ref,
    xs, xr, ys, yr, zs, zr, y_up, y_down,
    order_line, order_x, order_y, order_z, order_xy, order_xz, order_far, order_tile, pads,
    out_mid, out_high, out_low, in_mid, in_high, in_low, far_mid, far_high, far_low, column,
    relay, local_sem, send_sem, recv_sem, x_send, x_recv, y_send, y_recv, relay_in, relay_out, met,
):
    nx, ny, nz = sizes
    tall = pads.shape[1]
    x, y, z = lax.axis_index("gx"), lax.axis_index("gy"), lax.axis_index("gz")
    barrier = pltpu.get_barrier_semaphore()

    def neighbour(axis, sign):
        here = (x, y, z)[axis]
        to = [x, y, z]
        to[axis] = here + sign
        back = [x, y, z]
        back[axis] = here - sign
        below, above = here > 0, here < sizes[axis] - 1
        return (tuple(to), below if sign < 0 else above, tuple(back), above if sign < 0 else below)

    halos = [neighbour(axis, sign) for axis in range(3) for sign in (-1, 1)]
    always = x >= 0

    def offset(dx, dy):
        ok_to = (x + dx > 0) & (x + dx < nx)
        ok_from = (x > 0) & (x - dx >= 0) & (x - dx < nx)
        if dy > 0:
            ok_to, ok_from = ok_to & (y + dy < ny), ok_from & (y >= dy)
        if dy < 0:
            ok_to, ok_from = ok_to & (y + dy >= 0), ok_from & (y - dy < ny)
        return ((x + dx, y + dy, z), ok_to, (x - dx, y - dy, z), ok_from)

    carries = [offset(dx, dy) + (dx, dy) for dx, dy in CARRIES]
    collects = z == nz - 1
    direct = []
    for dx, dy in CARRIES + ((0, 0),):
        to, ok_to, back, ok_from = offset(dx, dy)
        to = to[:2] + (nz - 1,)
        direct.append((to, ok_to & jnp.logical_not(collects), back, ok_from, dx, dy))
    columns = []
    for r in range(1, nz):
        source = lax.rem(z - r + nz, nz)
        columns.append(((x, y, lax.rem(z + r, nz)), always, (x, y, source), always, source))

    def diagonal(offset):
        here = (x, y, z)
        to = tuple(h + d for h, d in zip(here, offset))
        back = tuple(h - d for h, d in zip(here, offset))
        ok_to, ok_from = always, always
        for axis, d in enumerate(offset):
            low, high = here[axis] >= abs(d), here[axis] + abs(d) < sizes[axis]
            if d > 0:
                ok_to, ok_from = ok_to & high, ok_from & low
            elif d < 0:
                ok_to, ok_from = ok_to & low, ok_from & high
        return (to, ok_to, back, ok_from)

    diagonals = [diagonal(offset) for offset in DIAGONALS]

    def diagonal_refs(offset):
        dx, dy, dz = offset
        if dy:
            return order_line.at[0 if dy < 0 else 1], order_xy.at[(1 + dx) // 2, (1 + dy) // 2]
        if dz:
            return orders_ref.at[0], order_xz.at[(1 + dx) // 2, (1 + dz) // 2]
        return orders_ref.at[0], order_far.at[(2 + dx) // 4]

    odd = lax.rem(x, 2) == 1
    even = jnp.logical_not(odd)
    relays = (
        ((x - 2, y, z), even & (x >= 2), (x + 2, y, z), even & (x + 2 < nx), (x + 1, y, z)),
        ((x + 2, y, z), odd & (x + 2 < nx), (x - 2, y, z), odd & (x >= 3), (x - 1, y, z)),
    )

    expected = jnp.int32(0)
    for entry in halos[:4] + columns + list(relays):
        to, ok_to, back, ok_from = entry[:4]

        @pl.when(ok_from)
        def _(back=back):
            pl.semaphore_signal(barrier, inc=1, device_id=back, device_id_type=MESH)

        expected = expected + jnp.where(ok_to, 1, 0).astype(jnp.int32)

    loads = [
        pltpu.make_async_copy(orders_hbm, orders_ref, local_sem.at[MODES]),
        pltpu.make_async_copy(table_hbm, table_ref, local_sem.at[MODES + 1]),
    ]
    for copy in loads:
        copy.start()

    def rhs_load(b):
        return pltpu.make_async_copy(rhs_hbm.at[:, b], rhs.at[:, b], local_sem.at[b])

    for b in range(MODES):
        rhs_load(b).start()

    def remote(src, dst, slot, to):
        if isinstance(slot, tuple):
            return pltpu.make_async_remote_copy(
                src_ref=src, dst_ref=dst, send_sem=y_send.at[slot], recv_sem=y_recv.at[slot],
                device_id=to, device_id_type=MESH,
            )
        return pltpu.make_async_remote_copy(
            src_ref=src, dst_ref=dst, send_sem=send_sem.at[slot], recv_sem=recv_sem.at[slot],
            device_id=to, device_id_type=MESH,
        )

    def start(entry, slot, src, dst):
        to, ok_to = entry[:2]

        @pl.when(ok_to)
        def _():
            remote(src, dst, slot, to).start()

    def receive(entry, slot, src, dst):
        to, _, _, ok_from = entry[:4]

        @pl.when(ok_from)
        def _():
            remote(src, dst, slot, to).wait_recv()

    def finish(entry, slot, src, dst):
        to, ok_to = entry[:2]

        @pl.when(ok_to)
        def _():
            remote(src, dst, slot, to).wait_send()

    stages = (
        ((xs, xr), (ys, yr), (zs, zr)),
        ((orders_ref, order_x), (order_line, order_y), (orders_ref, order_z)),
    )

    def over(action, stage, axis):
        src, dst = stages[stage][axis]
        for side in range(2):
            index = 2 * axis + side
            action(halos[index], 6 * stage + index, src.at[0 if src is orders_ref else side], dst.at[side])

    for stage, empty in ((0, 0.0), (1, -1)):
        for axis in range(3):
            for side in range(2):
                dst = stages[stage][axis][1]

                @pl.when(jnp.logical_not(halos[2 * axis + side][3]))
                def _(dst=dst, side=side, empty=empty):
                    dst[side] = jnp.full(dst.shape[1:], empty, dst.dtype)

    pads[...] = jnp.zeros(pads.shape, jnp.float32)
    order_tile[...] = jnp.full(order_tile.shape, -1, jnp.int32)
    for offset, entry in zip(DIAGONALS, diagonals):

        @pl.when(jnp.logical_not(entry[3]))
        def _(offset=offset):
            dst = diagonal_refs(offset)[1]
            dst[...] = jnp.full(dst.shape, -1, jnp.int32)

    targets = {0: (out_mid, in_mid), 1: (out_high, in_high), -1: (out_low, in_low)}

    def carry_refs(dx, dy):
        src, dst = targets[dy]
        at = dx + 1 if dy < 0 else dx + 2
        return src.at[at], dst.at[at]

    far_of = {0: far_mid, 1: far_high, -1: far_low}

    def direct_refs(dx, dy, source):
        at = dx + 1 if dy < 0 else dx + 2
        return targets[dy][0].at[at], far_of[dy].at[at, source]

    for _, _, _, ok_from, dx, dy in direct:

        @pl.when(jnp.logical_not(ok_from))
        def _(dx=dx, dy=dy):
            dst = far_of[dy].at[dx + 1 if dy < 0 else dx + 2]
            dst[...] = jnp.zeros(dst.shape, jnp.float32)

    for _, _, _, ok_from, dx, dy in carries:

        @pl.when(jnp.logical_not(ok_from))
        def _(dx=dx, dy=dy):
            dst = carry_refs(dx, dy)[1]
            dst[...] = jnp.zeros(dst.shape, jnp.float32)

    for copy in loads:
        copy.wait()
    orders = orders_ref[0]
    order_line[0] = orders[0:1]
    order_line[1] = orders[cells_y - 1 : cells_y]
    tile = (MODES, cells_y, cells_z)
    last_mode = lax.broadcasted_iota(jnp.int32, tile, 0)
    lane = lax.broadcasted_iota(jnp.int32, (1, 1, cells_z), 2)

    def active(a, b):
        return jnp.maximum(jnp.maximum(a, b), last_mode) <= orders[None]

    def loop(body, low=0, high=MODES):
        def step(index, carry):
            body(index)
            return carry

        lax.fori_loop(low, high, step, 0)

    def x_copy(side, b, to):
        return pltpu.make_async_remote_copy(
            src_ref=xs.at[side, b], dst_ref=xr.at[side, b],
            send_sem=x_send.at[side, b], recv_sem=x_recv.at[side, b],
            device_id=to, device_id_type=MESH,
        )

    def to_relay(side, b, to):
        return pltpu.make_async_remote_copy(
            src_ref=xs.at[side, b], dst_ref=relay.at[side, b],
            send_sem=x_send.at[side, b], recv_sem=relay_in.at[side, b],
            device_id=to, device_id_type=MESH,
        )

    def from_relay(side, b, to):
        return pltpu.make_async_remote_copy(
            src_ref=relay.at[side, b], dst_ref=xr.at[side, b],
            send_sem=relay_out.at[side, b], recv_sem=x_recv.at[side, b],
            device_id=to, device_id_type=MESH,
        )

    def forward(number):
        for side in range(2):
            back, relaying, target = relays[side][2:]

            @pl.when(relaying)
            def _():
                to_relay(side, number, target).wait_recv()
                from_relay(side, number, target).start()

    def x_receive(number):
        for side in range(2):

            @pl.when(halos[side][3])
            def _():
                x_copy(side, number, halos[side][0]).wait_recv()

    def x_traces(b):
        rhs_load(b).wait()
        values = []
        for a in range(MODES):
            value = jnp.where(active(a, b), table_ref[a, b] * rhs[a, b], 0.0)
            first[a, b] = value
            values.append(value)
        sides = traces(values)
        for side in range(2):
            for kind in range(2):
                xs[side, b, kind] = sides[side][kind]

    def x_start(b):
        for side in range(2):
            to, ok_to = halos[side][:2]
            via, used = relays[side][:2]
            if b < RELAYED:

                @pl.when(used)
                def _():
                    to_relay(side, b, via).start()

                ok_to = ok_to & jnp.logical_not(used)

            @pl.when(ok_to)
            def _():
                x_copy(side, b, to).start()

    def diagonal_over(action):
        for number, (offset, entry) in enumerate(zip(DIAGONALS, diagonals)):
            action(entry, 14 + number, *diagonal_refs(offset))

    def y_over(action, part):
        modes = Y_PARTS[part]
        for side in range(2):
            at = (side, slice(None)) + modes
            action(halos[2 + side], (side, part), ys.at[at], yr.at[at])

    def meet(action):
        for side in range(2):
            to, ok_to, _, ok_from = halos[side]

            @pl.when(ok_to if action == "tell" else ok_from)
            def _():
                if action == "tell":
                    pl.semaphore_signal(met.at[side], inc=1, device_id=to, device_id_type=MESH)
                else:
                    pl.semaphore_wait(met.at[side], 1)

    loop(x_traces, 0, 5)
    pl.semaphore_wait(barrier, expected)
    meet("tell")
    over(start, 1, 0)
    over(start, 1, 1)
    over(start, 1, 2)
    x_start(0)
    x_start(1)
    x_start(2)
    loop(x_traces, 5)

    def y_faces(a, values, send, up_buf, down_buf):
        down, up = traces(values)
        for kind in range(2):
            up_buf[kind, a, :, 0:cells_y, :] = down[kind]
            down_buf[kind, a, :, 1 : cells_y + 1, :] = up[kind]
            send[0, kind, a] = down[kind][:, 0:1, :]
            send[1, kind, a] = up[kind][:, cells_y - 1 : cells_y, :]

    def y_neighbours(a, received, up_buf, down_buf, part=slice(0, MODES)):
        for kind in range(2):
            up_buf[kind, a, part, cells_y : cells_y + 1, :] = received[0, kind, a, part]
            down_buf[kind, a, part, 0:1, :] = received[1, kind, a, part]
        return (
            [up_buf[kind, a, part, 1 : cells_y + 1, :] for kind in range(2)],
            [down_buf[kind, a, part, 0:cells_y, :] for kind in range(2)],
        )

    def z_faces(a, values, send):
        sides = traces(values)
        for side in range(2):
            for kind in range(2):
                send[side, kind, a] = sides[side][kind]

    def z_neighbours(a, send, received, part=slice(0, MODES)):
        def moved(side, kind, edge, amount):
            picked = jnp.where(lane == edge, received[side, kind, a, part], send[side, kind, a, part])
            return pltpu.roll(picked, amount, 2)

        return (
            [moved(0, kind, 0, cells_z - 1) for kind in range(2)],
            [moved(1, kind, cells_z - 1, 1) for kind in range(2)],
        )

    def y_traces(a):
        y_faces(a, [first[a, b] for b in range(MODES)], ys, y_up, y_down)

    loop(y_traces, 0, 2)
    y_over(start, 0)
    loop(y_traces, 2)
    y_over(start, 1)
    meet("hear")
    diagonal_over(start)
    x_start(3)
    y_over(start, 2)
    loop(lambda a: z_faces(a, [first[a, :, e] for e in range(MODES)], zs))
    over(start, 0, 2)

    def predict(a, b, part, total):
        right = rhs[a, b, part]
        modes = jnp.maximum(last_mode[part], jnp.maximum(a, b))
        scale = jnp.where(modes <= orders[None], table_ref[a, b, part], 0.0)
        return scale * (KEEP * right + STEP * (right - total)), scale * (-STEP)

    def x_own(b):
        values = [first[a, b] for a in range(MODES)]
        for a in range(MODES):
            acc[a, b] = own_row(a, values)

    def y_own(a):
        values = [first[a, b] for b in range(MODES)]
        for b in range(MODES):
            acc[a, b] += own_row(b, values)

    def z_own(a):
        values = [first[a, :, e] for e in range(MODES)]
        for e in range(MODES):
            acc[a, :, e] += own_row(e, values)

    def z_flux(a):
        term = face_terms(*z_neighbours(a, zs, zr))
        for e in range(MODES):
            acc[a, :, e] += term(e)

    def y_flux(a):
        term = face_terms(*y_neighbours(a, yr, y_up, y_down))
        for b in range(MODES):
            acc[a, b], coef[a, b] = predict(a, b, slice(0, MODES), acc[a, b] + term(b))

    def y_flux_part(part):
        def step(a):
            term = face_terms(*y_neighbours(a, yr, y_up, y_down, part))
            for b in range(MODES):
                acc[a, b, part], coef[a, b, part] = predict(a, b, part, acc[a, b, part] + term(b))

        loop(step, 2)

    loop(x_own)
    x_start(4)
    x_start(5)
    loop(y_own)
    x_start(6)
    loop(z_own)
    over(receive, 0, 2)
    loop(z_flux)
    forward(0)

    slots = iter(range(pads.shape[0]))

    def padded(value, at):
        slot = next(slots)
        pads[slot, at : at + cells_y, :] = value
        return pads[slot]

    near, border, layers = {}, {}, {}

    def gather_into(where_to, key, value):
        where_to[key] = where_to[key] + value if key in where_to else value

    def spread(values, shift, forced):
        centre, edge, x_low, x_high, y_low, y_high = {}, {}, {}, {}, {}, {}
        for b in range(2):
            line = [values[a, b, 0:2] for a in range(MODES)]
            down, up = traces(line)
            for a in range(2):
                own = own_row(a, line)
                below, above = one_sided(down, a, False), one_sided(up, a, True)
                for e in range(2):
                    centre[a, b, e] = forced[a, b, e] - own[e] if forced is not None else -own[e]
                    x_low[a, b, e] = -below[e]
                    x_high[a, b, e] = -above[e]
        for a in range(2):
            line = [values[a, b, 0:2] for b in range(MODES)]
            down, up = traces(line)
            for b in range(2):
                own = own_row(b, line)
                below, above = one_sided(down, b, False), one_sided(up, b, True)
                for e in range(2):
                    centre[a, b, e] = centre[a, b, e] - own[e]
                    y_low[a, b, e], y_high[a, b, e] = below[e], above[e]
            line = [values[a, 0:2, e] for e in range(MODES)]
            down, up = traces(line)
            for e in range(2):
                below = pltpu.roll(one_sided(down, e, False), cells_z - 1, 2)
                above = pltpu.roll(one_sided(up, e, True), 1, 2)
                inner = jnp.where(lane == cells_z - 1, 0.0, below) + jnp.where(lane == 0, 0.0, above)
                outer = jnp.where(lane == cells_z - 1, below, jnp.where(lane == 0, above, 0.0))
                own = own_row(e, line) + inner
                for b in range(2):
                    centre[a, b, e] = centre[a, b, e] - own[b]
                    edge[a, b, e] = -outer[b]
        resid = {
            key: padded(centre[key], 1) - padded(y_low[key], 0) - padded(y_high[key], 2)
            for key in OCTET
        }

        def masked(parts, degrees):
            return corners(
                {key: jnp.where(degrees >= max(key), parts[key], 0.0) for key in OCTET}
            )

        def settle_sums(tile_orders, low_orders, high_orders, edge_orders):
            cells, rim = masked(resid, tile_orders), masked(edge, edge_orders)
            low, high = masked(x_low, low_orders), masked(x_high, high_orders)
            for i, j, k in OCTET:
                moved = pltpu.roll(cells[i, j, k], 1, 0) if j else cells[i, j, k]
                gather_into(layers, (shift + i, k), moved)
                gather_into(border, (shift + i, j, k), rim[i, j, k])
                gather_into(near, (shift - 1 + i, j, k), low[i, j, k])
                gather_into(near, (shift + 1 + i, j, k), high[i, j, k])

        return settle_sums

    def ghost(values, side, other_orders):
        def put(a, b, high):
            part = slice(0, high)
            data = [xs[side, b, kind, part] for kind in range(2)]
            modes = jnp.maximum(last_mode[part], max(a, b))
            scale = jnp.where(modes <= other_orders[None], table_ref[a, b, part], 0.0) * (-STEP)
            values[a, b, part] = scale * one_sided(data, a, side == 1)

        for b in range(2):
            for a in range(MODES):
                put(a, b, MODES if a < 2 else 2)
        for b in range(2, MODES):
            for a in range(2):
                put(a, b, 2)

    for axis in range(3):
        over(receive, 1, axis)
    rows_of = (orders, order_x[0], order_x[1])
    lines_of = (order_y, order_xy.at[0], order_xy.at[1])
    sides_of = (order_z, order_xz.at[0], order_xz.at[1])

    def surroundings(at):
        order_tile[at, 1 : cells_y + 1] = rows_of[at]
        order_tile[at, 0:1] = lines_of[at][1]
        order_tile[at, cells_y + 1 : cells_y + 2] = lines_of[at][0]
        edge_orders = jnp.where(lane[0] == cells_z - 1, sides_of[at][1], sides_of[at][0])
        return order_tile[at], edge_orders

    ghost(ghost_up, 1, order_x[0])
    ghost(ghost_down, 0, order_x[1])
    y_over(receive, 0)
    loop(y_flux, 0, 2)
    y_over(receive, 1)
    y_flux_part(slice(0, 2))
    forward(1)
    tile_orders, edge_orders = surroundings(0)
    spread(acc, 0, rhs)(tile_orders, order_x[1], order_x[0], edge_orders)
    raised = spread(ghost_up, 1, None)
    lowered = spread(ghost_down, -1, None)
    diagonal_over(receive)

    @pl.when(collects)
    def _():
        for zz in range(nz - 1):
            pl.semaphore_signal(met.at[2], inc=1, device_id=(x, y, zz), device_id_type=MESH)

    forward(2)
    tile_orders, edge_orders = surroundings(1)
    raised(tile_orders, orders, order_far[0], edge_orders)
    tile_orders, edge_orders = surroundings(2)
    lowered(tile_orders, order_far[1], orders, edge_orders)

    row_lane = lane[0]
    sums = {}
    direct_slot = 24 + len(carries) + len(columns)

    @pl.when(jnp.logical_not(collects))
    def _():
        pl.semaphore_wait(met.at[2], 1)

    def direct_of(dx):
        for number, entry in enumerate(direct):
            if entry[4] == dx:
                start(entry, direct_slot + number * nz + z, *direct_refs(*entry[4:], z))

    def carries_of(dx):
        for number, entry in enumerate(carries):
            if entry[4] == dx:
                start(entry, 24 + number, *carry_refs(*entry[4:]))

    for dx in (1, -1, 2, 3, -2, 0):
        pair = []
        for k in range(2):
            parts = [layers[dx, k]] if (dx, k) in layers else []
            parts += [padded(near[dx, j, k], 1 + j) for j in range(2)]
            pair.append(functools.reduce(lambda p, q: p + q, parts))
        moved = pltpu.roll(pair[1], 1, 1)
        if (dx, 0, 0) in border:
            outer = [padded(border[dx, 0, k], 1) + padded(border[dx, 1, k], 2) for k in range(2)]
            outer_moved = pltpu.roll(outer[1], 1, 1)
            inside = pair[0] + jnp.where(row_lane == 0, outer_moved, moved)
            beyond = jnp.where(row_lane == 0, moved, outer_moved) + outer[0]
        else:
            inside = pair[0] + jnp.where(row_lane == 0, 0.0, moved)
            beyond = jnp.where(row_lane == 0, moved, 0.0)
        for part, value in enumerate((inside, beyond)):
            if dx == 0:
                sums[part] = value[1 : cells_y + 1]
            out_mid[dx + 2, part] = value[1 : cells_y + 1]
            out_high[dx + 2, part] = value[cells_y + 1 : cells_y + 3]
            if -1 <= dx <= 2:
                out_low[dx + 1, part] = value[0:1]
        direct_of(dx)
        carries_of(dx)

    forward(3)
    y_over(receive, 2)
    y_flux_part(slice(2, MODES))

    def x_flux(b):
        x_receive(b)
        term = face_terms(
            [xr[0, b, kind] for kind in range(2)], [xr[1, b, kind] for kind in range(2)]
        )
        for a in range(MODES):
            smooth[a, b] = acc[a, b] + coef[a, b] * term(a)

    for stage, axis in ((0, 2), (1, 0), (1, 1), (1, 2)):
        over(finish, stage, axis)
    for part in range(3):
        y_over(finish, part)
    diagonal_over(finish)
    for b in range(MODES):
        for side in range(2):

            @pl.when(halos[side][1])
            def _():
                x_copy(side, b, halos[side][0]).wait_send()

    for b in range(RELAYED):
        for side in range(2):

            @pl.when(relays[side][3])
            def _():
                from_relay(side, b, relays[side][4]).wait_send()

    loop(x_flux, RELAYED)
    loop(x_flux, 0, RELAYED)

    for number, entry in enumerate(carries):
        receive(entry, 24 + number, *carry_refs(*entry[4:]))

    for part in range(2):
        value = sums[part]
        for dx in REACH:
            if dx:
                value = value + in_mid[dx + 2, part]
        high = functools.reduce(lambda p, q: p + q, [in_high[at, part] for at in range(6)])
        low = functools.reduce(lambda p, q: p + q, [in_low[at, part] for at in range(4)])
        column[pl.ds(z, 1), part] = value[None]
        column[pl.ds(z, 1), part, 0:2] += high[None]
        column[pl.ds(z, 1), part, cells_y - 1 : cells_y] += low[None]

    def gather(number, arriving):
        entry = columns[number]
        at = entry[4] if arriving else z
        return remote(column.at[at], column.at[at], 24 + len(carries) + number, entry[0])

    def columns_over(action, arriving):
        for number, entry in enumerate(columns):
            to_collector = collects if arriving else entry[0][2] == nz - 1

            @pl.when((x > 0) & jnp.logical_not(to_collector))
            def _(number=number):
                action(number)

    columns_over(lambda number: gather(number, False).start(), False)
    for number, entry in enumerate(carries):
        finish(entry, 24 + number, *carry_refs(*entry[4:]))
    for number, entry in enumerate(direct):
        finish(entry, direct_slot + number * nz + z, *direct_refs(*entry[4:], z))
    @pl.when(collects)
    def _():
        for number, (to, _, back, ok_from, dx, dy) in enumerate(direct):
            for zz in range(nz - 1):
                slot = direct_slot + number * nz + zz
                receive((to, None, back, ok_from), slot, *direct_refs(dx, dy, zz))
        for zz in range(nz - 1):
            for part in range(2):
                column[zz, part] = functools.reduce(
                    lambda p, q: p + q, [far_mid[at, zz, part] for at in range(6)]
                )
                column[zz, part, 0:2] += functools.reduce(
                    lambda p, q: p + q, [far_high[at, zz, part] for at in range(6)]
                )
                column[zz, part, cells_y - 1 : cells_y] += functools.reduce(
                    lambda p, q: p + q, [far_low[at, zz, part] for at in range(4)]
                )

    columns_over(lambda number: gather(number, True).wait_recv(), True)
    columns_over(lambda number: gather(number, False).wait_send(), False)

    row = lax.broadcasted_iota(jnp.int32, (cells_y, cells_z), 0)
    spot = lax.broadcasted_iota(jnp.int32, (cells_y, cells_z), 1)
    for zz in range(nz):
        total = column[zz, 0]
        if zz > 0:
            total = total + jnp.where(spot < 2, column[zz - 1, 1], 0.0)
        if zz < nz - 1:
            total = total + jnp.where(spot == cells_z - 1, column[zz + 1, 1], 0.0)
        inside = (x > 0) & ((row > 0) | (y > 0))
        if zz == 0:
            inside = inside & (spot > 0)
        coarse_ref[0, :, zz * cells_z : (zz + 1) * cells_z] = jnp.where(inside, total, 0.0)


def drain(smooth, coarse, smooth_hbm, coarse_hbm, sem):
    copies = [
        pltpu.make_async_copy(smooth.at[a], smooth_hbm.at[a], sem.at[a]) for a in range(MODES)
    ]
    copies.append(pltpu.make_async_copy(coarse, coarse_hbm, sem.at[MODES]))
    for copy in copies:
        copy.start()
    for copy in copies:
        copy.wait()


def per_device(sizes, rhs, orders):
    _, cells_y, cells_z = orders.shape
    nz = sizes[2]
    table = jnp.asarray(
        np.broadcast_to(
            (1.0 / (DIAGONAL * THETA))[:, :, :, None, None], DIAGONAL.shape + (1, cells_z)
        ),
        jnp.float32,
    )
    field = rhs.reshape(rhs.shape[:3] + rhs.shape[4:])
    cells = (cells_y, cells_z)
    rows = 8 * ((cells_y + 8) // 8)
    tall = 8 * ((cells_y + 10) // 8)
    line = (2, 2, MODES, MODES)

    def buf(*shape):
        return pltpu.VMEM(shape, jnp.float32)

    def whole(*shape):
        return pltpu.VMEM(shape, jnp.int32)

    slots = 24 + len(CARRIES) + nz - 1 + (len(CARRIES) + 1) * nz
    coarse_shape = (1, cells_y, nz * cells_z)
    vmem = pl.BlockSpec(memory_space=pltpu.VMEM)
    hbm = pl.BlockSpec(memory_space=pltpu.HBM)
    smoothed, coarse = pl.pallas_call(
        functools.partial(kernel, sizes, cells_y, cells_z),
        out_shape=(pltpu.VMEM(field.shape, jnp.float32), pltpu.VMEM(coarse_shape, jnp.float32)),
        in_specs=[hbm, hbm, hbm],
        out_specs=(vmem, vmem),
        scratch_shapes=[buf(*field.shape)] * 6
        + [
            whole(*orders.shape), buf(*table.shape),
            buf(2, MODES, 2, MODES, *cells), buf(2, MODES, 2, MODES, *cells),
            buf(*line, 1, cells_z), buf(*line, 1, cells_z),
            buf(*line, *cells), buf(*line, *cells),
            buf(2, MODES, MODES, rows, cells_z), buf(2, MODES, MODES, rows, cells_z),
            whole(2, 1, cells_z), whole(2, *cells), whole(2, 1, cells_z), whole(2, *cells),
            whole(2, 2, 1, cells_z), whole(2, 2, *cells), whole(2, *cells), whole(3, tall, cells_z),
            buf(112, tall, cells_z),
            buf(6, 2, *cells), buf(6, 2, 2, cells_z), buf(4, 2, 1, cells_z),
            buf(6, 2, *cells), buf(6, 2, 2, cells_z), buf(4, 2, 1, cells_z),
            buf(6, nz, 2, *cells), buf(6, nz, 2, 2, cells_z), buf(4, nz, 2, 1, cells_z),
            buf(nz, 2, *cells),
            buf(2, RELAYED, 2, MODES, *cells),
            pltpu.SemaphoreType.DMA((MODES + 2,)),
            pltpu.SemaphoreType.DMA((slots,)),
            pltpu.SemaphoreType.DMA((slots,)),
            pltpu.SemaphoreType.DMA((2, MODES)),
            pltpu.SemaphoreType.DMA((2, MODES)),
            pltpu.SemaphoreType.DMA((2, 3)),
            pltpu.SemaphoreType.DMA((2, 3)),
            pltpu.SemaphoreType.DMA((2, RELAYED)),
            pltpu.SemaphoreType.DMA((2, RELAYED)),
            pltpu.SemaphoreType.REGULAR((3,)),
        ],
        compiler_params=pltpu.CompilerParams(collective_id=0, has_side_effects=True),
        name="smoother",
    )(field, orders, table)
    smoothed, coarse = pl.pallas_call(
        drain,
        out_shape=(
            jax.ShapeDtypeStruct(field.shape, jnp.float32),
            jax.ShapeDtypeStruct(coarse_shape, jnp.float32),
        ),
        in_specs=[vmem, vmem],
        out_specs=(hbm, hbm),
        scratch_shapes=[pltpu.SemaphoreType.DMA((MODES + 1,))],
        name="drain",
    )(
        pltpu.with_memory_space_constraint(smoothed, pltpu.VMEM),
        pltpu.with_memory_space_constraint(coarse, pltpu.VMEM),
    )
    return smoothed.reshape(rhs.shape), coarse


def solution(mesh):
    sizes = tuple(mesh.shape[axis] for axis in ("gx", "gy", "gz"))
    return jax.shard_map(
        functools.partial(per_device, sizes),
        mesh=mesh,
        in_specs=(P(None, None, None, "gx", "gy", "gz"), P("gx", "gy", "gz")),
        out_specs=(P(None, None, None, "gx", "gy", "gz"), P("gx", "gy", None)),
        check_vma=False,
    )
```

```python
import functools

import jax
import jax.numpy as jnp
import numpy as np
from jax import lax
from jax.experimental import pallas as pl
from jax.experimental.pallas import tpu as pltpu
from jax.sharding import PartitionSpec as P

PENALTY = 49.0
EIGEN_HIGH = 2.4
EIGEN_LOW = 0.24
MODES = 7
MESH = pl.DeviceIdType.MESH


def tables():
    degree = np.arange(MODES)
    normed = np.sqrt((2.0 * degree + 1.0) / 2.0)
    smaller = np.minimum(degree[:, None], degree[None, :])
    parity = (degree[:, None] + degree[None, :]) % 2 == 0
    stiffness = np.where(parity, normed[:, None] * normed[None, :] * smaller * (smaller + 1), 0.0)
    signs = (-1.0) ** degree
    slope = normed * degree * (degree + 1) / 2.0
    low, low_slope = normed * signs, -slope * signs
    own = stiffness + np.outer(normed, PENALTY * normed - 0.5 * slope) - 0.5 * np.outer(slope, normed)
    own = own + np.outer(low, PENALTY * low + 0.5 * low_slope) + 0.5 * np.outer(low_slope, low)
    one_axis = normed * normed * degree * (degree + 1) + 2.0 * (
        PENALTY * normed * normed - normed * slope
    )
    diagonal = (
        one_axis[:, None, None] + one_axis[None, :, None] + one_axis[None, None, :]
    ) / PENALTY
    return (
        own / PENALTY,
        0.5 * slope - PENALTY * normed,
        0.5 * normed,
        normed / PENALTY,
        slope / PENALTY,
        diagonal,
    )


OWN, JUMP, HALF, VALUE, SLOPE, DIAGONAL = tables()
THETA = 0.5 * (EIGEN_HIGH + EIGEN_LOW)
DELTA = 0.5 * (EIGEN_HIGH - EIGEN_LOW)
RHO_FIRST = DELTA / THETA
RHO_SECOND = 1.0 / (2.0 * THETA / DELTA - RHO_FIRST)
KEEP = 1.0 + RHO_SECOND * RHO_FIRST
STEP = 2.0 * RHO_SECOND / DELTA * THETA


def combine(weights, values):
    total = None
    for weight, value in zip(weights, values):
        term = value * float(weight)
        total = term if total is None else total + term
    return total


def traces(values):
    even, odd = values[0::2], values[1::2]
    jump_even, jump_odd = combine(JUMP[0::2], even), combine(JUMP[1::2], odd)
    half_even, half_odd = combine(HALF[0::2], even), combine(HALF[1::2], odd)
    down = (jump_even - jump_odd, half_even - half_odd)
    up = (jump_even + jump_odd, half_even + half_odd)
    return down, up


def own_row(row, values):
    start = row % 2
    return combine(OWN[row, start::2], values[start::2])


def face_terms(from_up, from_down):
    both = (from_up[0] + from_down[0], from_up[1] + from_down[1])
    apart = (from_up[0] - from_down[0], from_up[1] - from_down[1])

    def term(mode):
        pair = both if mode % 2 == 0 else apart
        if mode == 0:
            return pair[0] * float(VALUE[0])
        return pair[0] * float(VALUE[mode]) + pair[1] * float(SLOPE[mode])

    return term


def vertex_pair(zero, one):
    flat, tilt = np.sqrt(0.5) * zero, (np.sqrt(1.5) / 3.0) * one
    return flat - tilt, flat + tilt


def one_sided(data, mode, from_below):
    if mode == 0:
        return data[0] * float(VALUE[0])
    sign = -1.0 if from_below and mode % 2 else 1.0
    return data[0] * (sign * float(VALUE[mode])) + data[1] * (sign * float(SLOPE[mode]))


def corners(values):
    for axis in range(3):
        done = {}
        for key in values:
            if key[axis] == 0:
                other = tuple(1 if n == axis else key[n] for n in range(3))
                done[key], done[other] = vertex_pair(values[key], values[other])
        values = done
    return values


OCTET = [(a, b, e) for a in range(2) for b in range(2) for e in range(2)]
RELAYED = 4
SIGNS = (1, -1)
DIAGONALS = (
    [(dx, dy, 0) for dx in SIGNS for dy in SIGNS]
    + [(dx, 0, dz) for dx in SIGNS for dz in SIGNS]
    + [(2 * dx, 0, 0) for dx in SIGNS]
)
Y_PARTS = ((slice(0, 2), slice(0, MODES)), (slice(2, MODES), slice(0, 2)), (slice(2, MODES), slice(2, MODES)))
REACH = range(-2, 4)
CARRIES = (
    (1, 1), (-1, 1), (1, -1), (-1, -1), (3, 1), (2, 1), (-2, 1), (2, -1),
    (3, 0), (2, 0), (-2, 0), (1, 0), (-1, 0), (0, 1), (0, -1),
)


def kernel(
    sizes, cells_y, cells_z, rhs_hbm, orders_hbm, table_hbm, smooth, coarse_ref,
    rhs, first, acc, coef, ghost_up, ghost_down, orders_ref, table_ref,
    xs, xr, ys, yr, zs, zr, y_up, y_down,
    order_line, order_x, order_y, order_z, order_xy, order_xz, order_far, order_tile, pads,
    out_mid, out_high, out_low, in_mid, in_high, in_low, far_mid, far_high, far_low, column,
    relay, local_sem, send_sem, recv_sem, x_send, x_recv, y_send, y_recv, relay_in, relay_out, met,
):
    nx, ny, nz = sizes
    tall = pads.shape[1]
    x, y, z = lax.axis_index("gx"), lax.axis_index("gy"), lax.axis_index("gz")
    barrier = pltpu.get_barrier_semaphore()

    def neighbour(axis, sign):
        here = (x, y, z)[axis]
        to = [x, y, z]
        to[axis] = here + sign
        back = [x, y, z]
        back[axis] = here - sign
        below, above = here > 0, here < sizes[axis] - 1
        return (tuple(to), below if sign < 0 else above, tuple(back), above if sign < 0 else below)

    halos = [neighbour(axis, sign) for axis in range(3) for sign in (-1, 1)]
    always = x >= 0

    def offset(dx, dy):
        ok_to = (x + dx > 0) & (x + dx < nx)
        ok_from = (x > 0) & (x - dx >= 0) & (x - dx < nx)
        if dy > 0:
            ok_to, ok_from = ok_to & (y + dy < ny), ok_from & (y >= dy)
        if dy < 0:
            ok_to, ok_from = ok_to & (y + dy >= 0), ok_from & (y - dy < ny)
        return ((x + dx, y + dy, z), ok_to, (x - dx, y - dy, z), ok_from)

    carries = [offset(dx, dy) + (dx, dy) for dx, dy in CARRIES]
    collects = z == nz - 1
    direct = []
    for dx, dy in CARRIES + ((0, 0),):
        to, ok_to, back, ok_from = offset(dx, dy)
        to = to[:2] + (nz - 1,)
        direct.append((to, ok_to & jnp.logical_not(collects), back, ok_from, dx, dy))
    columns = []
    for r in range(1, nz):
        source = lax.rem(z - r + nz, nz)
        columns.append(((x, y, lax.rem(z + r, nz)), always, (x, y, source), always, source))

    def diagonal(offset):
        here = (x, y, z)
        to = tuple(h + d for h, d in zip(here, offset))
        back = tuple(h - d for h, d in zip(here, offset))
        ok_to, ok_from = always, always
        for axis, d in enumerate(offset):
            low, high = here[axis] >= abs(d), here[axis] + abs(d) < sizes[axis]
            if d > 0:
                ok_to, ok_from = ok_to & high, ok_from & low
            elif d < 0:
                ok_to, ok_from = ok_to & low, ok_from & high
        return (to, ok_to, back, ok_from)

    diagonals = [diagonal(offset) for offset in DIAGONALS]

    def diagonal_refs(offset):
        dx, dy, dz = offset
        if dy:
            return order_line.at[0 if dy < 0 else 1], order_xy.at[(1 + dx) // 2, (1 + dy) // 2]
        if dz:
            return orders_ref.at[0], order_xz.at[(1 + dx) // 2, (1 + dz) // 2]
        return orders_ref.at[0], order_far.at[(2 + dx) // 4]

    odd = lax.rem(x, 2) == 1
    even = jnp.logical_not(odd)
    relays = (
        ((x - 2, y, z), even & (x >= 2), (x + 2, y, z), even & (x + 2 < nx), (x + 1, y, z)),
        ((x + 2, y, z), odd & (x + 2 < nx), (x - 2, y, z), odd & (x >= 3), (x - 1, y, z)),
    )

    expected = jnp.int32(0)
    for entry in halos[:4] + columns + list(relays):
        to, ok_to, back, ok_from = entry[:4]

        @pl.when(ok_from)
        def _(back=back):
            pl.semaphore_signal(barrier, inc=1, device_id=back, device_id_type=MESH)

        expected = expected + jnp.where(ok_to, 1, 0).astype(jnp.int32)

    loads = [
        pltpu.make_async_copy(orders_hbm, orders_ref, local_sem.at[MODES]),
        pltpu.make_async_copy(table_hbm, table_ref, local_sem.at[MODES + 1]),
    ]
    for copy in loads:
        copy.start()

    def rhs_load(b):
        return pltpu.make_async_copy(rhs_hbm.at[:, b], rhs.at[:, b], local_sem.at[b])

    for b in range(MODES):
        rhs_load(b).start()

    def remote(src, dst, slot, to):
        if isinstance(slot, tuple):
            return pltpu.make_async_remote_copy(
                src_ref=src, dst_ref=dst, send_sem=y_send.at[slot], recv_sem=y_recv.at[slot],
                device_id=to, device_id_type=MESH,
            )
        return pltpu.make_async_remote_copy(
            src_ref=src, dst_ref=dst, send_sem=send_sem.at[slot], recv_sem=recv_sem.at[slot],
            device_id=to, device_id_type=MESH,
        )

    def start(entry, slot, src, dst):
        to, ok_to = entry[:2]

        @pl.when(ok_to)
        def _():
            remote(src, dst, slot, to).start()

    def receive(entry, slot, src, dst):
        to, _, _, ok_from = entry[:4]

        @pl.when(ok_from)
        def _():
            remote(src, dst, slot, to).wait_recv()

    def finish(entry, slot, src, dst):
        to, ok_to = entry[:2]

        @pl.when(ok_to)
        def _():
            remote(src, dst, slot, to).wait_send()

    stages = (
        ((xs, xr), (ys, yr), (zs, zr)),
        ((orders_ref, order_x), (order_line, order_y), (orders_ref, order_z)),
    )

    def over(action, stage, axis):
        src, dst = stages[stage][axis]
        for side in range(2):
            index = 2 * axis + side
            action(halos[index], 6 * stage + index, src.at[0 if src is orders_ref else side], dst.at[side])

    for stage, empty in ((0, 0.0), (1, -1)):
        for axis in range(3):
            for side in range(2):
                dst = stages[stage][axis][1]

                @pl.when(jnp.logical_not(halos[2 * axis + side][3]))
                def _(dst=dst, side=side, empty=empty):
                    dst[side] = jnp.full(dst.shape[1:], empty, dst.dtype)

    pads[...] = jnp.zeros(pads.shape, jnp.float32)
    order_tile[...] = jnp.full(order_tile.shape, -1, jnp.int32)
    for offset, entry in zip(DIAGONALS, diagonals):

        @pl.when(jnp.logical_not(entry[3]))
        def _(offset=offset):
            dst = diagonal_refs(offset)[1]
            dst[...] = jnp.full(dst.shape, -1, jnp.int32)

    targets = {0: (out_mid, in_mid), 1: (out_high, in_high), -1: (out_low, in_low)}

    def carry_refs(dx, dy):
        src, dst = targets[dy]
        at = dx + 1 if dy < 0 else dx + 2
        return src.at[at], dst.at[at]

    far_of = {0: far_mid, 1: far_high, -1: far_low}

    def direct_refs(dx, dy, source):
        at = dx + 1 if dy < 0 else dx + 2
        return targets[dy][0].at[at], far_of[dy].at[at, source]

    for _, _, _, ok_from, dx, dy in direct:

        @pl.when(jnp.logical_not(ok_from))
        def _(dx=dx, dy=dy):
            dst = far_of[dy].at[dx + 1 if dy < 0 else dx + 2]
            dst[...] = jnp.zeros(dst.shape, jnp.float32)

    for _, _, _, ok_from, dx, dy in carries:

        @pl.when(jnp.logical_not(ok_from))
        def _(dx=dx, dy=dy):
            dst = carry_refs(dx, dy)[1]
            dst[...] = jnp.zeros(dst.shape, jnp.float32)

    for copy in loads:
        copy.wait()
    orders = orders_ref[0]
    order_line[0] = orders[0:1]
    order_line[1] = orders[cells_y - 1 : cells_y]
    tile = (MODES, cells_y, cells_z)
    last_mode = lax.broadcasted_iota(jnp.int32, tile, 0)
    lane = lax.broadcasted_iota(jnp.int32, (1, 1, cells_z), 2)

    def active(a, b):
        return jnp.maximum(jnp.maximum(a, b), last_mode) <= orders[None]

    def loop(body, low=0, high=MODES):
        def step(index, carry):
            body(index)
            return carry

        lax.fori_loop(low, high, step, 0)

    def x_copy(side, b, to):
        return pltpu.make_async_remote_copy(
            src_ref=xs.at[side, b], dst_ref=xr.at[side, b],
            send_sem=x_send.at[side, b], recv_sem=x_recv.at[side, b],
            device_id=to, device_id_type=MESH,
        )

    def to_relay(side, b, to):
        return pltpu.make_async_remote_copy(
            src_ref=xs.at[side, b], dst_ref=relay.at[side, b],
            send_sem=x_send.at[side, b], recv_sem=relay_in.at[side, b],
            device_id=to, device_id_type=MESH,
        )

    def from_relay(side, b, to):
        return pltpu.make_async_remote_copy(
            src_ref=relay.at[side, b], dst_ref=xr.at[side, b],
            send_sem=relay_out.at[side, b], recv_sem=x_recv.at[side, b],
            device_id=to, device_id_type=MESH,
        )

    def forward(number):
        for side in range(2):
            back, relaying, target = relays[side][2:]

            @pl.when(relaying)
            def _():
                to_relay(side, number, target).wait_recv()
                from_relay(side, number, target).start()

    def x_receive(number):
        for side in range(2):

            @pl.when(halos[side][3])
            def _():
                x_copy(side, number, halos[side][0]).wait_recv()

    def x_traces(b):
        rhs_load(b).wait()
        values = []
        for a in range(MODES):
            value = jnp.where(active(a, b), table_ref[a, b] * rhs[a, b], 0.0)
            first[a, b] = value
            values.append(value)
        sides = traces(values)
        for side in range(2):
            for kind in range(2):
                xs[side, b, kind] = sides[side][kind]

    def x_start(b):
        for side in range(2):
            to, ok_to = halos[side][:2]
            via, used = relays[side][:2]
            if b < RELAYED:

                @pl.when(used)
                def _():
                    to_relay(side, b, via).start()

                ok_to = ok_to & jnp.logical_not(used)

            @pl.when(ok_to)
            def _():
                x_copy(side, b, to).start()

    def diagonal_over(action):
        for number, (offset, entry) in enumerate(zip(DIAGONALS, diagonals)):
            action(entry, 14 + number, *diagonal_refs(offset))

    def y_over(action, part):
        modes = Y_PARTS[part]
        for side in range(2):
            at = (side, slice(None)) + modes
            action(halos[2 + side], (side, part), ys.at[at], yr.at[at])

    def meet(action):
        for side in range(2):
            to, ok_to, _, ok_from = halos[side]

            @pl.when(ok_to if action == "tell" else ok_from)
            def _():
                if action == "tell":
                    pl.semaphore_signal(met.at[side], inc=1, device_id=to, device_id_type=MESH)
                else:
                    pl.semaphore_wait(met.at[side], 1)

    loop(x_traces, 0, 5)
    pl.semaphore_wait(barrier, expected)
    meet("tell")
    over(start, 1, 0)
    over(start, 1, 1)
    over(start, 1, 2)
    x_start(0)
    x_start(1)
    x_start(2)
    loop(x_traces, 5)

    def y_faces(a, values, send, up_buf, down_buf):
        down, up = traces(values)
        for kind in range(2):
            up_buf[kind, a, :, 0:cells_y, :] = down[kind]
            down_buf[kind, a, :, 1 : cells_y + 1, :] = up[kind]
            send[0, kind, a] = down[kind][:, 0:1, :]
            send[1, kind, a] = up[kind][:, cells_y - 1 : cells_y, :]

    def y_neighbours(a, received, up_buf, down_buf, part=slice(0, MODES)):
        for kind in range(2):
            up_buf[kind, a, part, cells_y : cells_y + 1, :] = received[0, kind, a, part]
            down_buf[kind, a, part, 0:1, :] = received[1, kind, a, part]
        return (
            [up_buf[kind, a, part, 1 : cells_y + 1, :] for kind in range(2)],
            [down_buf[kind, a, part, 0:cells_y, :] for kind in range(2)],
        )

    def z_faces(a, values, send):
        sides = traces(values)
        for side in range(2):
            for kind in range(2):
                send[side, kind, a] = sides[side][kind]

    def z_neighbours(a, send, received, part=slice(0, MODES)):
        def moved(side, kind, edge, amount):
            picked = jnp.where(lane == edge, received[side, kind, a, part], send[side, kind, a, part])
            return pltpu.roll(picked, amount, 2)

        return (
            [moved(0, kind, 0, cells_z - 1) for kind in range(2)],
            [moved(1, kind, cells_z - 1, 1) for kind in range(2)],
        )

    def y_traces(a):
        y_faces(a, [first[a, b] for b in range(MODES)], ys, y_up, y_down)

    loop(y_traces, 0, 2)
    y_over(start, 0)
    loop(y_traces, 2)
    y_over(start, 1)
    meet("hear")
    diagonal_over(start)
    x_start(3)
    y_over(start, 2)
    loop(lambda a: z_faces(a, [first[a, :, e] for e in range(MODES)], zs))
    over(start, 0, 2)

    def predict(a, b, part, total):
        right = rhs[a, b, part]
        modes = jnp.maximum(last_mode[part], jnp.maximum(a, b))
        scale = jnp.where(modes <= orders[None], table_ref[a, b, part], 0.0)
        return scale * (KEEP * right + STEP * (right - total)), scale * (-STEP)

    def x_own(b):
        values = [first[a, b] for a in range(MODES)]
        for a in range(MODES):
            acc[a, b] = own_row(a, values)

    def y_own(a):
        values = [first[a, b] for b in range(MODES)]
        for b in range(MODES):
            acc[a, b] += own_row(b, values)

    def z_own(a):
        values = [first[a, :, e] for e in range(MODES)]
        for e in range(MODES):
            acc[a, :, e] += own_row(e, values)

    def z_flux(a):
        term = face_terms(*z_neighbours(a, zs, zr))
        for e in range(MODES):
            acc[a, :, e] += term(e)

    def y_flux(a):
        term = face_terms(*y_neighbours(a, yr, y_up, y_down))
        for b in range(MODES):
            acc[a, b], coef[a, b] = predict(a, b, slice(0, MODES), acc[a, b] + term(b))

    def y_flux_part(part):
        def step(a):
            term = face_terms(*y_neighbours(a, yr, y_up, y_down, part))
            for b in range(MODES):
                acc[a, b, part], coef[a, b, part] = predict(a, b, part, acc[a, b, part] + term(b))

        loop(step, 2)

    loop(x_own)
    x_start(4)
    x_start(5)
    loop(y_own)
    x_start(6)
    loop(z_own)
    over(receive, 0, 2)
    loop(z_flux)
    forward(0)

    slots = iter(range(pads.shape[0]))

    def padded(value, at):
        slot = next(slots)
        pads[slot, at : at + cells_y, :] = value
        return pads[slot]

    near, border, layers = {}, {}, {}

    def gather_into(where_to, key, value):
        where_to[key] = where_to[key] + value if key in where_to else value

    def spread(values, shift, forced):
        centre, edge, x_low, x_high, y_low, y_high = {}, {}, {}, {}, {}, {}
        for b in range(2):
            line = [values[a, b, 0:2] for a in range(MODES)]
            down, up = traces(line)
            for a in range(2):
                own = own_row(a, line)
                below, above = one_sided(down, a, False), one_sided(up, a, True)
                for e in range(2):
                    centre[a, b, e] = forced[a, b, e] - own[e] if forced is not None else -own[e]
                    x_low[a, b, e] = -below[e]
                    x_high[a, b, e] = -above[e]
        for a in range(2):
            line = [values[a, b, 0:2] for b in range(MODES)]
            down, up = traces(line)
            for b in range(2):
                own = own_row(b, line)
                below, above = one_sided(down, b, False), one_sided(up, b, True)
                for e in range(2):
                    centre[a, b, e] = centre[a, b, e] - own[e]
                    y_low[a, b, e], y_high[a, b, e] = below[e], above[e]
            line = [values[a, 0:2, e] for e in range(MODES)]
            down, up = traces(line)
            for e in range(2):
                below = pltpu.roll(one_sided(down, e, False), cells_z - 1, 2)
                above = pltpu.roll(one_sided(up, e, True), 1, 2)
                inner = jnp.where(lane == cells_z - 1, 0.0, below) + jnp.where(lane == 0, 0.0, above)
                outer = jnp.where(lane == cells_z - 1, below, jnp.where(lane == 0, above, 0.0))
                own = own_row(e, line) + inner
                for b in range(2):
                    centre[a, b, e] = centre[a, b, e] - own[b]
                    edge[a, b, e] = -outer[b]
        resid = {
            key: padded(centre[key], 1) - padded(y_low[key], 0) - padded(y_high[key], 2)
            for key in OCTET
        }

        def masked(parts, degrees):
            return corners(
                {key: jnp.where(degrees >= max(key), parts[key], 0.0) for key in OCTET}
            )

        def settle_sums(tile_orders, low_orders, high_orders, edge_orders):
            cells, rim = masked(resid, tile_orders), masked(edge, edge_orders)
            low, high = masked(x_low, low_orders), masked(x_high, high_orders)
            for i, j, k in OCTET:
                moved = pltpu.roll(cells[i, j, k], 1, 0) if j else cells[i, j, k]
                gather_into(layers, (shift + i, k), moved)
                gather_into(border, (shift + i, j, k), rim[i, j, k])
                gather_into(near, (shift - 1 + i, j, k), low[i, j, k])
                gather_into(near, (shift + 1 + i, j, k), high[i, j, k])

        return settle_sums

    def ghost(values, side, other_orders):
        def put(a, b, high):
            part = slice(0, high)
            data = [xs[side, b, kind, part] for kind in range(2)]
            modes = jnp.maximum(last_mode[part], max(a, b))
            scale = jnp.where(modes <= other_orders[None], table_ref[a, b, part], 0.0) * (-STEP)
            values[a, b, part] = scale * one_sided(data, a, side == 1)

        for b in range(2):
            for a in range(MODES):
                put(a, b, MODES if a < 2 else 2)
        for b in range(2, MODES):
            for a in range(2):
                put(a, b, 2)

    for axis in range(3):
        over(receive, 1, axis)
    rows_of = (orders, order_x[0], order_x[1])
    lines_of = (order_y, order_xy.at[0], order_xy.at[1])
    sides_of = (order_z, order_xz.at[0], order_xz.at[1])

    def surroundings(at):
        order_tile[at, 1 : cells_y + 1] = rows_of[at]
        order_tile[at, 0:1] = lines_of[at][1]
        order_tile[at, cells_y + 1 : cells_y + 2] = lines_of[at][0]
        edge_orders = jnp.where(lane[0] == cells_z - 1, sides_of[at][1], sides_of[at][0])
        return order_tile[at], edge_orders

    ghost(ghost_up, 1, order_x[0])
    ghost(ghost_down, 0, order_x[1])
    y_over(receive, 0)
    loop(y_flux, 0, 2)
    y_over(receive, 1)
    y_flux_part(slice(0, 2))
    forward(1)
    tile_orders, edge_orders = surroundings(0)
    spread(acc, 0, rhs)(tile_orders, order_x[1], order_x[0], edge_orders)
    raised = spread(ghost_up, 1, None)
    lowered = spread(ghost_down, -1, None)
    diagonal_over(receive)

    @pl.when(collects)
    def _():
        for zz in range(nz - 1):
            pl.semaphore_signal(met.at[2], inc=1, device_id=(x, y, zz), device_id_type=MESH)

    forward(2)
    tile_orders, edge_orders = surroundings(1)
    raised(tile_orders, orders, order_far[0], edge_orders)
    tile_orders, edge_orders = surroundings(2)
    lowered(tile_orders, order_far[1], orders, edge_orders)

    row_lane = lane[0]
    sums = {}
    direct_slot = 24 + len(carries) + len(columns)

    @pl.when(jnp.logical_not(collects))
    def _():
        pl.semaphore_wait(met.at[2], 1)

    def direct_of(dx):
        for number, entry in enumerate(direct):
            if entry[4] == dx:
                start(entry, direct_slot + number * nz + z, *direct_refs(*entry[4:], z))

    def carries_of(dx):
        for number, entry in enumerate(carries):
            if entry[4] == dx:
                start(entry, 24 + number, *carry_refs(*entry[4:]))

    for dx in (1, -1, 2, 3, -2, 0):
        pair = []
        for k in range(2):
            parts = [layers[dx, k]] if (dx, k) in layers else []
            parts += [padded(near[dx, j, k], 1 + j) for j in range(2)]
            pair.append(functools.reduce(lambda p, q: p + q, parts))
        moved = pltpu.roll(pair[1], 1, 1)
        if (dx, 0, 0) in border:
            outer = [padded(border[dx, 0, k], 1) + padded(border[dx, 1, k], 2) for k in range(2)]
            outer_moved = pltpu.roll(outer[1], 1, 1)
            inside = pair[0] + jnp.where(row_lane == 0, outer_moved, moved)
            beyond = jnp.where(row_lane == 0, moved, outer_moved) + outer[0]
        else:
            inside = pair[0] + jnp.where(row_lane == 0, 0.0, moved)
            beyond = jnp.where(row_lane == 0, moved, 0.0)
        for part, value in enumerate((inside, beyond)):
            if dx == 0:
                sums[part] = value[1 : cells_y + 1]
            out_mid[dx + 2, part] = value[1 : cells_y + 1]
            out_high[dx + 2, part] = value[cells_y + 1 : cells_y + 3]
            if -1 <= dx <= 2:
                out_low[dx + 1, part] = value[0:1]
        direct_of(dx)
        carries_of(dx)

    forward(3)
    y_over(receive, 2)
    y_flux_part(slice(2, MODES))

    def x_flux(b):
        x_receive(b)
        term = face_terms(
            [xr[0, b, kind] for kind in range(2)], [xr[1, b, kind] for kind in range(2)]
        )
        for a in range(MODES):
            smooth[a, b] = acc[a, b] + coef[a, b] * term(a)

    for stage, axis in ((0, 2), (1, 0), (1, 1), (1, 2)):
        over(finish, stage, axis)
    for part in range(3):
        y_over(finish, part)
    diagonal_over(finish)
    for b in range(MODES):
        for side in range(2):

            @pl.when(halos[side][1])
            def _():
                x_copy(side, b, halos[side][0]).wait_send()

    for b in range(RELAYED):
        for side in range(2):

            @pl.when(relays[side][3])
            def _():
                from_relay(side, b, relays[side][4]).wait_send()

    loop(x_flux, RELAYED)
    for number, entry in enumerate(carries):
        finish(entry, 24 + number, *carry_refs(*entry[4:]))
    for number, entry in enumerate(direct):
        finish(entry, direct_slot + number * nz + z, *direct_refs(*entry[4:], z))

    loop(x_flux, 0, RELAYED)

    for number, entry in enumerate(carries):
        receive(entry, 24 + number, *carry_refs(*entry[4:]))

    for part in range(2):
        value = sums[part]
        for dx in REACH:
            if dx:
                value = value + in_mid[dx + 2, part]
        high = functools.reduce(lambda p, q: p + q, [in_high[at, part] for at in range(6)])
        low = functools.reduce(lambda p, q: p + q, [in_low[at, part] for at in range(4)])
        column[pl.ds(z, 1), part] = value[None]
        column[pl.ds(z, 1), part, 0:2] += high[None]
        column[pl.ds(z, 1), part, cells_y - 1 : cells_y] += low[None]

    def gather(number, arriving):
        entry = columns[number]
        at = entry[4] if arriving else z
        return remote(column.at[at], column.at[at], 24 + len(carries) + number, entry[0])

    def columns_over(action, arriving):
        for number, entry in enumerate(columns):
            to_collector = collects if arriving else entry[0][2] == nz - 1

            @pl.when((x > 0) & jnp.logical_not(to_collector))
            def _(number=number):
                action(number)

    columns_over(lambda number: gather(number, False).start(), False)
    @pl.when(collects)
    def _():
        for number, (to, _, back, ok_from, dx, dy) in enumerate(direct):
            for zz in range(nz - 1):
                slot = direct_slot + number * nz + zz
                receive((to, None, back, ok_from), slot, *direct_refs(dx, dy, zz))
        for zz in range(nz - 1):
            for part in range(2):
                column[zz, part] = functools.reduce(
                    lambda p, q: p + q, [far_mid[at, zz, part] for at in range(6)]
                )
                column[zz, part, 0:2] += functools.reduce(
                    lambda p, q: p + q, [far_high[at, zz, part] for at in range(6)]
                )
                column[zz, part, cells_y - 1 : cells_y] += functools.reduce(
                    lambda p, q: p + q, [far_low[at, zz, part] for at in range(4)]
                )

    columns_over(lambda number: gather(number, True).wait_recv(), True)
    columns_over(lambda number: gather(number, False).wait_send(), False)

    row = lax.broadcasted_iota(jnp.int32, (cells_y, cells_z), 0)
    spot = lax.broadcasted_iota(jnp.int32, (cells_y, cells_z), 1)
    for zz in range(nz):
        total = column[zz, 0]
        if zz > 0:
            total = total + jnp.where(spot < 2, column[zz - 1, 1], 0.0)
        if zz < nz - 1:
            total = total + jnp.where(spot == cells_z - 1, column[zz + 1, 1], 0.0)
        inside = (x > 0) & ((row > 0) | (y > 0))
        if zz == 0:
            inside = inside & (spot > 0)
        coarse_ref[0, :, zz * cells_z : (zz + 1) * cells_z] = jnp.where(inside, total, 0.0)


def drain(smooth, coarse, smooth_hbm, coarse_hbm, sem):
    copies = [
        pltpu.make_async_copy(smooth.at[a], smooth_hbm.at[a], sem.at[a]) for a in range(MODES)
    ]
    copies.append(pltpu.make_async_copy(coarse, coarse_hbm, sem.at[MODES]))
    for copy in copies:
        copy.start()
    for copy in copies:
        copy.wait()


def per_device(sizes, rhs, orders):
    _, cells_y, cells_z = orders.shape
    nz = sizes[2]
    table = jnp.asarray(
        np.broadcast_to(
            (1.0 / (DIAGONAL * THETA))[:, :, :, None, None], DIAGONAL.shape + (1, cells_z)
        ),
        jnp.float32,
    )
    field = rhs.reshape(rhs.shape[:3] + rhs.shape[4:])
    cells = (cells_y, cells_z)
    rows = 8 * ((cells_y + 8) // 8)
    tall = 8 * ((cells_y + 10) // 8)
    line = (2, 2, MODES, MODES)

    def buf(*shape):
        return pltpu.VMEM(shape, jnp.float32)

    def whole(*shape):
        return pltpu.VMEM(shape, jnp.int32)

    slots = 24 + len(CARRIES) + nz - 1 + (len(CARRIES) + 1) * nz
    coarse_shape = (1, cells_y, nz * cells_z)
    vmem = pl.BlockSpec(memory_space=pltpu.VMEM)
    hbm = pl.BlockSpec(memory_space=pltpu.HBM)
    smoothed, coarse = pl.pallas_call(
        functools.partial(kernel, sizes, cells_y, cells_z),
        out_shape=(pltpu.VMEM(field.shape, jnp.float32), pltpu.VMEM(coarse_shape, jnp.float32)),
        in_specs=[hbm, hbm, hbm],
        out_specs=(vmem, vmem),
        scratch_shapes=[buf(*field.shape)] * 6
        + [
            whole(*orders.shape), buf(*table.shape),
            buf(2, MODES, 2, MODES, *cells), buf(2, MODES, 2, MODES, *cells),
            buf(*line, 1, cells_z), buf(*line, 1, cells_z),
            buf(*line, *cells), buf(*line, *cells),
            buf(2, MODES, MODES, rows, cells_z), buf(2, MODES, MODES, rows, cells_z),
            whole(2, 1, cells_z), whole(2, *cells), whole(2, 1, cells_z), whole(2, *cells),
            whole(2, 2, 1, cells_z), whole(2, 2, *cells), whole(2, *cells), whole(3, tall, cells_z),
            buf(112, tall, cells_z),
            buf(6, 2, *cells), buf(6, 2, 2, cells_z), buf(4, 2, 1, cells_z),
            buf(6, 2, *cells), buf(6, 2, 2, cells_z), buf(4, 2, 1, cells_z),
            buf(6, nz, 2, *cells), buf(6, nz, 2, 2, cells_z), buf(4, nz, 2, 1, cells_z),
            buf(nz, 2, *cells),
            buf(2, RELAYED, 2, MODES, *cells),
            pltpu.SemaphoreType.DMA((MODES + 2,)),
            pltpu.SemaphoreType.DMA((slots,)),
            pltpu.SemaphoreType.DMA((slots,)),
            pltpu.SemaphoreType.DMA((2, MODES)),
            pltpu.SemaphoreType.DMA((2, MODES)),
            pltpu.SemaphoreType.DMA((2, 3)),
            pltpu.SemaphoreType.DMA((2, 3)),
            pltpu.SemaphoreType.DMA((2, RELAYED)),
            pltpu.SemaphoreType.DMA((2, RELAYED)),
            pltpu.SemaphoreType.REGULAR((3,)),
        ],
        compiler_params=pltpu.CompilerParams(collective_id=0, has_side_effects=True),
        name="smoother",
    )(field, orders, table)
    smoothed, coarse = pl.pallas_call(
        drain,
        out_shape=(
            jax.ShapeDtypeStruct(field.shape, jnp.float32),
            jax.ShapeDtypeStruct(coarse_shape, jnp.float32),
        ),
        in_specs=[vmem, vmem],
        out_specs=(hbm, hbm),
        scratch_shapes=[pltpu.SemaphoreType.DMA((MODES + 1,))],
        name="drain",
    )(
        pltpu.with_memory_space_constraint(smoothed, pltpu.VMEM),
        pltpu.with_memory_space_constraint(coarse, pltpu.VMEM),
    )
    return smoothed.reshape(rhs.shape), coarse


def solution(mesh):
    sizes = tuple(mesh.shape[axis] for axis in ("gx", "gy", "gz"))
    return jax.shard_map(
        functools.partial(per_device, sizes),
        mesh=mesh,
        in_specs=(P(None, None, None, "gx", "gy", "gz"), P("gx", "gy", "gz")),
        out_specs=(P(None, None, None, "gx", "gy", "gz"), P("gx", "gy", None)),
        check_vma=False,
    )
```
